32 devices in a mesh: scan: 8 (over z, x), tile: 4 (over y, core).
Axes of the slice: x: 2, y: 2, z: 4, core: 2. Of those that a mesh axis runs over, the one named last changes fastest.
Arguments:
- object_slab: float32 [2, 3072, 6144], P(None, 'tile', 'scan'), may hold values from -6 to 6
- probe_field: float32 [2, 512, 512], replicated, may hold values from -3 to 3
- intensities: bfloat16 [8, 4, 6, 512, 512], P('scan', 'tile'), may hold values from 0 to 2
- offsets: int32 [8, 4, 6, 2], P('scan', 'tile'), may hold values from 0 to 767
- live_count: int32 [8, 4], P(None, 'tile'), may hold values from 1 to 6, as said below
Outputs:
- object_grad: float32 [2, 3072, 6144], P(None, 'tile', 'scan')
The draws below stay inside these ranges and needn't reach their ends.
Inputs may be any that keep to these rules, and one draw needn't show every extreme that they name: The first live_count slots of a group hold its measured positions; some group has all 6 slots live.
All inputs are finite; a program needn't handle non-finite values.
Results may differ from the reference program's by a relative error of at most 0.014.
Values may be sent and summed in bfloat16 or wider, within the bound.
A program may use at most 128 MiB of HBM per device.

```python
import math
import jax
import jax.numpy as jnp
from jax import lax

W = 512
TILE = 768
SLOTS = 6
OBJ_Y = 3072
OBJ_X = 6144
N_SCAN = 8
N_TILE = 4


def draw_live_count(key, part):
    key_side, key_high, key_low, key_full = jax.random.split(key, 4)
    shape = (N_SCAN // 2, N_TILE)
    busy_left = jax.random.randint(key_side, shape, 0, 2)
    high = SLOTS - jax.random.randint(key_high, shape, 0, 2)
    low = 1 + jax.random.randint(key_low, shape, 0, max(SLOTS // 4, 1))
    left = jnp.where(busy_left == 1, high, low)
    right = jnp.where(busy_left == 1, low, high)
    counts = jnp.concatenate([left, right], axis=0)
    full_at = jax.random.randint(key_full, (), 0, N_SCAN * N_TILE)
    flat_ids = jnp.arange(N_SCAN * N_TILE, dtype=jnp.int32).reshape((N_SCAN, N_TILE))
    counts = jnp.where(flat_ids == full_at, SLOTS, counts)
    return counts.astype(jnp.int32)


def with_ends(drawn, stream_key, least, largest):
    shape = drawn.shape
    spot = [jax.random.randint(jax.random.fold_in(stream_key, axis), (), 0, shape[axis]) for axis in range(len(shape))]
    drawn = drawn.at[tuple(spot)].set(least)
    longest = shape.index(max(shape))
    spot[longest] = (spot[longest] + 1) % shape[longest]
    return drawn.at[tuple(spot)].set(largest)


def shard_levels(own_key, extent, cuts, low, high):
    def one(position, shards_of):
        draws = jax.random.uniform(jax.random.fold_in(jax.random.fold_in(own_key, 6), position), (shards_of,), jnp.float32, low / len(cuts), high / len(cuts))
        return jnp.repeat(jnp.exp(draws), extent[position] // shards_of).reshape((-1,) + (1,) * (len(extent) - position - 1))

    gain = one(*cuts[0])
    for cut in cuts[1:]:
        gain = gain * one(*cut)
    return gain


def normal_values(own_key, extent, width, most, pieces=(), held_as=jnp.bfloat16):
    result = width * jax.random.normal(own_key, extent, jnp.float32)
    if pieces:
        result = result * shard_levels(own_key, extent, pieces, -0.22, 0.18)
    return jnp.clip(result, -most, most).astype(held_as)


def setup_inputs(seed: int = 0) -> dict:
    arg_keys = jax.random.split(jax.random.key(seed), 6)
    return {
        "object_slab": normal_values(arg_keys[0], (2, OBJ_Y, OBJ_X), 1.0, 6.0, ((1, 4), (2, 8)), jnp.float32),
        "probe_field": normal_values(arg_keys[1], (2, W, W), 0.5, 3.0, (), jnp.float32),
        "intensities": jnp.clip(2.0 * jax.random.uniform(arg_keys[2], (N_SCAN, N_TILE, SLOTS, W, W), jnp.float32) ** shard_levels(arg_keys[2], (N_SCAN, N_TILE, SLOTS, W, W), ((0, 8), (1, 4)), -0.2, 0.2), 0.0, 2.0).astype(jnp.bfloat16),
        "offsets": with_ends(jax.random.randint(arg_keys[3], (N_SCAN, N_TILE, SLOTS, 2), 0, TILE), jax.random.fold_in(arg_keys[3], 1), 0, TILE - 1).astype(jnp.int32),
        "live_count": draw_live_count(jax.random.fold_in(arg_keys[5], 71), 0),
    }


def fourier_tables(side_len):
    across = jnp.arange(side_len, dtype=jnp.int32)
    phase = (across[:, None] * across[None, :] % side_len).astype(jnp.float32) * (2.0 * math.pi / side_len)
    factor = 1.0 / math.sqrt(side_len)
    return ((jnp.cos(phase) * factor).astype(jnp.bfloat16), (-jnp.sin(phase) * factor).astype(jnp.bfloat16))

def left_apply(table_re, table_im, part_re, part_im):
    side_len = part_re.shape[-1]
    joined = jnp.concatenate([part_re, part_im], axis=-1).astype(jnp.float32)
    with_re = jnp.einsum('ij,bjk->bik', table_re.astype(jnp.float32), joined)
    with_im = jnp.einsum('ij,bjk->bik', table_im.astype(jnp.float32), joined)
    return (with_re[..., :side_len] - with_im[..., side_len:], with_re[..., side_len:] + with_im[..., :side_len])

def right_apply(part_re, part_im, table_re, table_im):
    side_len = part_re.shape[-1]
    joined = jnp.concatenate([part_re, part_im], axis=-2).astype(jnp.float32)
    with_re = jnp.einsum('bij,jk->bik', joined, table_re.astype(jnp.float32))
    with_im = jnp.einsum('bij,jk->bik', joined, table_im.astype(jnp.float32))
    return (with_re[:, :side_len] - with_im[:, side_len:], with_im[:, :side_len] + with_re[:, side_len:])

def transform(exit_waves, measured, tables):
    table_re, table_im = tables
    conj_im = -table_im
    half_re, half_im = left_apply(table_re, table_im, exit_waves[:, 0], exit_waves[:, 1])
    half_re = half_re.astype(jnp.bfloat16)
    half_im = half_im.astype(jnp.bfloat16)
    far_re, far_im = right_apply(half_re, half_im, table_re, table_im)
    misfit = far_re * far_re + far_im * far_im - measured.astype(jnp.float32)
    mis_re = (misfit * far_re).astype(jnp.bfloat16)
    mis_im = (misfit * far_im).astype(jnp.bfloat16)
    back_re, back_im = left_apply(table_re, conj_im, mis_re, mis_im)
    back_re = back_re.astype(jnp.bfloat16)
    back_im = back_im.astype(jnp.bfloat16)
    grad_re, grad_im = right_apply(back_re, back_im, table_re, conj_im)
    return jnp.stack([grad_re, grad_im], axis=1).astype(jnp.bfloat16)

def exit_wave(probe_field, patches):
    probe_re = probe_field[0]
    probe_im = probe_field[1]
    real_part = probe_re * patches[:, 0] - probe_im * patches[:, 1]
    imag_part = probe_re * patches[:, 1] + probe_im * patches[:, 0]
    return jnp.stack([real_part, imag_part], axis=1).astype(jnp.bfloat16)

def object_gradient(probe_field, wave_grads):
    probe_re = probe_field[0]
    probe_im = probe_field[1]
    grad_re = wave_grads[:, 0].astype(jnp.float32)
    grad_im = wave_grads[:, 1].astype(jnp.float32)
    real_part = probe_re * grad_re + probe_im * grad_im
    imag_part = probe_re * grad_im - probe_im * grad_re
    return jnp.stack([real_part, imag_part], axis=1)

def reference(object_slab, probe_field, intensities, offsets, live_count):
    side_len = probe_field.shape[-1]
    grid_rows = object_slab.shape[1]
    grid_cols = object_slab.shape[2]
    padded = jnp.pad(object_slab, ((0, 0), (0, side_len), (0, side_len)))
    groups = N_SCAN * N_TILE
    flat_measured = intensities.reshape(groups, SLOTS, side_len, side_len)
    flat_shifts = offsets.reshape(groups, SLOTS, 2)
    flat_live = live_count.reshape(groups)
    group_ids = jnp.arange(groups, dtype=jnp.int32)
    scan_ids = group_ids // N_TILE
    tile_ids = group_ids % N_TILE
    zero_index = jnp.zeros((), jnp.int32)
    tables = fourier_tables(side_len)

    def one_group(gradient_sum, inputs):
        measured, shifts, live_total, scan_id, tile_id = inputs
        row_start = (tile_id * TILE + shifts[:, 0]).astype(jnp.int32)
        col_start = (scan_id * TILE + shifts[:, 1]).astype(jnp.int32)

        def cut_patch(row_at, col_at):
            return lax.dynamic_slice(padded, (zero_index, row_at, col_at), (2, side_len, side_len))
        patches = jax.vmap(cut_patch)(row_start, col_start)
        exit_waves = exit_wave(probe_field, patches)
        wave_grads = transform(exit_waves, measured, tables)
        live_mask = (jnp.arange(SLOTS, dtype=jnp.int32) < live_total).astype(jnp.float32)
        patch_grad = object_gradient(probe_field, wave_grads) * live_mask[:, None, None, None]

        def add_one(slot_index, running):
            corner = (zero_index, row_start[slot_index], col_start[slot_index])
            current = lax.dynamic_slice(running, corner, (2, side_len, side_len))
            return lax.dynamic_update_slice(running, current + patch_grad[slot_index], corner)
        return (lax.fori_loop(0, SLOTS, add_one, gradient_sum), None)
    gradient_sum = jnp.zeros(padded.shape, jnp.float32)
    gradient_sum, unused = lax.scan(one_group, gradient_sum, (flat_measured, flat_shifts, flat_live, scan_ids, tile_ids))
    return gradient_sum[:, :grid_rows, :grid_cols]
```

```python
import functools
import math

import jax
import jax.numpy as jnp
import numpy as np
from jax import lax
from jax.experimental import pallas as pl
from jax.experimental.pallas import tpu as pltpu
from jax.sharding import PartitionSpec as P

RADIX = 4
LANES = 128
GROUP = 16
TALL = 256


def residue_tables(side_len):
    part = side_len // RADIX
    freq = np.arange(side_len).reshape(part, RADIX).T
    across = np.arange(part)
    phase = (freq[:, :, None] * across[None, None, :] % side_len) * (2.0 * math.pi / side_len)
    factor = 1.0 / math.sqrt(side_len)
    cos = np.cos(phase) * factor
    sin = np.sin(phase) * factor
    rows = np.concatenate(
        [np.concatenate([cos, sin], axis=2), np.concatenate([-sin, cos], axis=2)], axis=1
    ).astype(np.float32)
    return jnp.asarray(rows, jnp.bfloat16), jnp.asarray(rows.swapaxes(1, 2), jnp.bfloat16)


def sorted_by_residue(side_len):
    at = np.arange(side_len)
    source = at % (side_len // RADIX) * RADIX + at // (side_len // RADIX)
    sort = (source[:, None] == at[None, :]).astype(np.float32)
    return jnp.asarray(sort, jnp.bfloat16), jnp.asarray(sort.T, jnp.bfloat16)


def dot(a, b):
    return jnp.dot(a, b, preferred_element_type=jnp.float32)


def butterfly(parts, sign):
    (r0, i0), (r1, i1), (r2, i2), (r3, i3) = parts
    ar, ai, br, bi = r0 + r2, i0 + i2, r1 + r3, i1 + i3
    cr, ci, dr, di = r0 - r2, i0 - i2, r1 - r3, i1 - i3
    plus = (cr - di, ci + dr)
    minus = (cr + di, ci - dr)
    first, third = (plus, minus) if sign > 0 else (minus, plus)
    return [(ar + br, ai + bi), first, (ar - br, ai - bi), third]


def neighbours(axes):
    result = []
    for name, count in axes:
        me = lax.axis_index(name)
        result.append((me > 0, {name: me - 1}, me < count - 1, {name: me + 1}))
    return result


def meet(peers):
    barrier = pltpu.get_barrier_semaphore()
    for has_low, low, has_high, high in peers:
        for there, peer in ((has_low, low), (has_high, high)):

            @pl.when(there)
            def _(peer=peer):
                pl.semaphore_signal(
                    barrier, inc=1, device_id=peer, device_id_type=pl.DeviceIdType.MESH
                )

    count = sum(
        there.astype(jnp.int32) for has_low, _, has_high, _ in peers for there in (has_low, has_high)
    )
    pl.semaphore_wait(barrier, count)


def remote(source, target, sends, receives, index, peer):
    return pltpu.make_async_remote_copy(
        src_ref=source,
        dst_ref=target,
        send_sem=sends.at[index],
        recv_sem=receives.at[index],
        device_id=peer,
        device_id_type=pl.DeviceIdType.MESH,
    )


def quarter_turns(cos, sin, q):
    return ((cos, sin), (sin, -cos), (-cos, -sin), (-sin, cos))[q]


def in_place(mask, cos, sin, q):
    wrapped = quarter_turns(cos, sin, q)
    return jnp.where(mask, cos, wrapped[0]), jnp.where(mask, sin, wrapped[1])


def gather_kernel(
    axes,
    shift_ref,
    own_hbm,
    measured_hbm,
    probe_hbm,
    rows_hbm,
    cols_hbm,
    sort_hbm,
    unsort_hbm,
    field,
    probes,
    tables,
    arranged,
    grown,
    own,
    measured,
    extended,
    rows_ref,
    cols_ref,
    doubled,
    sort,
    unsort,
    sends,
    receives,
    fetches,
):
    slots, side_len = measured.shape[:2]
    tile_len = own.shape[1]
    part = side_len // RADIX
    own_blocks = tile_len // LANES
    side_blocks = side_len // LANES
    scan, tile = neighbours(axes)
    has_left, left, has_right, _ = scan
    has_up, up, has_down, _ = tile
    first = pltpu.make_async_copy(
        own_hbm.at[:, :side_len, :side_len], own.at[:, :side_len, :side_len], fetches.at[0]
    )
    second = pltpu.make_async_copy(
        own_hbm.at[:, side_len:, :side_len], own.at[:, side_len:, :side_len], fetches.at[1]
    )
    third = pltpu.make_async_copy(
        own_hbm.at[:, :side_len, side_len:], own.at[:, :side_len, side_len:], fetches.at[2]
    )
    fourth = pltpu.make_async_copy(
        own_hbm.at[:, side_len:, side_len:], own.at[:, side_len:, side_len:], fetches.at[3]
    )
    constants = [
        pltpu.make_async_copy(source, target, fetches.at[4 + i])
        for i, (source, target) in enumerate(
            (
                (sort_hbm, sort),
                (unsort_hbm, unsort),
                (measured_hbm, measured),
                (rows_hbm, rows_ref),
                (cols_hbm, cols_ref),
            )
        )
    ]
    for c in range(2):
        for b in range(side_blocks):
            cols = slice(b * LANES, (b + 1) * LANES)
            for source, target in (
                (probe_hbm.at[c, :, cols], extended.at[c, b, GROUP:, :]),
                (probe_hbm.at[c, side_len - GROUP :, cols], extended.at[c, b, :GROUP, :]),
            ):
                constants.append(
                    pltpu.make_async_copy(source, target, fetches.at[4 + len(constants)])
                )
    for load in [first, second, third, fourth] + constants:
        load.start()
    near = slice(0, side_blocks)
    far = slice(own_blocks, own_blocks + side_blocks)
    top = remote(
        field.at[:, near, :side_len, :], field.at[:, far, :side_len, :], sends, receives, 0, left
    )
    rest = remote(
        field.at[:, near, side_len:tile_len, :],
        field.at[:, far, side_len:tile_len, :],
        sends,
        receives,
        1,
        left,
    )
    under = remote(
        field.at[:, :own_blocks, :side_len, :],
        field.at[:, :own_blocks, tile_len:, :],
        sends,
        receives,
        2,
        up,
    )
    across = remote(
        field.at[:, far, :side_len, :], field.at[:, far, tile_len:, :], sends, receives, 3, up
    )

    def narrow(blocks, at):
        for c in range(2):
            for b in blocks:
                field[c, b, at, :] = own[c, at, b * LANES : (b + 1) * LANES].astype(jnp.bfloat16)

    first.wait()
    narrow(range(side_blocks), slice(0, side_len))
    meet((scan, tile))

    @pl.when(has_left)
    def _():
        top.start()

    second.wait()
    third.wait()
    narrow(range(side_blocks), slice(side_len, tile_len))
    narrow(range(side_blocks, own_blocks), slice(0, side_len))

    @pl.when(has_left)
    def _():
        rest.start()

    @pl.when(has_up)
    def _():
        under.start()

    @pl.when(jnp.logical_not(has_right))
    def _():
        field[:, far, :tile_len, :] = jnp.zeros(
            (2, side_blocks, tile_len, LANES), jnp.bfloat16
        )

    @pl.when(jnp.logical_not(has_down))
    def _():
        field[:, :, tile_len:, :] = jnp.zeros(
            (2, own_blocks + side_blocks, side_len, LANES), jnp.bfloat16
        )

    fourth.wait()
    narrow(range(side_blocks, own_blocks), slice(side_len, tile_len))
    for load in constants:
        load.wait()

    def sort_slot(slot, carry):
        rows = dot(sort[...], measured[slot]).astype(jnp.bfloat16)
        both = dot(rows, unsort[...]).astype(jnp.bfloat16)
        for b in range(RADIX):
            arranged[slot, b] = both[:, b * part : (b + 1) * part]
        return carry

    lax.fori_loop(0, slots, sort_slot, 0)

    grown[...] = jnp.zeros_like(grown)
    for q in range(RADIX):
        for i in range(2):
            for at in (0, part):
                doubled[q, i, at : at + part, :] = cols_ref[
                    q, i * part : (i + 1) * part, :part
                ].astype(jnp.float32)

    lane = lax.broadcasted_iota(jnp.int32, (1, LANES), 1)
    line = lax.broadcasted_iota(jnp.int32, (part, LANES), 0)
    chunk = 32

    def prepare(slot, carry):
        lift = lax.rem(shift_ref[0, slot], GROUP)
        turn = lax.rem(shift_ref[1, slot], LANES)

        def move_probe(i, carry):
            at = pl.multiple_of(i * chunk, chunk)
            for c in range(2):
                turned = [
                    pltpu.roll(extended[c, b, pl.ds(GROUP - lift + at, chunk), :], turn, 1)
                    for b in range(side_blocks)
                ]
                for b in range(side_blocks):
                    probes[slot, c, b, pl.ds(at, chunk), :] = jnp.where(
                        lane >= turn, turned[b], turned[b - 1]
                    )
            return carry

        lax.fori_loop(0, side_len // chunk, move_probe, 0)
        for k, by in enumerate((lift, turn)):
            for q in range(RADIX):
                cos = pltpu.roll(rows_ref[q, :part, :part].astype(jnp.float32), by, 1)
                sin = pltpu.roll(rows_ref[q, :part, part:].astype(jnp.float32), by, 1)
                cos, sin = in_place(lane >= by, cos, sin, q)
                tables[slot, 0, k, q, 0, :part, :] = cos.astype(jnp.bfloat16)
                tables[slot, 0, k, q, 1, :part, :] = sin.astype(jnp.bfloat16)
                tables[slot, 0, k, q, 0, part:, :] = (-sin).astype(jnp.bfloat16)
                tables[slot, 0, k, q, 1, part:, :] = cos.astype(jnp.bfloat16)
                cos = doubled[q, 0, pl.ds(part - by, part), :]
                sin = doubled[q, 1, pl.ds(part - by, part), :]
                cos, sin = in_place(line >= by, cos, sin, q)
                tables[slot, 1, k, q, 0, :part, :] = cos.astype(jnp.bfloat16)
                tables[slot, 1, k, q, 1, :part, :] = (-sin).astype(jnp.bfloat16)
                tables[slot, 1, k, q, 0, part:, :] = sin.astype(jnp.bfloat16)
                tables[slot, 1, k, q, 1, part:, :] = cos.astype(jnp.bfloat16)
        return carry

    lax.fori_loop(0, slots, prepare, 0)

    @pl.when(has_right)
    def _():
        top.wait_recv()

    @pl.when(has_up)
    def _():
        across.start()

    @pl.when(has_down)
    def _():
        under.wait_recv()

    @pl.when(has_right)
    def _():
        rest.wait_recv()

    @pl.when(has_down)
    def _():
        across.wait_recv()

    @pl.when(has_left)
    def _():
        top.wait_send()
        rest.wait_send()

    @pl.when(has_up)
    def _():
        under.wait_send()
        across.wait_send()


def gather(axes, shifts, own, measured, probe, tables):
    slots, side_len = measured.shape[:2]
    tile_len = own.shape[1]
    span = tile_len + side_len
    part = side_len // RADIX
    side_blocks = side_len // LANES
    hbm = pl.BlockSpec(memory_space=pltpu.HBM)
    vmem = pl.BlockSpec(memory_space=pltpu.VMEM)
    table = (slots, 2, 2, RADIX, 2, 2 * part, part)
    scratch = [
        (own.shape, jnp.float32),
        (measured.shape, jnp.bfloat16),
        ((2, side_blocks, side_len + GROUP, LANES), jnp.float32),
        (tables[0].shape, jnp.bfloat16),
        (tables[1].shape, jnp.bfloat16),
        ((RADIX, 2, 2 * part, part), jnp.float32),
        ((side_len, side_len), jnp.bfloat16),
        ((side_len, side_len), jnp.bfloat16),
    ]
    call = pl.pallas_call(
        functools.partial(gather_kernel, axes),
        out_shape=[
            pltpu.VMEM((2, span // LANES, span, LANES), jnp.bfloat16),
            pltpu.VMEM((slots, 2, side_blocks, side_len, LANES), jnp.float32),
            pltpu.VMEM(table, jnp.bfloat16),
            pltpu.VMEM((slots, RADIX, side_len, part), jnp.bfloat16),
            pltpu.VMEM((2, span // LANES, span, LANES), jnp.float32),
        ],
        in_specs=[pl.BlockSpec(memory_space=pltpu.SMEM)] + [hbm] * 7,
        out_specs=[vmem] * 5,
        scratch_shapes=[pltpu.VMEM(*each) for each in scratch]
        + [
            pltpu.SemaphoreType.DMA((4,)),
            pltpu.SemaphoreType.DMA((4,)),
            pltpu.SemaphoreType.DMA((9 + 4 * side_blocks,)),
        ],
        compiler_params=pltpu.CompilerParams(
            collective_id=0, has_side_effects=True, vmem_limit_bytes=room(scratch)
        ),
    )
    prepared = call(shifts, own, measured, probe, *tables, *sorted_by_residue(side_len))
    held = [pltpu.with_memory_space_constraint(each, pltpu.VMEM) for each in prepared]
    return held, room(scratch)


def room(scratch):
    return sum(math.prod(shape) * jnp.dtype(kind).itemsize for shape, kind in scratch) + (1 << 20)


def scatter_kernel(
    axes,
    grown,
    total,
    spill,
    dropped,
    both,
    landed,
    from_left,
    from_up,
    sends,
    receives,
):
    side_len = landed.shape[2]
    tile_len = total.shape[1]
    own_blocks = tile_len // LANES
    side_blocks = side_len // LANES
    scan, tile = neighbours(axes)
    has_left, _, has_right, right = scan
    has_up, _, has_down, down = tile
    corner = remote(both, landed, sends, receives, 0, down)
    under = remote(dropped, from_up, sends, receives, 1, down)
    rest = remote(
        spill.at[:, :, side_len:, :], from_left.at[:, :, side_len:, :], sends, receives, 2, right
    )
    top = remote(
        spill.at[:, :, :side_len, :], from_left.at[:, :, :side_len, :], sends, receives, 3, right
    )
    both[...] = grown[:, own_blocks:, tile_len:, :].astype(jnp.bfloat16)
    meet((scan, tile))

    @pl.when(has_down)
    def _():
        corner.start()

    spill[:, :, side_len:, :] = grown[:, own_blocks:, side_len:tile_len, :].astype(jnp.bfloat16)

    @pl.when(has_right)
    def _():
        rest.start()

    dropped[...] = grown[:, :own_blocks, tile_len:, :].astype(jnp.bfloat16)

    @pl.when(has_down)
    def _():
        under.start()

    @pl.when(jnp.logical_not(has_up))
    def _():
        landed[...] = jnp.zeros_like(landed)

    for c in range(2):
        for b in range(own_blocks):
            total[c, :, b * LANES : (b + 1) * LANES] = grown[c, b, :tile_len, :]

    @pl.when(has_up)
    def _():
        corner.wait_recv()

    spill[:, :, :side_len, :] = (
        grown[:, own_blocks:, :side_len, :] + landed[...].astype(jnp.float32)
    ).astype(jnp.bfloat16)

    @pl.when(has_right)
    def _():
        top.start()

    def add(blocks, at, source):
        for c in range(2):
            for b in blocks:
                total[c, at, b * LANES : (b + 1) * LANES] += source[c, b, at, :].astype(jnp.float32)

    @pl.when(has_left)
    def _():
        rest.wait_recv()
        add(range(side_blocks), slice(side_len, tile_len), from_left)

    @pl.when(has_up)
    def _():
        under.wait_recv()
        add(range(own_blocks), slice(0, side_len), from_up)

    @pl.when(has_left)
    def _():
        top.wait_recv()
        add(range(side_blocks), slice(0, side_len), from_left)

    @pl.when(has_right)
    def _():
        rest.wait_send()
        top.wait_send()

    @pl.when(has_down)
    def _():
        corner.wait_send()
        under.wait_send()


def scatter(axes, grown, tile_len):
    span = grown.shape[2]
    side_len = span - tile_len
    own_blocks = tile_len // LANES
    side_blocks = side_len // LANES
    vmem = pl.BlockSpec(memory_space=pltpu.VMEM)
    scratch = [
        ((2, side_blocks, tile_len, LANES), jnp.bfloat16),
        ((2, own_blocks, side_len, LANES), jnp.bfloat16),
        ((2, side_blocks, side_len, LANES), jnp.bfloat16),
        ((2, side_blocks, side_len, LANES), jnp.bfloat16),
        ((2, side_blocks, tile_len, LANES), jnp.bfloat16),
        ((2, own_blocks, side_len, LANES), jnp.bfloat16),
    ]
    return pl.pallas_call(
        functools.partial(scatter_kernel, axes),
        out_shape=pltpu.VMEM((2, tile_len, tile_len), jnp.float32),
        in_specs=[vmem],
        out_specs=vmem,
        scratch_shapes=[pltpu.VMEM(*each) for each in scratch]
        + [pltpu.SemaphoreType.DMA((4,)), pltpu.SemaphoreType.DMA((4,))],
        compiler_params=pltpu.CompilerParams(
            collective_id=1, has_side_effects=True, vmem_limit_bytes=room(scratch)
        ),
    )(grown)


def side_by_side(*blocks):
    return jnp.concatenate(blocks, axis=1)


def solve_kernel(
    live_ref,
    shift_ref,
    field,
    probes,
    tables,
    measured,
    zeros,
    grown,
    mixed,
    halves,
    misfits,
    spectra,
    backs,
):
    side_len = probes.shape[3]
    part = side_len // RADIX
    side_blocks = side_len // LANES
    lane = lax.broadcasted_iota(jnp.int32, (1, LANES), 1)
    line = lax.broadcasted_iota(jnp.int32, (GROUP, LANES), 0)

    def one_slot(slot, carry):
        row = shift_ref[0, slot]
        col = shift_ref[1, slot]
        lift = lax.rem(row, GROUP)
        turn = lax.rem(col, LANES)
        base = pl.multiple_of(row - lift, GROUP)
        block = lax.div(col, LANES)
        stay = lane >= turn
        below = line >= lift

        def table(side, kind, q):
            return side_by_side(tables[slot, side, kind, q, 0], tables[slot, side, kind, q, 1])

        def piece(c, b, at):
            def cut(b):
                start = pl.multiple_of(base + at, GROUP)
                value = field[c, block + b, pl.ds(start, GROUP), :].astype(jnp.float32)
                if at == 0:
                    start = pl.multiple_of(base + side_len, GROUP)
                    wrapped = field[c, block + b, pl.ds(start, GROUP), :].astype(jnp.float32)
                    value = jnp.where(below, value, wrapped)
                return value

            return cut(b) if b else jnp.where(stay, cut(0), cut(side_blocks))

        for at in range(0, part, GROUP):
            for b in range(side_blocks):
                waves = []
                for p in range(RADIX):
                    here = at + p * part
                    re, im = piece(0, b, here), piece(1, b, here)
                    probe_re = probes[slot, 0, b, here : here + GROUP, :]
                    probe_im = probes[slot, 1, b, here : here + GROUP, :]
                    waves.append((probe_re * re - probe_im * im, probe_re * im + probe_im * re))
                for q, (re, im) in enumerate(butterfly(waves, -1)):
                    mixed[q, b, at : at + GROUP, :] = re.astype(jnp.bfloat16)
                    mixed[q, b, at + part : at + part + GROUP, :] = im.astype(jnp.bfloat16)

        for q in range(RADIX):
            half = dot(table(0, 0, q), side_by_side(*(mixed[q, b] for b in range(RADIX))))
            parts = [
                (half[:part, p * part : (p + 1) * part], half[part:, p * part : (p + 1) * part])
                for p in range(RADIX)
            ]
            for other, (re, im) in enumerate(butterfly(parts, -1)):
                halves[other, 0, q * part : (q + 1) * part, :] = re.astype(jnp.bfloat16)
                halves[other, 1, q * part : (q + 1) * part, :] = im.astype(jnp.bfloat16)

        for other in range(RADIX):
            far = dot(side_by_side(halves[other, 0], halves[other, 1]), table(1, 1, other))
            for q in range(RADIX):
                rows = slice(q * part, (q + 1) * part)
                far_re, far_im = far[rows, :part], far[rows, part:]
                seen = measured[slot, other, rows, :].astype(jnp.float32)
                misfit = far_re * far_re + far_im * far_im - seen
                misfits[q, other, :part, :] = (misfit * far_re).astype(jnp.bfloat16)
                misfits[q, other, part:, :] = (misfit * far_im).astype(jnp.bfloat16)

        for q in range(RADIX):
            mixture = dot(
                table(1, 0, q), side_by_side(*(misfits[q, b] for b in range(RADIX)))
            )
            for b in range(RADIX):
                spectra[q, b] = mixture[:, b * part : (b + 1) * part]

        for at in range(0, part, GROUP):
            for other in range(RADIX):
                parts = [
                    (spectra[q, other, at : at + GROUP, :], spectra[q, other, part + at : part + at + GROUP, :])
                    for q in range(RADIX)
                ]
                for p, (re, im) in enumerate(butterfly(parts, 1)):
                    here = slice(at + p * part, at + p * part + GROUP)
                    backs[other, 0, here, :] = re.astype(jnp.bfloat16)
                    backs[other, 1, here, :] = im.astype(jnp.bfloat16)

        tall = TALL

        def add(c, b, at, value):
            where = pl.ds(pl.multiple_of(base + at, GROUP), value.shape[0])
            grown[c, block + b, where, :] += value

        def add_wrapped(c, b, at, value):
            if at == 0:
                add(c, b, 0, jnp.where(below, value[:GROUP], 0.0))
                add(c, b, side_len, jnp.where(below, 0.0, value[:GROUP]))
                add(c, b, GROUP, value[GROUP:])
            else:
                add(c, b, at, value)

        for at in range(0, side_len, tall):
            parts = []
            for other in range(RADIX):
                back = side_by_side(
                    backs[other, 0, at : at + tall, :], backs[other, 1, at : at + tall, :]
                )
                grad = dot(back, table(0, 1, other))
                parts.append((grad[:, :part], grad[:, part:]))
            for b, (re, im) in enumerate(butterfly(parts, 1)):
                probe_re = probes[slot, 0, b, at : at + tall, :]
                probe_im = probes[slot, 1, b, at : at + tall, :]
                values = (probe_re * re + probe_im * im, probe_re * im - probe_im * re)
                for c, value in enumerate(values):
                    if b == 0:
                        add_wrapped(c, 0, at, jnp.where(stay, value, 0.0))
                        add_wrapped(c, side_blocks, at, jnp.where(stay, 0.0, value))
                    else:
                        add_wrapped(c, b, at, value)
        return carry

    lax.fori_loop(0, live_ref[0, lax.axis_index("scan")], one_slot, 0)


def solve(live_counts, shifts, prepared, limit):
    grown = prepared[-1]
    side_len = prepared[1].shape[3]
    part = side_len // RADIX
    smem = pl.BlockSpec(memory_space=pltpu.SMEM)
    vmem = pl.BlockSpec(memory_space=pltpu.VMEM)
    wide = (RADIX, RADIX, 2 * part, part)
    tall = (RADIX, 2, side_len, part)
    scratch = [
        (wide, jnp.bfloat16),
        (tall, jnp.bfloat16),
        (wide, jnp.bfloat16),
        (wide, jnp.float32),
        (tall, jnp.bfloat16),
    ]
    return pl.pallas_call(
        solve_kernel,
        out_shape=pltpu.VMEM(grown.shape, grown.dtype),
        in_specs=[smem, smem] + [vmem] * len(prepared),
        out_specs=vmem,
        scratch_shapes=[pltpu.VMEM(*each) for each in scratch],
        input_output_aliases={1 + len(prepared): 0},
        compiler_params=pltpu.CompilerParams(vmem_limit_bytes=limit),
    )(live_counts, shifts, *prepared)


def shards(axes, object_slab, probe_field, intensities, offsets, live_count):
    tables = residue_tables(probe_field.shape[-1])
    shifts = offsets[0, 0].T
    prepared, limit = gather(axes, shifts, object_slab, intensities[0, 0], probe_field, tables)
    grown = solve(live_count.T, shifts, prepared, limit)
    return scatter(axes, grown, object_slab.shape[1])


def solution(mesh):
    placed = (
        P(None, "tile", "scan"),
        P(),
        P("scan", "tile", None, None, None),
        P("scan", "tile", None, None),
        P(None, "tile"),
    )
    axes = tuple((name, mesh.shape[name]) for name in ("scan", "tile"))
    return jax.shard_map(
        functools.partial(shards, axes), mesh=mesh, in_specs=placed, out_specs=P(None, "tile", "scan"), check_vma=False
    )
```

```python
import functools
import math

import jax
import jax.numpy as jnp
import numpy as np
from jax import lax
from jax.experimental import pallas as pl
from jax.experimental.pallas import tpu as pltpu
from jax.sharding import PartitionSpec as P

RADIX = 4
LANES = 128
GROUP = 16
TALL = 256


def residue_tables(side_len):
    part = side_len // RADIX
    freq = np.arange(side_len).reshape(part, RADIX).T
    across = np.arange(part)
    phase = (freq[:, :, None] * across[None, None, :] % side_len) * (2.0 * math.pi / side_len)
    factor = 1.0 / math.sqrt(side_len)
    cos = np.cos(phase) * factor
    sin = np.sin(phase) * factor
    rows = np.concatenate(
        [np.concatenate([cos, sin], axis=2), np.concatenate([-sin, cos], axis=2)], axis=1
    ).astype(np.float32)
    return jnp.asarray(rows, jnp.bfloat16), jnp.asarray(rows.swapaxes(1, 2), jnp.bfloat16)


def sorted_by_residue(side_len):
    at = np.arange(side_len)
    source = at % (side_len // RADIX) * RADIX + at // (side_len // RADIX)
    sort = (source[:, None] == at[None, :]).astype(np.float32)
    return jnp.asarray(sort, jnp.bfloat16), jnp.asarray(sort.T, jnp.bfloat16)


def dot(a, b):
    return jnp.dot(a, b, preferred_element_type=jnp.float32)


def butterfly(parts, sign):
    (r0, i0), (r1, i1), (r2, i2), (r3, i3) = parts
    ar, ai, br, bi = r0 + r2, i0 + i2, r1 + r3, i1 + i3
    cr, ci, dr, di = r0 - r2, i0 - i2, r1 - r3, i1 - i3
    plus = (cr - di, ci + dr)
    minus = (cr + di, ci - dr)
    first, third = (plus, minus) if sign > 0 else (minus, plus)
    return [(ar + br, ai + bi), first, (ar - br, ai - bi), third]


def neighbours(axes):
    result = []
    for name, count in axes:
        me = lax.axis_index(name)
        result.append((me > 0, {name: me - 1}, me < count - 1, {name: me + 1}))
    return result


def greet(peers):
    barrier = pltpu.get_barrier_semaphore()
    for has_low, low, has_high, high in peers:
        for there, peer in ((has_low, low), (has_high, high)):

            @pl.when(there)
            def _(peer=peer):
                pl.semaphore_signal(
                    barrier, inc=1, device_id=peer, device_id_type=pl.DeviceIdType.MESH
                )


def all_here(peers):
    count = sum(
        there.astype(jnp.int32) for has_low, _, has_high, _ in peers for there in (has_low, has_high)
    )
    pl.semaphore_wait(pltpu.get_barrier_semaphore(), count)


def remote(source, target, sends, receives, index, peer):
    return pltpu.make_async_remote_copy(
        src_ref=source,
        dst_ref=target,
        send_sem=sends.at[index],
        recv_sem=receives.at[index],
        device_id=peer,
        device_id_type=pl.DeviceIdType.MESH,
    )


def quarter_turns(cos, sin, q):
    return ((cos, sin), (sin, -cos), (-cos, -sin), (-sin, cos))[q]


def in_place(mask, cos, sin, q):
    wrapped = quarter_turns(cos, sin, q)
    return jnp.where(mask, cos, wrapped[0]), jnp.where(mask, sin, wrapped[1])


def gather_kernel(
    axes,
    shift_ref,
    own_hbm,
    measured_hbm,
    probe_hbm,
    rows_hbm,
    cols_hbm,
    sort_hbm,
    unsort_hbm,
    field,
    probes,
    tables,
    arranged,
    grown,
    own,
    measured,
    extended,
    rows_ref,
    cols_ref,
    doubled,
    sort,
    unsort,
    sends,
    receives,
    fetches,
):
    slots, side_len = measured.shape[:2]
    tile_len = own.shape[1]
    part = side_len // RADIX
    own_blocks = tile_len // LANES
    side_blocks = side_len // LANES
    scan, tile = neighbours(axes)
    has_left, left, has_right, _ = scan
    has_up, up, has_down, _ = tile
    greet((scan, tile))
    first = pltpu.make_async_copy(
        own_hbm.at[:, :side_len, :side_len], own.at[:, :side_len, :side_len], fetches.at[0]
    )
    second = pltpu.make_async_copy(
        own_hbm.at[:, side_len:, :side_len], own.at[:, side_len:, :side_len], fetches.at[1]
    )
    third = pltpu.make_async_copy(
        own_hbm.at[:, :side_len, side_len:], own.at[:, :side_len, side_len:], fetches.at[2]
    )
    fourth = pltpu.make_async_copy(
        own_hbm.at[:, side_len:, side_len:], own.at[:, side_len:, side_len:], fetches.at[3]
    )
    constants = [
        pltpu.make_async_copy(source, target, fetches.at[4 + i])
        for i, (source, target) in enumerate(
            (
                (sort_hbm, sort),
                (unsort_hbm, unsort),
                (measured_hbm, measured),
                (rows_hbm, rows_ref),
                (cols_hbm, cols_ref),
            )
        )
    ]
    for c in range(2):
        for b in range(side_blocks):
            cols = slice(b * LANES, (b + 1) * LANES)
            for source, target in (
                (probe_hbm.at[c, :, cols], extended.at[c, b, GROUP:, :]),
                (probe_hbm.at[c, side_len - GROUP :, cols], extended.at[c, b, :GROUP, :]),
            ):
                constants.append(
                    pltpu.make_async_copy(source, target, fetches.at[4 + len(constants)])
                )
    for load in [first, second, third, fourth] + constants:
        load.start()
    near = slice(0, side_blocks)
    far = slice(own_blocks, own_blocks + side_blocks)
    halves = [
        (c, slice(at, at + side_blocks // 2))
        for c in range(2)
        for at in range(0, side_blocks, side_blocks // 2)
    ]

    def moved(blocks):
        return slice(blocks.start + own_blocks, blocks.stop + own_blocks)

    tops = [
        remote(
            field.at[c, blocks, :side_len, :],
            field.at[c, moved(blocks), :side_len, :],
            sends,
            receives,
            3 + i,
            left,
        )
        for i, (c, blocks) in enumerate(halves)
    ]
    rest = remote(
        field.at[:, near, side_len:tile_len, :],
        field.at[:, far, side_len:tile_len, :],
        sends,
        receives,
        1,
        left,
    )
    under = remote(
        field.at[:, :own_blocks, :side_len, :],
        field.at[:, :own_blocks, tile_len:, :],
        sends,
        receives,
        2,
        up,
    )
    acrosses = [
        remote(
            field.at[c, moved(blocks), :side_len, :],
            field.at[c, moved(blocks), tile_len:, :],
            sends,
            receives,
            3 + len(halves) + i,
            up,
        )
        for i, (c, blocks) in enumerate(halves)
    ]

    def narrow(blocks, at):
        for c in range(2):
            for b in blocks:
                field[c, b, at, :] = own[c, at, b * LANES : (b + 1) * LANES].astype(jnp.bfloat16)

    first.wait()
    narrow(range(side_blocks), slice(0, side_len))
    all_here((scan, tile))

    @pl.when(has_left)
    def _():
        for each in tops:
            each.start()

    second.wait()
    third.wait()
    narrow(range(side_blocks), slice(side_len, tile_len))
    narrow(range(side_blocks, own_blocks), slice(0, side_len))

    @pl.when(has_left)
    def _():
        rest.start()

    @pl.when(has_up)
    def _():
        under.start()

    @pl.when(jnp.logical_not(has_right))
    def _():
        field[:, far, :tile_len, :] = jnp.zeros(
            (2, side_blocks, tile_len, LANES), jnp.bfloat16
        )

    @pl.when(jnp.logical_not(has_down))
    def _():
        field[:, :, tile_len:, :] = jnp.zeros(
            (2, own_blocks + side_blocks, side_len, LANES), jnp.bfloat16
        )

    fourth.wait()
    narrow(range(side_blocks, own_blocks), slice(side_len, tile_len))
    for load in constants:
        load.wait()

    def sort_slot(slot, carry):
        rows = dot(sort[...], measured[slot]).astype(jnp.bfloat16)
        both = dot(rows, unsort[...]).astype(jnp.bfloat16)
        for b in range(RADIX):
            arranged[slot, b] = both[:, b * part : (b + 1) * part]
        return carry

    lax.fori_loop(0, slots, sort_slot, 0)

    grown[...] = jnp.zeros_like(grown)
    for q in range(RADIX):
        for i in range(2):
            for at in (0, part):
                doubled[q, i, at : at + part, :] = cols_ref[
                    q, i * part : (i + 1) * part, :part
                ].astype(jnp.float32)

    lane = lax.broadcasted_iota(jnp.int32, (1, LANES), 1)
    line = lax.broadcasted_iota(jnp.int32, (part, LANES), 0)
    chunk = 32

    def prepare(slot, carry):
        lift = lax.rem(shift_ref[0, slot], GROUP)
        turn = lax.rem(shift_ref[1, slot], LANES)

        def move_probe(i, carry):
            at = pl.multiple_of(i * chunk, chunk)
            for c in range(2):
                turned = [
                    pltpu.roll(extended[c, b, pl.ds(GROUP - lift + at, chunk), :], turn, 1)
                    for b in range(side_blocks)
                ]
                for b in range(side_blocks):
                    probes[slot, c, b, pl.ds(at, chunk), :] = jnp.where(
                        lane >= turn, turned[b], turned[b - 1]
                    )
            return carry

        lax.fori_loop(0, side_len // chunk, move_probe, 0)
        for k, by in enumerate((lift, turn)):
            for q in range(RADIX):
                cos = pltpu.roll(rows_ref[q, :part, :part].astype(jnp.float32), by, 1)
                sin = pltpu.roll(rows_ref[q, :part, part:].astype(jnp.float32), by, 1)
                cos, sin = in_place(lane >= by, cos, sin, q)
                tables[slot, 0, k, q, 0, :part, :] = cos.astype(jnp.bfloat16)
                tables[slot, 0, k, q, 1, :part, :] = sin.astype(jnp.bfloat16)
                tables[slot, 0, k, q, 0, part:, :] = (-sin).astype(jnp.bfloat16)
                tables[slot, 0, k, q, 1, part:, :] = cos.astype(jnp.bfloat16)
                cos = doubled[q, 0, pl.ds(part - by, part), :]
                sin = doubled[q, 1, pl.ds(part - by, part), :]
                cos, sin = in_place(line >= by, cos, sin, q)
                tables[slot, 1, k, q, 0, :part, :] = cos.astype(jnp.bfloat16)
                tables[slot, 1, k, q, 1, :part, :] = (-sin).astype(jnp.bfloat16)
                tables[slot, 1, k, q, 0, part:, :] = sin.astype(jnp.bfloat16)
                tables[slot, 1, k, q, 1, part:, :] = cos.astype(jnp.bfloat16)
        return carry

    lax.fori_loop(0, slots, prepare, 0)

    for top, across in zip(tops, acrosses):

        @pl.when(has_right)
        def _(top=top):
            top.wait_recv()

        @pl.when(has_up)
        def _(across=across):
            across.start()

    @pl.when(has_down)
    def _():
        under.wait_recv()

    @pl.when(has_right)
    def _():
        rest.wait_recv()

    @pl.when(has_down)
    def _():
        for each in acrosses:
            each.wait_recv()

    @pl.when(has_left)
    def _():
        for each in tops:
            each.wait_send()
        rest.wait_send()

    @pl.when(has_up)
    def _():
        under.wait_send()
        for each in acrosses:
            each.wait_send()


def gather(axes, shifts, own, measured, probe, tables):
    slots, side_len = measured.shape[:2]
    tile_len = own.shape[1]
    span = tile_len + side_len
    part = side_len // RADIX
    side_blocks = side_len // LANES
    hbm = pl.BlockSpec(memory_space=pltpu.HBM)
    vmem = pl.BlockSpec(memory_space=pltpu.VMEM)
    table = (slots, 2, 2, RADIX, 2, 2 * part, part)
    scratch = [
        (own.shape, jnp.float32),
        (measured.shape, jnp.bfloat16),
        ((2, side_blocks, side_len + GROUP, LANES), jnp.float32),
        (tables[0].shape, jnp.bfloat16),
        (tables[1].shape, jnp.bfloat16),
        ((RADIX, 2, 2 * part, part), jnp.float32),
        ((side_len, side_len), jnp.bfloat16),
        ((side_len, side_len), jnp.bfloat16),
    ]
    call = pl.pallas_call(
        functools.partial(gather_kernel, axes),
        out_shape=[
            pltpu.VMEM((2, span // LANES, span, LANES), jnp.bfloat16),
            pltpu.VMEM((slots, 2, side_blocks, side_len, LANES), jnp.float32),
            pltpu.VMEM(table, jnp.bfloat16),
            pltpu.VMEM((slots, RADIX, side_len, part), jnp.bfloat16),
            pltpu.VMEM((2, span // LANES, span, LANES), jnp.float32),
        ],
        in_specs=[pl.BlockSpec(memory_space=pltpu.SMEM)] + [hbm] * 7,
        out_specs=[vmem] * 5,
        scratch_shapes=[pltpu.VMEM(*each) for each in scratch]
        + [
            pltpu.SemaphoreType.DMA((3 + 8,)),
            pltpu.SemaphoreType.DMA((3 + 8,)),
            pltpu.SemaphoreType.DMA((9 + 4 * side_blocks,)),
        ],
        compiler_params=pltpu.CompilerParams(
            collective_id=0, has_side_effects=True, vmem_limit_bytes=room(scratch)
        ),
    )
    prepared = call(shifts, own, measured, probe, *tables, *sorted_by_residue(side_len))
    held = [pltpu.with_memory_space_constraint(each, pltpu.VMEM) for each in prepared]
    return held, room(scratch)


def room(scratch):
    return sum(math.prod(shape) * jnp.dtype(kind).itemsize for shape, kind in scratch) + (1 << 20)


def scatter_kernel(
    axes,
    grown,
    total,
    spill,
    dropped,
    both,
    landed,
    from_left,
    from_up,
    sends,
    receives,
):
    side_len = landed.shape[2]
    tile_len = total.shape[1]
    own_blocks = tile_len // LANES
    side_blocks = side_len // LANES
    scan, tile = neighbours(axes)
    has_left, _, has_right, right = scan
    has_up, _, has_down, down = tile
    corner = remote(both, landed, sends, receives, 0, down)
    under = remote(dropped, from_up, sends, receives, 1, down)
    rest = remote(
        spill.at[:, :, side_len:, :], from_left.at[:, :, side_len:, :], sends, receives, 2, right
    )
    top = remote(
        spill.at[:, :, :side_len, :], from_left.at[:, :, :side_len, :], sends, receives, 3, right
    )
    greet((scan, tile))
    spill[:, :, side_len:, :] = grown[:, own_blocks:, side_len:tile_len, :].astype(jnp.bfloat16)
    both[...] = grown[:, own_blocks:, tile_len:, :].astype(jnp.bfloat16)
    all_here((scan, tile))

    @pl.when(has_right)
    def _():
        rest.start()

    @pl.when(has_down)
    def _():
        corner.start()

    dropped[...] = grown[:, :own_blocks, tile_len:, :].astype(jnp.bfloat16)

    @pl.when(has_down)
    def _():
        under.start()

    @pl.when(jnp.logical_not(has_up))
    def _():
        landed[...] = jnp.zeros_like(landed)

    for c in range(2):
        for b in range(own_blocks):
            total[c, :, b * LANES : (b + 1) * LANES] = grown[c, b, :tile_len, :]

    @pl.when(has_up)
    def _():
        corner.wait_recv()

    spill[:, :, :side_len, :] = (
        grown[:, own_blocks:, :side_len, :] + landed[...].astype(jnp.float32)
    ).astype(jnp.bfloat16)

    @pl.when(has_right)
    def _():
        top.start()

    def add(blocks, at, source):
        for c in range(2):
            for b in blocks:
                total[c, at, b * LANES : (b + 1) * LANES] += source[c, b, at, :].astype(jnp.float32)

    @pl.when(has_left)
    def _():
        rest.wait_recv()
        add(range(side_blocks), slice(side_len, tile_len), from_left)

    @pl.when(has_up)
    def _():
        under.wait_recv()
        add(range(own_blocks), slice(0, side_len), from_up)

    @pl.when(has_left)
    def _():
        top.wait_recv()
        add(range(side_blocks), slice(0, side_len), from_left)

    @pl.when(has_right)
    def _():
        rest.wait_send()
        top.wait_send()

    @pl.when(has_down)
    def _():
        corner.wait_send()
        under.wait_send()


def scatter(axes, grown, tile_len):
    span = grown.shape[2]
    side_len = span - tile_len
    own_blocks = tile_len // LANES
    side_blocks = side_len // LANES
    vmem = pl.BlockSpec(memory_space=pltpu.VMEM)
    scratch = [
        ((2, side_blocks, tile_len, LANES), jnp.bfloat16),
        ((2, own_blocks, side_len, LANES), jnp.bfloat16),
        ((2, side_blocks, side_len, LANES), jnp.bfloat16),
        ((2, side_blocks, side_len, LANES), jnp.bfloat16),
        ((2, side_blocks, tile_len, LANES), jnp.bfloat16),
        ((2, own_blocks, side_len, LANES), jnp.bfloat16),
    ]
    return pl.pallas_call(
        functools.partial(scatter_kernel, axes),
        out_shape=pltpu.VMEM((2, tile_len, tile_len), jnp.float32),
        in_specs=[vmem],
        out_specs=vmem,
        scratch_shapes=[pltpu.VMEM(*each) for each in scratch]
        + [pltpu.SemaphoreType.DMA((4,)), pltpu.SemaphoreType.DMA((4,))],
        compiler_params=pltpu.CompilerParams(
            collective_id=1, has_side_effects=True, vmem_limit_bytes=room(scratch)
        ),
    )(grown)


def side_by_side(*blocks):
    return jnp.concatenate(blocks, axis=1)


def solve_kernel(
    live_ref,
    shift_ref,
    field,
    probes,
    tables,
    measured,
    zeros,
    grown,
    mixed,
    halves,
    misfits,
    spectra,
    backs,
):
    side_len = probes.shape[3]
    part = side_len // RADIX
    side_blocks = side_len // LANES
    lane = lax.broadcasted_iota(jnp.int32, (1, LANES), 1)
    line = lax.broadcasted_iota(jnp.int32, (GROUP, LANES), 0)

    def one_slot(slot, carry):
        row = shift_ref[0, slot]
        col = shift_ref[1, slot]
        lift = lax.rem(row, GROUP)
        turn = lax.rem(col, LANES)
        base = pl.multiple_of(row - lift, GROUP)
        block = lax.div(col, LANES)
        stay = lane >= turn
        below = line >= lift

        def table(side, kind, q):
            return side_by_side(tables[slot, side, kind, q, 0], tables[slot, side, kind, q, 1])

        def piece(c, b, at):
            def cut(b):
                start = pl.multiple_of(base + at, GROUP)
                value = field[c, block + b, pl.ds(start, GROUP), :].astype(jnp.float32)
                if at == 0:
                    start = pl.multiple_of(base + side_len, GROUP)
                    wrapped = field[c, block + b, pl.ds(start, GROUP), :].astype(jnp.float32)
                    value = jnp.where(below, value, wrapped)
                return value

            return cut(b) if b else jnp.where(stay, cut(0), cut(side_blocks))

        for at in range(0, part, GROUP):
            for b in range(side_blocks):
                waves = []
                for p in range(RADIX):
                    here = at + p * part
                    re, im = piece(0, b, here), piece(1, b, here)
                    probe_re = probes[slot, 0, b, here : here + GROUP, :]
                    probe_im = probes[slot, 1, b, here : here + GROUP, :]
                    waves.append((probe_re * re - probe_im * im, probe_re * im + probe_im * re))
                for q, (re, im) in enumerate(butterfly(waves, -1)):
                    mixed[q, b, at : at + GROUP, :] = re.astype(jnp.bfloat16)
                    mixed[q, b, at + part : at + part + GROUP, :] = im.astype(jnp.bfloat16)

        for q in range(RADIX):
            half = dot(table(0, 0, q), side_by_side(*(mixed[q, b] for b in range(RADIX))))
            parts = [
                (half[:part, p * part : (p + 1) * part], half[part:, p * part : (p + 1) * part])
                for p in range(RADIX)
            ]
            for other, (re, im) in enumerate(butterfly(parts, -1)):
                halves[other, 0, q * part : (q + 1) * part, :] = re.astype(jnp.bfloat16)
                halves[other, 1, q * part : (q + 1) * part, :] = im.astype(jnp.bfloat16)

        for other in range(RADIX):
            far = dot(side_by_side(halves[other, 0], halves[other, 1]), table(1, 1, other))
            for q in range(RADIX):
                rows = slice(q * part, (q + 1) * part)
                far_re, far_im = far[rows, :part], far[rows, part:]
                seen = measured[slot, other, rows, :].astype(jnp.float32)
                misfit = far_re * far_re + far_im * far_im - seen
                misfits[q, other, :part, :] = (misfit * far_re).astype(jnp.bfloat16)
                misfits[q, other, part:, :] = (misfit * far_im).astype(jnp.bfloat16)

        for q in range(RADIX):
            mixture = dot(
                table(1, 0, q), side_by_side(*(misfits[q, b] for b in range(RADIX)))
            )
            for b in range(RADIX):
                spectra[q, b] = mixture[:, b * part : (b + 1) * part]

        for at in range(0, part, GROUP):
            for other in range(RADIX):
                parts = [
                    (spectra[q, other, at : at + GROUP, :], spectra[q, other, part + at : part + at + GROUP, :])
                    for q in range(RADIX)
                ]
                for p, (re, im) in enumerate(butterfly(parts, 1)):
                    here = slice(at + p * part, at + p * part + GROUP)
                    backs[other, 0, here, :] = re.astype(jnp.bfloat16)
                    backs[other, 1, here, :] = im.astype(jnp.bfloat16)

        tall = TALL

        def add(c, b, at, value):
            where = pl.ds(pl.multiple_of(base + at, GROUP), value.shape[0])
            grown[c, block + b, where, :] += value

        def add_wrapped(c, b, at, value):
            if at == 0:
                add(c, b, 0, jnp.where(below, value[:GROUP], 0.0))
                add(c, b, side_len, jnp.where(below, 0.0, value[:GROUP]))
                add(c, b, GROUP, value[GROUP:])
            else:
                add(c, b, at, value)

        for at in range(0, side_len, tall):
            parts = []
            for other in range(RADIX):
                back = side_by_side(
                    backs[other, 0, at : at + tall, :], backs[other, 1, at : at + tall, :]
                )
                grad = dot(back, table(0, 1, other))
                parts.append((grad[:, :part], grad[:, part:]))
            for b, (re, im) in enumerate(butterfly(parts, 1)):
                probe_re = probes[slot, 0, b, at : at + tall, :]
                probe_im = probes[slot, 1, b, at : at + tall, :]
                values = (probe_re * re + probe_im * im, probe_re * im - probe_im * re)
                for c, value in enumerate(values):
                    if b == 0:
                        add_wrapped(c, 0, at, jnp.where(stay, value, 0.0))
                        add_wrapped(c, side_blocks, at, jnp.where(stay, 0.0, value))
                    else:
                        add_wrapped(c, b, at, value)
        return carry

    lax.fori_loop(0, live_ref[0, lax.axis_index("scan")], one_slot, 0)


def solve(live_counts, shifts, prepared, limit):
    grown = prepared[-1]
    side_len = prepared[1].shape[3]
    part = side_len // RADIX
    smem = pl.BlockSpec(memory_space=pltpu.SMEM)
    vmem = pl.BlockSpec(memory_space=pltpu.VMEM)
    wide = (RADIX, RADIX, 2 * part, part)
    tall = (RADIX, 2, side_len, part)
    scratch = [
        (wide, jnp.bfloat16),
        (tall, jnp.bfloat16),
        (wide, jnp.bfloat16),
        (wide, jnp.float32),
        (tall, jnp.bfloat16),
    ]
    return pl.pallas_call(
        solve_kernel,
        out_shape=pltpu.VMEM(grown.shape, grown.dtype),
        in_specs=[smem, smem] + [vmem] * len(prepared),
        out_specs=vmem,
        scratch_shapes=[pltpu.VMEM(*each) for each in scratch],
        input_output_aliases={1 + len(prepared): 0},
        compiler_params=pltpu.CompilerParams(vmem_limit_bytes=limit),
    )(live_counts, shifts, *prepared)


def shards(axes, object_slab, probe_field, intensities, offsets, live_count):
    tables = residue_tables(probe_field.shape[-1])
    shifts = offsets[0, 0].T
    prepared, limit = gather(axes, shifts, object_slab, intensities[0, 0], probe_field, tables)
    grown = solve(live_count.T, shifts, prepared, limit)
    return scatter(axes, grown, object_slab.shape[1])


def solution(mesh):
    placed = (
        P(None, "tile", "scan"),
        P(),
        P("scan", "tile", None, None, None),
        P("scan", "tile", None, None),
        P(None, "tile"),
    )
    axes = tuple((name, mesh.shape[name]) for name in ("scan", "tile"))
    return jax.shard_map(
        functools.partial(shards, axes), mesh=mesh, in_specs=placed, out_specs=P(None, "tile", "scan"), check_vma=False
    )
```

```python
import functools
import math

import jax
import jax.numpy as jnp
import numpy as np
from jax import lax
from jax.experimental import pallas as pl
from jax.experimental.pallas import tpu as pltpu
from jax.sharding import PartitionSpec as P

RADIX = 4
LANES = 128
GROUP = 16


def residue_tables(side_len):
    part = side_len // RADIX
    freq = np.arange(side_len).reshape(part, RADIX).T
    across = np.arange(part)
    phase = (freq[:, :, None] * across[None, None, :] % side_len) * (2.0 * math.pi / side_len)
    factor = 1.0 / math.sqrt(side_len)
    cos = np.cos(phase) * factor
    sin = np.sin(phase) * factor
    rows = np.concatenate(
        [np.concatenate([cos, sin], axis=2), np.concatenate([-sin, cos], axis=2)], axis=1
    ).astype(np.float32)
    return jnp.asarray(rows, jnp.bfloat16), jnp.asarray(rows.swapaxes(1, 2), jnp.bfloat16)


def sorted_by_residue(side_len):
    at = np.arange(side_len)
    source = at % (side_len // RADIX) * RADIX + at // (side_len // RADIX)
    sort = (source[:, None] == at[None, :]).astype(np.float32)
    return jnp.asarray(sort, jnp.bfloat16), jnp.asarray(sort.T, jnp.bfloat16)


def dot(a, b):
    return jnp.dot(a, b, preferred_element_type=jnp.float32)


def butterfly(parts, sign):
    (r0, i0), (r1, i1), (r2, i2), (r3, i3) = parts
    ar, ai, br, bi = r0 + r2, i0 + i2, r1 + r3, i1 + i3
    cr, ci, dr, di = r0 - r2, i0 - i2, r1 - r3, i1 - i3
    plus = (cr - di, ci + dr)
    minus = (cr + di, ci - dr)
    first, third = (plus, minus) if sign > 0 else (minus, plus)
    return [(ar + br, ai + bi), first, (ar - br, ai - bi), third]


def neighbours(axes):
    result = []
    for name, count in axes:
        me = lax.axis_index(name)
        result.append((me > 0, {name: me - 1}, me < count - 1, {name: me + 1}))
    return result


def greet(peers):
    barrier = pltpu.get_barrier_semaphore()
    for has_low, low, has_high, high in peers:
        for there, peer in ((has_low, low), (has_high, high)):

            @pl.when(there)
            def _(peer=peer):
                pl.semaphore_signal(
                    barrier, inc=1, device_id=peer, device_id_type=pl.DeviceIdType.MESH
                )


def all_here(peers):
    count = sum(
        there.astype(jnp.int32) for has_low, _, has_high, _ in peers for there in (has_low, has_high)
    )
    pl.semaphore_wait(pltpu.get_barrier_semaphore(), count)


def remote(source, target, sends, receives, index, peer):
    return pltpu.make_async_remote_copy(
        src_ref=source,
        dst_ref=target,
        send_sem=sends.at[index],
        recv_sem=receives.at[index],
        device_id=peer,
        device_id_type=pl.DeviceIdType.MESH,
    )


def quarter_turns(cos, sin, q):
    return ((cos, sin), (sin, -cos), (-cos, -sin), (-sin, cos))[q]


def in_place(mask, cos, sin, q):
    wrapped = quarter_turns(cos, sin, q)
    return jnp.where(mask, cos, wrapped[0]), jnp.where(mask, sin, wrapped[1])


def gather_kernel(
    axes,
    shift_ref,
    own_hbm,
    measured_hbm,
    probe_hbm,
    rows_hbm,
    cols_hbm,
    sort_hbm,
    unsort_hbm,
    field,
    probes,
    tables,
    arranged,
    grown,
    own,
    measured,
    extended,
    rows_ref,
    cols_ref,
    doubled,
    sort,
    unsort,
    sends,
    receives,
    fetches,
    freed,
):
    slots, side_len = measured.shape[:2]
    tile_len = own.shape[1]
    part = side_len // RADIX
    own_blocks = tile_len // LANES
    side_blocks = side_len // LANES
    scan, tile = neighbours(axes)
    has_left, left, has_right, _ = scan
    has_up, up, has_down, down = tile
    greet((scan, tile))
    first = pltpu.make_async_copy(
        own_hbm.at[:, :side_len, :side_len], own.at[:, :side_len, :side_len], fetches.at[0]
    )
    second = pltpu.make_async_copy(
        own_hbm.at[:, side_len:, :side_len], own.at[:, side_len:, :side_len], fetches.at[1]
    )
    third = pltpu.make_async_copy(
        own_hbm.at[:, :side_len, side_len:], own.at[:, :side_len, side_len:], fetches.at[2]
    )
    fourth = pltpu.make_async_copy(
        own_hbm.at[:, side_len:, side_len:], own.at[:, side_len:, side_len:], fetches.at[3]
    )
    constants = [
        pltpu.make_async_copy(source, target, fetches.at[4 + i])
        for i, (source, target) in enumerate(
            (
                (sort_hbm, sort),
                (unsort_hbm, unsort),
                (measured_hbm, measured),
                (rows_hbm, rows_ref),
                (cols_hbm, cols_ref),
            )
        )
    ]
    for c in range(2):
        for b in range(side_blocks):
            cols = slice(b * LANES, (b + 1) * LANES)
            for source, target in (
                (probe_hbm.at[c, :, cols], extended.at[c, b, GROUP:, :]),
                (probe_hbm.at[c, side_len - GROUP :, cols], extended.at[c, b, :GROUP, :]),
            ):
                constants.append(
                    pltpu.make_async_copy(source, target, fetches.at[4 + len(constants)])
                )
    for load in [first, second, third, fourth] + constants:
        load.start()
    near = slice(0, side_blocks)
    far = slice(own_blocks, own_blocks + side_blocks)
    halves = [
        (c, slice(at, at + side_blocks // 2))
        for c in range(2)
        for at in range(0, side_blocks, side_blocks // 2)
    ]

    def moved(blocks):
        return slice(blocks.start + own_blocks, blocks.stop + own_blocks)

    tops = [
        remote(
            field.at[c, blocks, :side_len, :],
            field.at[c, moved(blocks), :side_len, :],
            sends,
            receives,
            3 + i,
            left,
        )
        for i, (c, blocks) in enumerate(halves)
    ]
    rest = remote(
        field.at[:, near, side_len:tile_len, :],
        field.at[:, far, side_len:tile_len, :],
        sends,
        receives,
        1,
        left,
    )
    under = remote(
        field.at[:, :own_blocks, :side_len, :],
        field.at[:, :own_blocks, tile_len:, :],
        sends,
        receives,
        2,
        up,
    )
    acrosses = [
        remote(
            field.at[c, moved(blocks), :side_len, :],
            field.at[c, moved(blocks), tile_len:, :],
            sends,
            receives,
            3 + len(halves) + i,
            up,
        )
        for i, (c, blocks) in enumerate(halves)
    ]

    def narrow(blocks, at):
        for c in range(2):
            for b in blocks:
                field[c, b, at, :] = own[c, at, b * LANES : (b + 1) * LANES].astype(jnp.bfloat16)

    first.wait()
    narrow(range(side_blocks), slice(0, side_len))
    all_here((scan, tile))

    @pl.when(has_left)
    def _():
        for each in tops:
            each.start()

    second.wait()
    third.wait()
    narrow(range(side_blocks), slice(side_len, tile_len))
    narrow(range(side_blocks, own_blocks), slice(0, side_len))

    odd = lax.rem(lax.axis_index(axes[1][0]), 2) == 1
    first_turn = jnp.logical_and(has_left, jnp.logical_not(odd))
    second_turn = jnp.logical_and(has_left, odd)

    @pl.when(first_turn)
    def _():
        rest.start()

    @pl.when(has_up)
    def _():
        under.start()

    @pl.when(jnp.logical_not(has_right))
    def _():
        field[:, far, :tile_len, :] = jnp.zeros(
            (2, side_blocks, tile_len, LANES), jnp.bfloat16
        )

    @pl.when(jnp.logical_not(has_down))
    def _():
        field[:, :, tile_len:, :] = jnp.zeros(
            (2, own_blocks + side_blocks, side_len, LANES), jnp.bfloat16
        )

    fourth.wait()
    narrow(range(side_blocks, own_blocks), slice(side_len, tile_len))
    for load in constants:
        load.wait()

    def sort_slot(slot, carry):
        rows = dot(sort[...], measured[slot]).astype(jnp.bfloat16)
        both = dot(rows, unsort[...]).astype(jnp.bfloat16)
        for b in range(RADIX):
            arranged[slot, b] = both[:, b * part : (b + 1) * part]
        return carry

    lax.fori_loop(0, slots, sort_slot, 0)

    grown[...] = jnp.zeros_like(grown)
    for q in range(RADIX):
        for i in range(2):
            for at in (0, part):
                doubled[q, i, at : at + part, :] = cols_ref[
                    q, i * part : (i + 1) * part, :part
                ].astype(jnp.float32)

    lane = lax.broadcasted_iota(jnp.int32, (1, LANES), 1)
    line = lax.broadcasted_iota(jnp.int32, (part, LANES), 0)
    chunk = 32

    def prepare(slot, carry):
        lift = lax.rem(shift_ref[0, slot], GROUP)
        turn = lax.rem(shift_ref[1, slot], LANES)

        def move_probe(i, carry):
            at = pl.multiple_of(i * chunk, chunk)
            for c in range(2):
                turned = [
                    pltpu.roll(extended[c, b, pl.ds(GROUP - lift + at, chunk), :], turn, 1)
                    for b in range(side_blocks)
                ]
                for b in range(side_blocks):
                    probes[slot, c, b, pl.ds(at, chunk), :] = jnp.where(
                        lane >= turn, turned[b], turned[b - 1]
                    )
            return carry

        lax.fori_loop(0, side_len // chunk, move_probe, 0)
        for k, by in enumerate((lift, turn)):
            for q in range(RADIX):
                cos = pltpu.roll(rows_ref[q, :part, :part].astype(jnp.float32), by, 1)
                sin = pltpu.roll(rows_ref[q, :part, part:].astype(jnp.float32), by, 1)
                cos, sin = in_place(lane >= by, cos, sin, q)
                tables[slot, 0, k, q, 0, :part, :] = cos.astype(jnp.bfloat16)
                tables[slot, 0, k, q, 1, :part, :] = sin.astype(jnp.bfloat16)
                tables[slot, 0, k, q, 0, part:, :] = (-sin).astype(jnp.bfloat16)
                tables[slot, 0, k, q, 1, part:, :] = cos.astype(jnp.bfloat16)
                cos = doubled[q, 0, pl.ds(part - by, part), :]
                sin = doubled[q, 1, pl.ds(part - by, part), :]
                cos, sin = in_place(line >= by, cos, sin, q)
                tables[slot, 1, k, q, 0, :part, :] = cos.astype(jnp.bfloat16)
                tables[slot, 1, k, q, 1, :part, :] = (-sin).astype(jnp.bfloat16)
                tables[slot, 1, k, q, 0, part:, :] = sin.astype(jnp.bfloat16)
                tables[slot, 1, k, q, 1, part:, :] = cos.astype(jnp.bfloat16)
        return carry

    lax.fori_loop(0, slots, prepare, 0)

    for top, across in zip(tops, acrosses):

        @pl.when(has_right)
        def _(top=top):
            top.wait_recv()

        @pl.when(has_up)
        def _(across=across):
            across.start()

    @pl.when(first_turn)
    def _():
        for each in tops:
            each.wait_send()
        rest.wait_send()

    @pl.when(jnp.logical_and(first_turn, has_down))
    def _():
        pl.semaphore_signal(
            freed, inc=1, device_id=down, device_id_type=pl.DeviceIdType.MESH
        )

    @pl.when(second_turn)
    def _():
        pl.semaphore_wait(freed, 1)
        rest.start()

    @pl.when(has_down)
    def _():
        under.wait_recv()

    @pl.when(has_right)
    def _():
        rest.wait_recv()

    @pl.when(has_down)
    def _():
        for each in acrosses:
            each.wait_recv()

    @pl.when(second_turn)
    def _():
        for each in tops:
            each.wait_send()
        rest.wait_send()

    @pl.when(has_up)
    def _():
        under.wait_send()
        for each in acrosses:
            each.wait_send()


def gather(axes, shifts, own, measured, probe, tables):
    slots, side_len = measured.shape[:2]
    tile_len = own.shape[1]
    span = tile_len + side_len
    part = side_len // RADIX
    side_blocks = side_len // LANES
    hbm = pl.BlockSpec(memory_space=pltpu.HBM)
    vmem = pl.BlockSpec(memory_space=pltpu.VMEM)
    table = (slots, 2, 2, RADIX, 2, 2 * part, part)
    scratch = [
        (own.shape, jnp.float32),
        (measured.shape, jnp.bfloat16),
        ((2, side_blocks, side_len + GROUP, LANES), jnp.float32),
        (tables[0].shape, jnp.bfloat16),
        (tables[1].shape, jnp.bfloat16),
        ((RADIX, 2, 2 * part, part), jnp.float32),
        ((side_len, side_len), jnp.bfloat16),
        ((side_len, side_len), jnp.bfloat16),
    ]
    call = pl.pallas_call(
        functools.partial(gather_kernel, axes),
        out_shape=[
            pltpu.VMEM((2, span // LANES, span, LANES), jnp.bfloat16),
            pltpu.VMEM((slots, 2, side_blocks, side_len, LANES), jnp.float32),
            pltpu.VMEM(table, jnp.bfloat16),
            pltpu.VMEM((slots, RADIX, side_len, part), jnp.bfloat16),
            pltpu.VMEM((2, span // LANES, span, LANES), jnp.float32),
        ],
        in_specs=[pl.BlockSpec(memory_space=pltpu.SMEM)] + [hbm] * 7,
        out_specs=[vmem] * 5,
        scratch_shapes=[pltpu.VMEM(*each) for each in scratch]
        + [
            pltpu.SemaphoreType.DMA((3 + 8,)),
            pltpu.SemaphoreType.DMA((3 + 8,)),
            pltpu.SemaphoreType.DMA((9 + 4 * side_blocks,)),
            pltpu.SemaphoreType.REGULAR,
        ],
        compiler_params=pltpu.CompilerParams(
            collective_id=0, has_side_effects=True, vmem_limit_bytes=room(scratch)
        ),
    )
    prepared = call(shifts, own, measured, probe, *tables, *sorted_by_residue(side_len))
    held = [pltpu.with_memory_space_constraint(each, pltpu.VMEM) for each in prepared]
    return held, room(scratch)


def room(scratch):
    return sum(math.prod(shape) * jnp.dtype(kind).itemsize for shape, kind in scratch) + (1 << 20)


def scatter_kernel(
    axes,
    grown,
    total,
    spill,
    dropped,
    both,
    landed,
    from_left,
    from_up,
    sends,
    receives,
):
    side_len = landed.shape[2]
    tile_len = total.shape[1]
    own_blocks = tile_len // LANES
    side_blocks = side_len // LANES
    scan, tile = neighbours(axes)
    has_left, _, has_right, right = scan
    has_up, _, has_down, down = tile
    corner = remote(both, landed, sends, receives, 0, down)
    under = remote(dropped, from_up, sends, receives, 1, down)
    rest = remote(
        spill.at[:, :, side_len:, :], from_left.at[:, :, side_len:, :], sends, receives, 2, right
    )
    top = remote(
        spill.at[:, :, :side_len, :], from_left.at[:, :, :side_len, :], sends, receives, 3, right
    )
    greet((scan, tile))
    spill[:, :, side_len:, :] = grown[:, own_blocks:, side_len:tile_len, :].astype(jnp.bfloat16)
    both[...] = grown[:, own_blocks:, tile_len:, :].astype(jnp.bfloat16)
    all_here((scan, tile))

    @pl.when(has_right)
    def _():
        rest.start()

    @pl.when(has_down)
    def _():
        corner.start()

    dropped[...] = grown[:, :own_blocks, tile_len:, :].astype(jnp.bfloat16)

    @pl.when(has_down)
    def _():
        under.start()

    @pl.when(jnp.logical_not(has_up))
    def _():
        landed[...] = jnp.zeros_like(landed)

    for c in range(2):
        for b in range(own_blocks):
            total[c, :, b * LANES : (b + 1) * LANES] = grown[c, b, :tile_len, :]

    @pl.when(has_up)
    def _():
        corner.wait_recv()

    spill[:, :, :side_len, :] = (
        grown[:, own_blocks:, :side_len, :] + landed[...].astype(jnp.float32)
    ).astype(jnp.bfloat16)

    @pl.when(has_right)
    def _():
        top.start()

    def add(blocks, at, source):
        for c in range(2):
            for b in blocks:
                total[c, at, b * LANES : (b + 1) * LANES] += source[c, b, at, :].astype(jnp.float32)

    @pl.when(has_left)
    def _():
        rest.wait_recv()
        add(range(side_blocks), slice(side_len, tile_len), from_left)

    @pl.when(has_up)
    def _():
        under.wait_recv()
        add(range(own_blocks), slice(0, side_len), from_up)

    @pl.when(has_left)
    def _():
        top.wait_recv()
        add(range(side_blocks), slice(0, side_len), from_left)

    @pl.when(has_right)
    def _():
        rest.wait_send()
        top.wait_send()

    @pl.when(has_down)
    def _():
        corner.wait_send()
        under.wait_send()


def scatter(axes, grown, tile_len):
    span = grown.shape[2]
    side_len = span - tile_len
    own_blocks = tile_len // LANES
    side_blocks = side_len // LANES
    vmem = pl.BlockSpec(memory_space=pltpu.VMEM)
    scratch = [
        ((2, side_blocks, tile_len, LANES), jnp.bfloat16),
        ((2, own_blocks, side_len, LANES), jnp.bfloat16),
        ((2, side_blocks, side_len, LANES), jnp.bfloat16),
        ((2, side_blocks, side_len, LANES), jnp.bfloat16),
        ((2, side_blocks, tile_len, LANES), jnp.bfloat16),
        ((2, own_blocks, side_len, LANES), jnp.bfloat16),
    ]
    return pl.pallas_call(
        functools.partial(scatter_kernel, axes),
        out_shape=pltpu.VMEM((2, tile_len, tile_len), jnp.float32),
        in_specs=[vmem],
        out_specs=vmem,
        scratch_shapes=[pltpu.VMEM(*each) for each in scratch]
        + [pltpu.SemaphoreType.DMA((4,)), pltpu.SemaphoreType.DMA((4,))],
        compiler_params=pltpu.CompilerParams(
            collective_id=1, has_side_effects=True, vmem_limit_bytes=room(scratch)
        ),
    )(grown)


def side_by_side(*blocks):
    return jnp.concatenate(blocks, axis=1)


def solve_kernel(
    live_ref,
    shift_ref,
    field,
    probes,
    tables,
    measured,
    zeros,
    grown,
    mixed,
    halves,
    misfits,
    spectra,
    backs,
):
    side_len = probes.shape[3]
    part = side_len // RADIX
    side_blocks = side_len // LANES
    lane = lax.broadcasted_iota(jnp.int32, (1, LANES), 1)
    line = lax.broadcasted_iota(jnp.int32, (GROUP, LANES), 0)

    def one_slot(slot, carry):
        row = shift_ref[0, slot]
        col = shift_ref[1, slot]
        lift = lax.rem(row, GROUP)
        turn = lax.rem(col, LANES)
        base = pl.multiple_of(row - lift, GROUP)
        block = lax.div(col, LANES)
        stay = lane >= turn
        below = line >= lift

        def table(side, kind, q):
            return side_by_side(tables[slot, side, kind, q, 0], tables[slot, side, kind, q, 1])

        def piece(c, b, at):
            def cut(b):
                start = pl.multiple_of(base + at, GROUP)
                value = field[c, block + b, pl.ds(start, GROUP), :].astype(jnp.float32)
                if at == 0:
                    start = pl.multiple_of(base + side_len, GROUP)
                    wrapped = field[c, block + b, pl.ds(start, GROUP), :].astype(jnp.float32)
                    value = jnp.where(below, value, wrapped)
                return value

            return cut(b) if b else jnp.where(stay, cut(0), cut(side_blocks))

        def exit_waves(blocks):
            for at in range(0, part, GROUP):
                for b in blocks:
                    waves = []
                    for p in range(RADIX):
                        here = at + p * part
                        re, im = piece(0, b, here), piece(1, b, here)
                        probe_re = probes[slot, 0, b, here : here + GROUP, :]
                        probe_im = probes[slot, 1, b, here : here + GROUP, :]
                        waves.append((probe_re * re - probe_im * im, probe_re * im + probe_im * re))
                    for q, (re, im) in enumerate(butterfly(waves, -1)):
                        mixed[q, b, at : at + GROUP, :] = re.astype(jnp.bfloat16)
                        mixed[q, b, at + part : at + part + GROUP, :] = im.astype(jnp.bfloat16)

        def split(value):
            return [
                (value[:part, at : at + part], value[part:, at : at + part])
                for at in range(0, value.shape[1], part)
            ]

        def left(q, blocks):
            return split(dot(table(0, 0, q), side_by_side(*(mixed[q, b] for b in blocks))))

        def far_field(other):
            return dot(side_by_side(halves[other, 0], halves[other, 1]), table(1, 1, other))

        def misfit_of(other, far):
            for q in range(RADIX):
                rows = slice(q * part, (q + 1) * part)
                far_re, far_im = far[rows, :part], far[rows, part:]
                seen = measured[slot, other, rows, :].astype(jnp.float32)
                misfit = far_re * far_re + far_im * far_im - seen
                misfits[q, other, :part, :] = (misfit * far_re).astype(jnp.bfloat16)
                misfits[q, other, part:, :] = (misfit * far_im).astype(jnp.bfloat16)

        def left_back(q, pair):
            mixture = dot(table(1, 0, q), side_by_side(*(misfits[q, other] for other in pair)))
            for i, other in enumerate(pair):
                spectra[q, other] = mixture[:, i * part : (i + 1) * part]

        def mix(ats, pair):
            for at in ats:
                for other in pair:
                    parts = [
                        (
                            spectra[q, other, at : at + GROUP, :],
                            spectra[q, other, part + at : part + at + GROUP, :],
                        )
                        for q in range(RADIX)
                    ]
                    for p, (re, im) in enumerate(butterfly(parts, 1)):
                        here = slice(at + p * part, at + p * part + GROUP)
                        backs[other, 0, here, :] = re.astype(jnp.bfloat16)
                        backs[other, 1, here, :] = im.astype(jnp.bfloat16)

        def add(c, b, at, value):
            where = pl.ds(pl.multiple_of(base + at, GROUP), value.shape[0])
            grown[c, block + b, where, :] += value

        def add_wrapped(c, b, at, value):
            if at == 0:
                add(c, b, 0, jnp.where(below, value[:GROUP], 0.0))
                add(c, b, side_len, jnp.where(below, 0.0, value[:GROUP]))
                add(c, b, GROUP, value[GROUP:])
            else:
                add(c, b, at, value)

        def right_back(at, tall):
            parts = []
            for other in range(RADIX):
                back = jnp.concatenate(
                    [
                        side_by_side(
                            backs[other, 0, here : here + tall, :],
                            backs[other, 1, here : here + tall, :],
                        )
                        for here in range(at, side_len, part)
                    ],
                    axis=0,
                )
                grad = dot(back, table(0, 1, other))
                parts.append((grad[:, :part], grad[:, part:]))
            return parts

        def accumulate(at, tall, parts):
            for p in range(RADIX):
                here = at + p * part
                rows = slice(p * tall, (p + 1) * tall)
                some = [(re[rows], im[rows]) for re, im in parts]
                for b, (re, im) in enumerate(butterfly(some, 1)):
                    probe_re = probes[slot, 0, b, here : here + tall, :]
                    probe_im = probes[slot, 1, b, here : here + tall, :]
                    values = (probe_re * re + probe_im * im, probe_re * im - probe_im * re)
                    for c, value in enumerate(values):
                        if b == 0:
                            add_wrapped(c, 0, here, jnp.where(stay, value, 0.0))
                            add_wrapped(c, side_blocks, here, jnp.where(stay, 0.0, value))
                        else:
                            add_wrapped(c, b, here, value)

        exit_waves((0, 2))
        early = [left(q, (0, 2)) for q in range(RADIX)]
        exit_waves((1, 3))
        for q in range(RADIX):
            rows = slice(q * part, (q + 1) * part)
            (r0, r2), (r1, r3) = early[q], left(q, (1, 3))
            for other, (re, im) in enumerate(butterfly([r0, r1, r2, r3], -1)):
                halves[other, 0, rows, :] = re.astype(jnp.bfloat16)
                halves[other, 1, rows, :] = im.astype(jnp.bfloat16)
        ahead = far_field(0)
        for other in range(RADIX):
            far = ahead
            if other + 1 < RADIX:
                ahead = far_field(other + 1)
            misfit_of(other, far)
            if other == 2:
                for q in range(RADIX):
                    left_back(q, (0, 1))
        tall = part // 2
        ats = [range(at, at + tall, GROUP) for at in range(0, part, tall)]
        for q in range(RADIX):
            left_back(q, (2, 3))
        mix(ats[0], (0, 1))
        mix(ats[0], (2, 3))
        first = right_back(0, tall)
        mix(ats[1], (0, 1))
        mix(ats[1], (2, 3))
        second = right_back(tall, tall)
        accumulate(0, tall, first)
        accumulate(tall, tall, second)
        return carry

    lax.fori_loop(0, live_ref[0, lax.axis_index("scan")], one_slot, 0)


def solve(live_counts, shifts, prepared, limit):
    grown = prepared[-1]
    side_len = prepared[1].shape[3]
    part = side_len // RADIX
    smem = pl.BlockSpec(memory_space=pltpu.SMEM)
    vmem = pl.BlockSpec(memory_space=pltpu.VMEM)
    wide = (RADIX, RADIX, 2 * part, part)
    tall = (RADIX, 2, side_len, part)
    scratch = [
        (wide, jnp.bfloat16),
        (tall, jnp.bfloat16),
        (wide, jnp.bfloat16),
        (wide, jnp.float32),
        (tall, jnp.bfloat16),
    ]
    return pl.pallas_call(
        solve_kernel,
        out_shape=pltpu.VMEM(grown.shape, grown.dtype),
        in_specs=[smem, smem] + [vmem] * len(prepared),
        out_specs=vmem,
        scratch_shapes=[pltpu.VMEM(*each) for each in scratch],
        input_output_aliases={1 + len(prepared): 0},
        compiler_params=pltpu.CompilerParams(vmem_limit_bytes=limit),
    )(live_counts, shifts, *prepared)


def shards(axes, object_slab, probe_field, intensities, offsets, live_count):
    tables = residue_tables(probe_field.shape[-1])
    shifts = offsets[0, 0].T
    prepared, limit = gather(axes, shifts, object_slab, intensities[0, 0], probe_field, tables)
    grown = solve(live_count.T, shifts, prepared, limit)
    return scatter(axes, grown, object_slab.shape[1])


def solution(mesh):
    placed = (
        P(None, "tile", "scan"),
        P(),
        P("scan", "tile", None, None, None),
        P("scan", "tile", None, None),
        P(None, "tile"),
    )
    axes = tuple((name, mesh.shape[name]) for name in ("scan", "tile"))
    return jax.shard_map(
        functools.partial(shards, axes), mesh=mesh, in_specs=placed, out_specs=P(None, "tile", "scan"), check_vma=False
    )
```

```python
import functools
import math

import jax
import jax.numpy as jnp
import numpy as np
from jax import lax
from jax.experimental import pallas as pl
from jax.experimental.pallas import tpu as pltpu
from jax.sharding import PartitionSpec as P

RADIX = 4
LANES = 128
GROUP = 16


def residue_tables(side_len):
    part = side_len // RADIX
    freq = np.arange(side_len).reshape(part, RADIX).T
    across = np.arange(part)
    phase = (freq[:, :, None] * across[None, None, :] % side_len) * (2.0 * math.pi / side_len)
    factor = 1.0 / math.sqrt(side_len)
    cos = np.cos(phase) * factor
    sin = np.sin(phase) * factor
    rows = np.concatenate(
        [np.concatenate([cos, sin], axis=2), np.concatenate([-sin, cos], axis=2)], axis=1
    ).astype(np.float32)
    return jnp.asarray(rows, jnp.bfloat16), jnp.asarray(rows.swapaxes(1, 2), jnp.bfloat16)


def sorted_by_residue(side_len):
    at = np.arange(side_len)
    source = at % (side_len // RADIX) * RADIX + at // (side_len // RADIX)
    sort = (source[:, None] == at[None, :]).astype(np.float32)
    return jnp.asarray(sort, jnp.bfloat16), jnp.asarray(sort.T, jnp.bfloat16)


def dot(a, b):
    return jnp.dot(a, b, preferred_element_type=jnp.float32)


def butterfly(parts, sign):
    (r0, i0), (r1, i1), (r2, i2), (r3, i3) = parts
    ar, ai, br, bi = r0 + r2, i0 + i2, r1 + r3, i1 + i3
    cr, ci, dr, di = r0 - r2, i0 - i2, r1 - r3, i1 - i3
    plus = (cr - di, ci + dr)
    minus = (cr + di, ci - dr)
    first, third = (plus, minus) if sign > 0 else (minus, plus)
    return [(ar + br, ai + bi), first, (ar - br, ai - bi), third]


def neighbours(axes):
    result = []
    for name, count in axes:
        me = lax.axis_index(name)
        result.append((me > 0, {name: me - 1}, me < count - 1, {name: me + 1}))
    return result


def greet(peers):
    barrier = pltpu.get_barrier_semaphore()
    for has_low, low, has_high, high in peers:
        for there, peer in ((has_low, low), (has_high, high)):

            @pl.when(there)
            def _(peer=peer):
                pl.semaphore_signal(
                    barrier, inc=1, device_id=peer, device_id_type=pl.DeviceIdType.MESH
                )


def all_here(peers):
    count = sum(
        there.astype(jnp.int32) for has_low, _, has_high, _ in peers for there in (has_low, has_high)
    )
    pl.semaphore_wait(pltpu.get_barrier_semaphore(), count)


def remote(source, target, sends, receives, index, peer):
    return pltpu.make_async_remote_copy(
        src_ref=source,
        dst_ref=target,
        send_sem=sends.at[index],
        recv_sem=receives.at[index],
        device_id=peer,
        device_id_type=pl.DeviceIdType.MESH,
    )


def quarter_turns(cos, sin, q):
    return ((cos, sin), (sin, -cos), (-cos, -sin), (-sin, cos))[q]


def in_place(mask, cos, sin, q):
    wrapped = quarter_turns(cos, sin, q)
    return jnp.where(mask, cos, wrapped[0]), jnp.where(mask, sin, wrapped[1])


def gather_kernel(
    axes,
    shift_ref,
    own_hbm,
    measured_hbm,
    probe_hbm,
    rows_hbm,
    cols_hbm,
    sort_hbm,
    unsort_hbm,
    field,
    probes,
    tables,
    arranged,
    grown,
    own,
    measured,
    extended,
    rows_ref,
    cols_ref,
    doubled,
    sort,
    unsort,
    sends,
    receives,
    fetches,
    freed,
):
    slots, side_len = measured.shape[:2]
    tile_len = own.shape[1]
    part = side_len // RADIX
    own_blocks = tile_len // LANES
    side_blocks = side_len // LANES
    scan, tile = neighbours(axes)
    has_left, left, has_right, _ = scan
    has_up, up, has_down, down = tile
    greet((scan, tile))
    first = pltpu.make_async_copy(
        own_hbm.at[:, :side_len, :side_len], own.at[:, :side_len, :side_len], fetches.at[0]
    )
    second = pltpu.make_async_copy(
        own_hbm.at[:, side_len:, :side_len], own.at[:, side_len:, :side_len], fetches.at[1]
    )
    third = pltpu.make_async_copy(
        own_hbm.at[:, :side_len, side_len:], own.at[:, :side_len, side_len:], fetches.at[2]
    )
    fourth = pltpu.make_async_copy(
        own_hbm.at[:, side_len:, side_len:], own.at[:, side_len:, side_len:], fetches.at[3]
    )
    constants = [
        pltpu.make_async_copy(source, target, fetches.at[4 + i])
        for i, (source, target) in enumerate(
            (
                (sort_hbm, sort),
                (unsort_hbm, unsort),
                (measured_hbm, measured),
                (rows_hbm, rows_ref),
                (cols_hbm, cols_ref),
            )
        )
    ]
    for c in range(2):
        for b in range(side_blocks):
            cols = slice(b * LANES, (b + 1) * LANES)
            for source, target in (
                (probe_hbm.at[c, :, cols], extended.at[c, b, GROUP:, :]),
                (probe_hbm.at[c, side_len - GROUP :, cols], extended.at[c, b, :GROUP, :]),
            ):
                constants.append(
                    pltpu.make_async_copy(source, target, fetches.at[4 + len(constants)])
                )
    for load in [first, second, third, fourth] + constants:
        load.start()
    near = slice(0, side_blocks)
    far = slice(own_blocks, own_blocks + side_blocks)
    halves = [
        (c, slice(at, at + side_blocks // 2))
        for c in range(2)
        for at in range(0, side_blocks, side_blocks // 2)
    ]

    def moved(blocks):
        return slice(blocks.start + own_blocks, blocks.stop + own_blocks)

    tops = [
        remote(
            field.at[c, blocks, :side_len, :],
            field.at[c, moved(blocks), :side_len, :],
            sends,
            receives,
            3 + i,
            left,
        )
        for i, (c, blocks) in enumerate(halves)
    ]
    rests = [
        remote(
            field.at[c, near, side_len:tile_len, :],
            field.at[c, far, side_len:tile_len, :],
            sends,
            receives,
            c,
            left,
        )
        for c in range(2)
    ]
    under = remote(
        field.at[:, :own_blocks, :side_len, :],
        field.at[:, :own_blocks, tile_len:, :],
        sends,
        receives,
        2,
        up,
    )
    acrosses = [
        remote(
            field.at[c, moved(blocks), :side_len, :],
            field.at[c, moved(blocks), tile_len:, :],
            sends,
            receives,
            3 + len(halves) + i,
            up,
        )
        for i, (c, blocks) in enumerate(halves)
    ]

    def narrow(blocks, at):
        for c in range(2):
            for b in blocks:
                field[c, b, at, :] = own[c, at, b * LANES : (b + 1) * LANES].astype(jnp.bfloat16)

    first.wait()
    narrow(range(side_blocks), slice(0, side_len))
    all_here((scan, tile))

    @pl.when(has_left)
    def _():
        for each in tops:
            each.start()

    second.wait()
    third.wait()
    narrow(range(side_blocks), slice(side_len, tile_len))
    narrow(range(side_blocks, own_blocks), slice(0, side_len))

    odd = lax.rem(lax.axis_index(axes[1][0]), 2) == 1
    first_turn = jnp.logical_and(has_left, jnp.logical_not(odd))
    second_turn = jnp.logical_and(has_left, odd)

    @pl.when(first_turn)
    def _():
        for each in rests:
            each.start()

    @pl.when(has_up)
    def _():
        under.start()

    @pl.when(jnp.logical_not(has_right))
    def _():
        field[:, far, :tile_len, :] = jnp.zeros(
            (2, side_blocks, tile_len, LANES), jnp.bfloat16
        )

    @pl.when(jnp.logical_not(has_down))
    def _():
        field[:, :, tile_len:, :] = jnp.zeros(
            (2, own_blocks + side_blocks, side_len, LANES), jnp.bfloat16
        )

    fourth.wait()
    narrow(range(side_blocks, own_blocks), slice(side_len, tile_len))
    for load in constants:
        load.wait()

    def sort_slot(slot, carry):
        rows = dot(sort[...], measured[slot]).astype(jnp.bfloat16)
        both = dot(rows, unsort[...]).astype(jnp.bfloat16)
        for b in range(RADIX):
            arranged[slot, b] = both[:, b * part : (b + 1) * part]
        return carry

    lax.fori_loop(0, slots, sort_slot, 0)

    grown[...] = jnp.zeros_like(grown)
    for q in range(RADIX):
        for i in range(2):
            for at in (0, part):
                doubled[q, i, at : at + part, :] = cols_ref[
                    q, i * part : (i + 1) * part, :part
                ].astype(jnp.float32)

    lane = lax.broadcasted_iota(jnp.int32, (1, LANES), 1)
    line = lax.broadcasted_iota(jnp.int32, (part, LANES), 0)
    chunk = 32

    def prepare(slot, carry):
        lift = lax.rem(shift_ref[0, slot], GROUP)
        turn = lax.rem(shift_ref[1, slot], LANES)

        def move_probe(i, carry):
            at = pl.multiple_of(i * chunk, chunk)
            for c in range(2):
                turned = [
                    pltpu.roll(extended[c, b, pl.ds(GROUP - lift + at, chunk), :], turn, 1)
                    for b in range(side_blocks)
                ]
                for b in range(side_blocks):
                    probes[slot, c, b, pl.ds(at, chunk), :] = jnp.where(
                        lane >= turn, turned[b], turned[b - 1]
                    )
            return carry

        lax.fori_loop(0, side_len // chunk, move_probe, 0)
        for k, by in enumerate((lift, turn)):
            for q in range(RADIX):
                cos = pltpu.roll(rows_ref[q, :part, :part].astype(jnp.float32), by, 1)
                sin = pltpu.roll(rows_ref[q, :part, part:].astype(jnp.float32), by, 1)
                cos, sin = in_place(lane >= by, cos, sin, q)
                tables[slot, 0, k, q, 0, :part, :] = cos.astype(jnp.bfloat16)
                tables[slot, 0, k, q, 1, :part, :] = sin.astype(jnp.bfloat16)
                tables[slot, 0, k, q, 0, part:, :] = (-sin).astype(jnp.bfloat16)
                tables[slot, 0, k, q, 1, part:, :] = cos.astype(jnp.bfloat16)
                cos = doubled[q, 0, pl.ds(part - by, part), :]
                sin = doubled[q, 1, pl.ds(part - by, part), :]
                cos, sin = in_place(line >= by, cos, sin, q)
                tables[slot, 1, k, q, 0, :part, :] = cos.astype(jnp.bfloat16)
                tables[slot, 1, k, q, 1, :part, :] = (-sin).astype(jnp.bfloat16)
                tables[slot, 1, k, q, 0, part:, :] = sin.astype(jnp.bfloat16)
                tables[slot, 1, k, q, 1, part:, :] = cos.astype(jnp.bfloat16)
        return carry

    lax.fori_loop(0, slots, prepare, 0)

    for top, across in zip(tops, acrosses):

        @pl.when(has_right)
        def _(top=top):
            top.wait_recv()

        @pl.when(has_up)
        def _(across=across):
            across.start()

    @pl.when(first_turn)
    def _():
        for each in tops + rests[:1]:
            each.wait_send()

    @pl.when(jnp.logical_and(first_turn, has_down))
    def _():
        pl.semaphore_signal(
            freed, inc=1, device_id=down, device_id_type=pl.DeviceIdType.MESH
        )

    @pl.when(second_turn)
    def _():
        pl.semaphore_wait(freed, 1)
        for each in rests:
            each.start()

    @pl.when(first_turn)
    def _():
        rests[1].wait_send()

    @pl.when(has_down)
    def _():
        under.wait_recv()

    @pl.when(has_right)
    def _():
        for each in rests:
            each.wait_recv()

    @pl.when(has_down)
    def _():
        for each in acrosses:
            each.wait_recv()

    @pl.when(second_turn)
    def _():
        for each in tops + rests:
            each.wait_send()

    @pl.when(has_up)
    def _():
        under.wait_send()
        for each in acrosses:
            each.wait_send()


def gather(axes, shifts, own, measured, probe, tables):
    slots, side_len = measured.shape[:2]
    tile_len = own.shape[1]
    span = tile_len + side_len
    part = side_len // RADIX
    side_blocks = side_len // LANES
    hbm = pl.BlockSpec(memory_space=pltpu.HBM)
    vmem = pl.BlockSpec(memory_space=pltpu.VMEM)
    table = (slots, 2, 2, RADIX, 2, 2 * part, part)
    scratch = [
        (own.shape, jnp.float32),
        (measured.shape, jnp.bfloat16),
        ((2, side_blocks, side_len + GROUP, LANES), jnp.float32),
        (tables[0].shape, jnp.bfloat16),
        (tables[1].shape, jnp.bfloat16),
        ((RADIX, 2, 2 * part, part), jnp.float32),
        ((side_len, side_len), jnp.bfloat16),
        ((side_len, side_len), jnp.bfloat16),
    ]
    call = pl.pallas_call(
        functools.partial(gather_kernel, axes),
        out_shape=[
            pltpu.VMEM((2, span // LANES, span, LANES), jnp.bfloat16),
            pltpu.VMEM((slots, 2, side_blocks, side_len, LANES), jnp.float32),
            pltpu.VMEM(table, jnp.bfloat16),
            pltpu.VMEM((slots, RADIX, side_len, part), jnp.bfloat16),
            pltpu.VMEM((2, span // LANES, span, LANES), jnp.float32),
        ],
        in_specs=[pl.BlockSpec(memory_space=pltpu.SMEM)] + [hbm] * 7,
        out_specs=[vmem] * 5,
        scratch_shapes=[pltpu.VMEM(*each) for each in scratch]
        + [
            pltpu.SemaphoreType.DMA((3 + 8,)),
            pltpu.SemaphoreType.DMA((3 + 8,)),
            pltpu.SemaphoreType.DMA((9 + 4 * side_blocks,)),
            pltpu.SemaphoreType.REGULAR,
        ],
        compiler_params=pltpu.CompilerParams(
            collective_id=0, has_side_effects=True, vmem_limit_bytes=room(scratch)
        ),
    )
    prepared = call(shifts, own, measured, probe, *tables, *sorted_by_residue(side_len))
    held = [pltpu.with_memory_space_constraint(each, pltpu.VMEM) for each in prepared]
    return held, room(scratch)


def room(scratch):
    return sum(math.prod(shape) * jnp.dtype(kind).itemsize for shape, kind in scratch) + (1 << 20)


def scatter_kernel(
    axes,
    grown,
    total,
    spill,
    dropped,
    both,
    landed,
    from_left,
    from_up,
    sends,
    receives,
    ready,
):
    side_len = landed.shape[2]
    tile_len = total.shape[1]
    own_blocks = tile_len // LANES
    side_blocks = side_len // LANES
    scan, tile = neighbours(axes)
    has_left, left, has_right, right = scan
    has_up, up, has_down, down = tile
    odd = lax.rem(lax.axis_index(axes[1][0]), 2) == 1
    even = jnp.logical_not(odd)
    barrier = pltpu.get_barrier_semaphore()

    def tell(there, sem, peer):
        @pl.when(there)
        def _():
            pl.semaphore_signal(
                sem, inc=1, device_id=peer, device_id_type=pl.DeviceIdType.MESH
            )

    tell(has_left, barrier, left)
    tell(jnp.logical_and(even, has_up), barrier, up)
    tell(jnp.logical_and(even, has_down), barrier, down)
    corner = remote(both, landed, sends, receives, 0, down)
    under = remote(dropped, from_up, sends, receives, 1, down)
    rest = remote(
        spill.at[:, :, side_len:, :], from_left.at[:, :, side_len:, :], sends, receives, 2, right
    )
    top = remote(
        spill.at[:, :, :side_len, :], from_left.at[:, :, :side_len, :], sends, receives, 3, right
    )
    spill[:, :, side_len:, :] = grown[:, own_blocks:, side_len:tile_len, :].astype(jnp.bfloat16)
    both[...] = grown[:, own_blocks:, tile_len:, :].astype(jnp.bfloat16)
    from_even = has_up.astype(jnp.int32) + has_down.astype(jnp.int32)
    awaited = has_right.astype(jnp.int32) + jnp.where(odd, from_even, 0)

    @pl.when(awaited > 0)
    def _():
        pl.semaphore_wait(barrier, awaited)

    @pl.when(has_right)
    def _():
        rest.start()

    tell(odd, ready, up)

    @pl.when(jnp.logical_and(odd, has_down))
    def _():
        corner.start()

    @pl.when(jnp.logical_not(has_up))
    def _():
        spill[:, :, :side_len, :] = grown[:, own_blocks:, :side_len, :].astype(jnp.bfloat16)

    @pl.when(jnp.logical_and(jnp.logical_not(has_up), has_right))
    def _():
        top.start()

    dropped[...] = grown[:, :own_blocks, tile_len:, :].astype(jnp.bfloat16)

    @pl.when(jnp.logical_and(odd, has_down))
    def _():
        under.start()

    for c in range(2):
        for b in range(own_blocks):
            total[c, :, b * LANES : (b + 1) * LANES] = grown[c, b, :tile_len, :]

    @pl.when(jnp.logical_and(even, has_down))
    def _():
        pl.semaphore_wait(ready, 1)
        corner.start()
        under.start()

    @pl.when(has_up)
    def _():
        corner.wait_recv()
        spill[:, :, :side_len, :] = (
            grown[:, own_blocks:, :side_len, :] + landed[...].astype(jnp.float32)
        ).astype(jnp.bfloat16)

    @pl.when(jnp.logical_and(has_up, has_right))
    def _():
        top.start()

    def add(blocks, at, source):
        for c in range(2):
            for b in blocks:
                total[c, at, b * LANES : (b + 1) * LANES] += source[c, b, at, :].astype(jnp.float32)

    @pl.when(has_left)
    def _():
        rest.wait_recv()
        add(range(side_blocks), slice(side_len, tile_len), from_left)

    @pl.when(has_up)
    def _():
        under.wait_recv()
        add(range(own_blocks), slice(0, side_len), from_up)

    @pl.when(has_left)
    def _():
        top.wait_recv()
        add(range(side_blocks), slice(0, side_len), from_left)

    @pl.when(has_right)
    def _():
        rest.wait_send()
        top.wait_send()

    @pl.when(has_down)
    def _():
        corner.wait_send()
        under.wait_send()


def scatter(axes, grown, tile_len):
    span = grown.shape[2]
    side_len = span - tile_len
    own_blocks = tile_len // LANES
    side_blocks = side_len // LANES
    vmem = pl.BlockSpec(memory_space=pltpu.VMEM)
    scratch = [
        ((2, side_blocks, tile_len, LANES), jnp.bfloat16),
        ((2, own_blocks, side_len, LANES), jnp.bfloat16),
        ((2, side_blocks, side_len, LANES), jnp.bfloat16),
        ((2, side_blocks, side_len, LANES), jnp.bfloat16),
        ((2, side_blocks, tile_len, LANES), jnp.bfloat16),
        ((2, own_blocks, side_len, LANES), jnp.bfloat16),
    ]
    return pl.pallas_call(
        functools.partial(scatter_kernel, axes),
        out_shape=pltpu.VMEM((2, tile_len, tile_len), jnp.float32),
        in_specs=[vmem],
        out_specs=vmem,
        scratch_shapes=[pltpu.VMEM(*each) for each in scratch]
        + [
            pltpu.SemaphoreType.DMA((4,)),
            pltpu.SemaphoreType.DMA((4,)),
            pltpu.SemaphoreType.REGULAR,
        ],
        compiler_params=pltpu.CompilerParams(
            collective_id=1, has_side_effects=True, vmem_limit_bytes=room(scratch)
        ),
    )(grown)


def side_by_side(*blocks):
    return jnp.concatenate(blocks, axis=1)


def solve_kernel(
    live_ref,
    shift_ref,
    field,
    probes,
    tables,
    measured,
    zeros,
    grown,
    mixed,
    halves,
    misfits,
    spectra,
    backs,
):
    side_len = probes.shape[3]
    part = side_len // RADIX
    side_blocks = side_len // LANES
    lane = lax.broadcasted_iota(jnp.int32, (1, LANES), 1)
    line = lax.broadcasted_iota(jnp.int32, (GROUP, LANES), 0)

    def one_slot(slot, carry):
        row = shift_ref[0, slot]
        col = shift_ref[1, slot]
        lift = lax.rem(row, GROUP)
        turn = lax.rem(col, LANES)
        base = pl.multiple_of(row - lift, GROUP)
        block = lax.div(col, LANES)
        stay = lane >= turn
        below = line >= lift

        def table(side, kind, q):
            return side_by_side(tables[slot, side, kind, q, 0], tables[slot, side, kind, q, 1])

        def piece(c, b, at):
            def cut(b):
                start = pl.multiple_of(base + at, GROUP)
                value = field[c, block + b, pl.ds(start, GROUP), :].astype(jnp.float32)
                if at == 0:
                    start = pl.multiple_of(base + side_len, GROUP)
                    wrapped = field[c, block + b, pl.ds(start, GROUP), :].astype(jnp.float32)
                    value = jnp.where(below, value, wrapped)
                return value

            return cut(b) if b else jnp.where(stay, cut(0), cut(side_blocks))

        def exit_waves(blocks):
            for at in range(0, part, GROUP):
                for b in blocks:
                    waves = []
                    for p in range(RADIX):
                        here = at + p * part
                        re, im = piece(0, b, here), piece(1, b, here)
                        probe_re = probes[slot, 0, b, here : here + GROUP, :]
                        probe_im = probes[slot, 1, b, here : here + GROUP, :]
                        waves.append((probe_re * re - probe_im * im, probe_re * im + probe_im * re))
                    for q, (re, im) in enumerate(butterfly(waves, -1)):
                        mixed[q, b, at : at + GROUP, :] = re.astype(jnp.bfloat16)
                        mixed[q, b, at + part : at + part + GROUP, :] = im.astype(jnp.bfloat16)

        def split(value):
            return [
                (value[:part, at : at + part], value[part:, at : at + part])
                for at in range(0, value.shape[1], part)
            ]

        def left(q, blocks):
            return split(dot(table(0, 0, q), side_by_side(*(mixed[q, b] for b in blocks))))

        def far_field(other):
            return dot(side_by_side(halves[other, 0], halves[other, 1]), table(1, 1, other))

        def misfit_of(other, far):
            for q in range(RADIX):
                rows = slice(q * part, (q + 1) * part)
                far_re, far_im = far[rows, :part], far[rows, part:]
                seen = measured[slot, other, rows, :].astype(jnp.float32)
                misfit = far_re * far_re + far_im * far_im - seen
                misfits[q, other, :part, :] = (misfit * far_re).astype(jnp.bfloat16)
                misfits[q, other, part:, :] = (misfit * far_im).astype(jnp.bfloat16)

        def left_back(q, pair):
            mixture = dot(table(1, 0, q), side_by_side(*(misfits[q, other] for other in pair)))
            for i, other in enumerate(pair):
                spectra[q, other] = mixture[:, i * part : (i + 1) * part]

        def mix(ats, pair):
            for at in ats:
                for other in pair:
                    parts = [
                        (
                            spectra[q, other, at : at + GROUP, :],
                            spectra[q, other, part + at : part + at + GROUP, :],
                        )
                        for q in range(RADIX)
                    ]
                    for p, (re, im) in enumerate(butterfly(parts, 1)):
                        here = slice(at + p * part, at + p * part + GROUP)
                        backs[other, 0, here, :] = re.astype(jnp.bfloat16)
                        backs[other, 1, here, :] = im.astype(jnp.bfloat16)

        def add(c, b, at, value):
            where = pl.ds(pl.multiple_of(base + at, GROUP), value.shape[0])
            grown[c, block + b, where, :] += value

        def add_wrapped(c, b, at, value):
            if at == 0:
                add(c, b, 0, jnp.where(below, value[:GROUP], 0.0))
                add(c, b, side_len, jnp.where(below, 0.0, value[:GROUP]))
                add(c, b, GROUP, value[GROUP:])
            else:
                add(c, b, at, value)

        def right_back(at, tall):
            parts = []
            for other in range(RADIX):
                back = jnp.concatenate(
                    [
                        side_by_side(
                            backs[other, 0, here : here + tall, :],
                            backs[other, 1, here : here + tall, :],
                        )
                        for here in range(at, side_len, part)
                    ],
                    axis=0,
                )
                grad = dot(back, table(0, 1, other))
                parts.append((grad[:, :part], grad[:, part:]))
            return parts

        def accumulate(at, tall, parts):
            for p in range(RADIX):
                here = at + p * part
                rows = slice(p * tall, (p + 1) * tall)
                some = [(re[rows], im[rows]) for re, im in parts]
                for b, (re, im) in enumerate(butterfly(some, 1)):
                    probe_re = probes[slot, 0, b, here : here + tall, :]
                    probe_im = probes[slot, 1, b, here : here + tall, :]
                    values = (probe_re * re + probe_im * im, probe_re * im - probe_im * re)
                    for c, value in enumerate(values):
                        if b == 0:
                            add_wrapped(c, 0, here, jnp.where(stay, value, 0.0))
                            add_wrapped(c, side_blocks, here, jnp.where(stay, 0.0, value))
                        else:
                            add_wrapped(c, b, here, value)

        exit_waves((0, 2))
        early = [left(q, (0, 2)) for q in range(RADIX)]
        exit_waves((1, 3))
        for q in range(RADIX):
            rows = slice(q * part, (q + 1) * part)
            (r0, r2), (r1, r3) = early[q], left(q, (1, 3))
            for other, (re, im) in enumerate(butterfly([r0, r1, r2, r3], -1)):
                halves[other, 0, rows, :] = re.astype(jnp.bfloat16)
                halves[other, 1, rows, :] = im.astype(jnp.bfloat16)
        ahead = far_field(0)
        for other in range(RADIX):
            far = ahead
            if other + 1 < RADIX:
                ahead = far_field(other + 1)
            misfit_of(other, far)
            if other == 2:
                for q in range(RADIX):
                    left_back(q, (0, 1))
        tall = part // 2
        ats = [range(at, at + tall, GROUP) for at in range(0, part, tall)]
        for q in range(RADIX):
            left_back(q, (2, 3))
        mix(ats[0], (0, 1))
        mix(ats[0], (2, 3))
        first = right_back(0, tall)
        mix(ats[1], (0, 1))
        mix(ats[1], (2, 3))
        second = right_back(tall, tall)
        accumulate(0, tall, first)
        accumulate(tall, tall, second)
        return carry

    lax.fori_loop(0, live_ref[0, lax.axis_index("scan")], one_slot, 0)


def solve(live_counts, shifts, prepared, limit):
    grown = prepared[-1]
    side_len = prepared[1].shape[3]
    part = side_len // RADIX
    smem = pl.BlockSpec(memory_space=pltpu.SMEM)
    vmem = pl.BlockSpec(memory_space=pltpu.VMEM)
    wide = (RADIX, RADIX, 2 * part, part)
    tall = (RADIX, 2, side_len, part)
    scratch = [
        (wide, jnp.bfloat16),
        (tall, jnp.bfloat16),
        (wide, jnp.bfloat16),
        (wide, jnp.float32),
        (tall, jnp.bfloat16),
    ]
    return pl.pallas_call(
        solve_kernel,
        out_shape=pltpu.VMEM(grown.shape, grown.dtype),
        in_specs=[smem, smem] + [vmem] * len(prepared),
        out_specs=vmem,
        scratch_shapes=[pltpu.VMEM(*each) for each in scratch],
        input_output_aliases={1 + len(prepared): 0},
        compiler_params=pltpu.CompilerParams(vmem_limit_bytes=limit),
    )(live_counts, shifts, *prepared)


def shards(axes, object_slab, probe_field, intensities, offsets, live_count):
    tables = residue_tables(probe_field.shape[-1])
    shifts = offsets[0, 0].T
    prepared, limit = gather(axes, shifts, object_slab, intensities[0, 0], probe_field, tables)
    grown = solve(live_count.T, shifts, prepared, limit)
    return scatter(axes, grown, object_slab.shape[1])


def solution(mesh):
    placed = (
        P(None, "tile", "scan"),
        P(),
        P("scan", "tile", None, None, None),
        P("scan", "tile", None, None),
        P(None, "tile"),
    )
    axes = tuple((name, mesh.shape[name]) for name in ("scan", "tile"))
    return jax.shard_map(
        functools.partial(shards, axes), mesh=mesh, in_specs=placed, out_specs=P(None, "tile", "scan"), check_vma=False
    )
```

```python
import functools
import math

import jax
import jax.numpy as jnp
import numpy as np
from jax import lax
from jax.experimental import pallas as pl
from jax.experimental.pallas import tpu as pltpu
from jax.sharding import PartitionSpec as P

RADIX = 4
LANES = 128
GROUP = 16


def residue_tables(side_len):
    part = side_len // RADIX
    freq = np.arange(side_len).reshape(part, RADIX).T
    across = np.arange(part)
    phase = (freq[:, :, None] * across[None, None, :] % side_len) * (2.0 * math.pi / side_len)
    factor = 1.0 / math.sqrt(side_len)
    cos = np.cos(phase) * factor
    sin = np.sin(phase) * factor
    rows = np.concatenate(
        [np.concatenate([cos, sin], axis=2), np.concatenate([-sin, cos], axis=2)], axis=1
    ).astype(np.float32)
    return jnp.asarray(rows, jnp.bfloat16), jnp.asarray(rows.swapaxes(1, 2), jnp.bfloat16)


def sorted_by_residue(side_len):
    at = np.arange(side_len)
    source = at % (side_len // RADIX) * RADIX + at // (side_len // RADIX)
    sort = (source[:, None] == at[None, :]).astype(np.float32)
    return jnp.asarray(sort, jnp.bfloat16), jnp.asarray(sort.T, jnp.bfloat16)


def dot(a, b):
    return jnp.dot(a, b, preferred_element_type=jnp.float32)


def butterfly(parts, sign):
    (r0, i0), (r1, i1), (r2, i2), (r3, i3) = parts
    ar, ai, br, bi = r0 + r2, i0 + i2, r1 + r3, i1 + i3
    cr, ci, dr, di = r0 - r2, i0 - i2, r1 - r3, i1 - i3
    plus = (cr - di, ci + dr)
    minus = (cr + di, ci - dr)
    first, third = (plus, minus) if sign > 0 else (minus, plus)
    return [(ar + br, ai + bi), first, (ar - br, ai - bi), third]


def neighbours(axes):
    result = []
    for name, count in axes:
        me = lax.axis_index(name)
        result.append((me > 0, {name: me - 1}, me < count - 1, {name: me + 1}))
    return result


def greet(peers):
    barrier = pltpu.get_barrier_semaphore()
    for has_low, low, has_high, high in peers:
        for there, peer in ((has_low, low), (has_high, high)):

            @pl.when(there)
            def _(peer=peer):
                pl.semaphore_signal(
                    barrier, inc=1, device_id=peer, device_id_type=pl.DeviceIdType.MESH
                )


def all_here(peers):
    count = sum(
        there.astype(jnp.int32) for has_low, _, has_high, _ in peers for there in (has_low, has_high)
    )
    pl.semaphore_wait(pltpu.get_barrier_semaphore(), count)


def remote(source, target, sends, receives, index, peer):
    return pltpu.make_async_remote_copy(
        src_ref=source,
        dst_ref=target,
        send_sem=sends.at[index],
        recv_sem=receives.at[index],
        device_id=peer,
        device_id_type=pl.DeviceIdType.MESH,
    )


def quarter_turns(cos, sin, q):
    return ((cos, sin), (sin, -cos), (-cos, -sin), (-sin, cos))[q]


def in_place(mask, cos, sin, q):
    wrapped = quarter_turns(cos, sin, q)
    return jnp.where(mask, cos, wrapped[0]), jnp.where(mask, sin, wrapped[1])


def leads(count, row):
    odd = lax.rem(row, 2) == 1
    before_last = jnp.logical_and(row == count - 2, jnp.logical_not(odd))
    return jnp.logical_or(
        jnp.logical_and(odd, row == count - 1),
        jnp.logical_and(jnp.logical_not(odd), jnp.logical_not(before_last)),
    )


def gather_kernel(
    axes,
    shift_ref,
    own_hbm,
    measured_hbm,
    probe_hbm,
    rows_hbm,
    cols_hbm,
    sort_hbm,
    unsort_hbm,
    field,
    probes,
    tables,
    arranged,
    grown,
    own,
    measured,
    extended,
    rows_ref,
    cols_ref,
    doubled,
    sort,
    unsort,
    sends,
    receives,
    fetches,
    freed,
):
    slots, side_len = measured.shape[:2]
    tile_len = own.shape[1]
    part = side_len // RADIX
    own_blocks = tile_len // LANES
    side_blocks = side_len // LANES
    scan, tile = neighbours(axes)
    has_left, left, has_right, _ = scan
    has_up, up, has_down, down = tile
    greet((scan, tile))
    first = pltpu.make_async_copy(
        own_hbm.at[:, :side_len, :side_len], own.at[:, :side_len, :side_len], fetches.at[0]
    )
    second = pltpu.make_async_copy(
        own_hbm.at[:, side_len:, :side_len], own.at[:, side_len:, :side_len], fetches.at[1]
    )
    third = pltpu.make_async_copy(
        own_hbm.at[:, :side_len, side_len:], own.at[:, :side_len, side_len:], fetches.at[2]
    )
    fourth = pltpu.make_async_copy(
        own_hbm.at[:, side_len:, side_len:], own.at[:, side_len:, side_len:], fetches.at[3]
    )
    constants = [
        pltpu.make_async_copy(source, target, fetches.at[4 + i])
        for i, (source, target) in enumerate(
            (
                (sort_hbm, sort),
                (unsort_hbm, unsort),
                (measured_hbm, measured),
                (rows_hbm, rows_ref),
                (cols_hbm, cols_ref),
            )
        )
    ]
    for c in range(2):
        for b in range(side_blocks):
            cols = slice(b * LANES, (b + 1) * LANES)
            for source, target in (
                (probe_hbm.at[c, :, cols], extended.at[c, b, GROUP:, :]),
                (probe_hbm.at[c, side_len - GROUP :, cols], extended.at[c, b, :GROUP, :]),
            ):
                constants.append(
                    pltpu.make_async_copy(source, target, fetches.at[4 + len(constants)])
                )
    for load in [first, second, third, fourth] + constants:
        load.start()
    near = slice(0, side_blocks)
    far = slice(own_blocks, own_blocks + side_blocks)
    halves = [
        (c, slice(at, at + side_blocks // 2))
        for c in range(2)
        for at in range(0, side_blocks, side_blocks // 2)
    ]

    def moved(blocks):
        return slice(blocks.start + own_blocks, blocks.stop + own_blocks)

    tops = [
        remote(
            field.at[c, blocks, :side_len, :],
            field.at[c, moved(blocks), :side_len, :],
            sends,
            receives,
            3 + i,
            left,
        )
        for i, (c, blocks) in enumerate(halves)
    ]
    rests = [
        remote(
            field.at[c, near, side_len:tile_len, :],
            field.at[c, far, side_len:tile_len, :],
            sends,
            receives,
            c,
            left,
        )
        for c in range(2)
    ]
    under = remote(
        field.at[:, :own_blocks, :side_len, :],
        field.at[:, :own_blocks, tile_len:, :],
        sends,
        receives,
        2,
        up,
    )
    acrosses = [
        remote(
            field.at[c, moved(blocks), :side_len, :],
            field.at[c, moved(blocks), tile_len:, :],
            sends,
            receives,
            3 + len(halves) + i,
            up,
        )
        for i, (c, blocks) in enumerate(halves)
    ]

    def narrow(blocks, at):
        for c in range(2):
            for b in blocks:
                field[c, b, at, :] = own[c, at, b * LANES : (b + 1) * LANES].astype(jnp.bfloat16)

    first.wait()
    narrow(range(side_blocks), slice(0, side_len))
    all_here((scan, tile))

    row = lax.axis_index(axes[1][0])
    odd = lax.rem(row, 2) == 1
    leading = leads(axes[1][1], row)
    first_turn = jnp.logical_and(has_left, leading)
    second_turn = jnp.logical_and(has_left, jnp.logical_not(leading))
    keeps_back = jnp.logical_not(jnp.logical_or(leading, odd))

    @pl.when(jnp.logical_and(has_left, jnp.logical_not(keeps_back)))
    def _():
        for each in tops:
            each.start()

    second.wait()
    third.wait()
    narrow(range(side_blocks), slice(side_len, tile_len))
    narrow(range(side_blocks, own_blocks), slice(0, side_len))

    @pl.when(first_turn)
    def _():
        for each in rests:
            each.start()

    @pl.when(has_up)
    def _():
        under.start()

    @pl.when(jnp.logical_not(has_right))
    def _():
        field[:, far, :tile_len, :] = jnp.zeros(
            (2, side_blocks, tile_len, LANES), jnp.bfloat16
        )

    @pl.when(jnp.logical_not(has_down))
    def _():
        field[:, :, tile_len:, :] = jnp.zeros(
            (2, own_blocks + side_blocks, side_len, LANES), jnp.bfloat16
        )

    fourth.wait()
    narrow(range(side_blocks, own_blocks), slice(side_len, tile_len))
    for load in constants:
        load.wait()

    def sort_slot(slot, carry):
        rows = dot(sort[...], measured[slot]).astype(jnp.bfloat16)
        both = dot(rows, unsort[...]).astype(jnp.bfloat16)
        for b in range(RADIX):
            arranged[slot, b] = both[:, b * part : (b + 1) * part]
        return carry

    lax.fori_loop(0, slots, sort_slot, 0)

    grown[...] = jnp.zeros_like(grown)
    for q in range(RADIX):
        for i in range(2):
            for at in (0, part):
                doubled[q, i, at : at + part, :] = cols_ref[
                    q, i * part : (i + 1) * part, :part
                ].astype(jnp.float32)

    lane = lax.broadcasted_iota(jnp.int32, (1, LANES), 1)
    line = lax.broadcasted_iota(jnp.int32, (part, LANES), 0)
    chunk = 32

    def prepare(slot, carry):
        lift = lax.rem(shift_ref[0, slot], GROUP)
        turn = lax.rem(shift_ref[1, slot], LANES)

        def move_probe(i, carry):
            at = pl.multiple_of(i * chunk, chunk)
            for c in range(2):
                turned = [
                    pltpu.roll(extended[c, b, pl.ds(GROUP - lift + at, chunk), :], turn, 1)
                    for b in range(side_blocks)
                ]
                for b in range(side_blocks):
                    probes[slot, c, b, pl.ds(at, chunk), :] = jnp.where(
                        lane >= turn, turned[b], turned[b - 1]
                    )
            return carry

        lax.fori_loop(0, side_len // chunk, move_probe, 0)
        for k, by in enumerate((lift, turn)):
            for q in range(RADIX):
                cos = pltpu.roll(rows_ref[q, :part, :part].astype(jnp.float32), by, 1)
                sin = pltpu.roll(rows_ref[q, :part, part:].astype(jnp.float32), by, 1)
                cos, sin = in_place(lane >= by, cos, sin, q)
                tables[slot, 0, k, q, 0, :part, :] = cos.astype(jnp.bfloat16)
                tables[slot, 0, k, q, 1, :part, :] = sin.astype(jnp.bfloat16)
                tables[slot, 0, k, q, 0, part:, :] = (-sin).astype(jnp.bfloat16)
                tables[slot, 0, k, q, 1, part:, :] = cos.astype(jnp.bfloat16)
                cos = doubled[q, 0, pl.ds(part - by, part), :]
                sin = doubled[q, 1, pl.ds(part - by, part), :]
                cos, sin = in_place(line >= by, cos, sin, q)
                tables[slot, 1, k, q, 0, :part, :] = cos.astype(jnp.bfloat16)
                tables[slot, 1, k, q, 1, :part, :] = (-sin).astype(jnp.bfloat16)
                tables[slot, 1, k, q, 0, part:, :] = sin.astype(jnp.bfloat16)
                tables[slot, 1, k, q, 1, part:, :] = cos.astype(jnp.bfloat16)
        return carry

    lax.fori_loop(0, slots, prepare, 0)

    late = jnp.logical_and(has_left, keeps_back)

    @pl.when(late)
    def _():
        pl.semaphore_wait(freed, 1)
        for each in tops + rests:
            each.start()

    for top, across in zip(tops, acrosses):

        @pl.when(has_right)
        def _(top=top):
            top.wait_recv()

        @pl.when(has_up)
        def _(across=across):
            across.start()

    def hand_over(peer):
        pl.semaphore_signal(freed, inc=1, device_id=peer, device_id_type=pl.DeviceIdType.MESH)

    @pl.when(first_turn)
    def _():
        for each in tops:
            each.wait_send()

    @pl.when(jnp.logical_and(first_turn, odd))
    def _():
        hand_over(up)

    @pl.when(first_turn)
    def _():
        for each in rests:
            each.wait_send()

    @pl.when(jnp.logical_and(first_turn, jnp.logical_and(has_down, jnp.logical_not(odd))))
    def _():
        hand_over(down)

    @pl.when(jnp.logical_and(second_turn, odd))
    def _():
        pl.semaphore_wait(freed, 1)
        for each in rests:
            each.start()

    @pl.when(has_down)
    def _():
        under.wait_recv()

    @pl.when(has_right)
    def _():
        for each in rests:
            each.wait_recv()

    @pl.when(has_down)
    def _():
        for each in acrosses:
            each.wait_recv()

    @pl.when(second_turn)
    def _():
        for each in tops + rests:
            each.wait_send()

    @pl.when(has_up)
    def _():
        under.wait_send()
        for each in acrosses:
            each.wait_send()


def gather(axes, shifts, own, measured, probe, tables):
    slots, side_len = measured.shape[:2]
    tile_len = own.shape[1]
    span = tile_len + side_len
    part = side_len // RADIX
    side_blocks = side_len // LANES
    hbm = pl.BlockSpec(memory_space=pltpu.HBM)
    vmem = pl.BlockSpec(memory_space=pltpu.VMEM)
    table = (slots, 2, 2, RADIX, 2, 2 * part, part)
    scratch = [
        (own.shape, jnp.float32),
        (measured.shape, jnp.bfloat16),
        ((2, side_blocks, side_len + GROUP, LANES), jnp.float32),
        (tables[0].shape, jnp.bfloat16),
        (tables[1].shape, jnp.bfloat16),
        ((RADIX, 2, 2 * part, part), jnp.float32),
        ((side_len, side_len), jnp.bfloat16),
        ((side_len, side_len), jnp.bfloat16),
    ]
    call = pl.pallas_call(
        functools.partial(gather_kernel, axes),
        out_shape=[
            pltpu.VMEM((2, span // LANES, span, LANES), jnp.bfloat16),
            pltpu.VMEM((slots, 2, side_blocks, side_len, LANES), jnp.float32),
            pltpu.VMEM(table, jnp.bfloat16),
            pltpu.VMEM((slots, RADIX, side_len, part), jnp.bfloat16),
            pltpu.VMEM((2, span // LANES, span, LANES), jnp.float32),
        ],
        in_specs=[pl.BlockSpec(memory_space=pltpu.SMEM)] + [hbm] * 7,
        out_specs=[vmem] * 5,
        scratch_shapes=[pltpu.VMEM(*each) for each in scratch]
        + [
            pltpu.SemaphoreType.DMA((3 + 8,)),
            pltpu.SemaphoreType.DMA((3 + 8,)),
            pltpu.SemaphoreType.DMA((9 + 4 * side_blocks,)),
            pltpu.SemaphoreType.REGULAR,
        ],
        compiler_params=pltpu.CompilerParams(
            collective_id=0, has_side_effects=True, vmem_limit_bytes=room(scratch)
        ),
    )
    prepared = call(shifts, own, measured, probe, *tables, *sorted_by_residue(side_len))
    held = [pltpu.with_memory_space_constraint(each, pltpu.VMEM) for each in prepared]
    return held, room(scratch)


def room(scratch):
    return sum(math.prod(shape) * jnp.dtype(kind).itemsize for shape, kind in scratch) + (1 << 20)


def scatter_kernel(
    axes,
    grown,
    total,
    spill,
    dropped,
    both,
    landed,
    from_left,
    from_up,
    sends,
    receives,
    ready,
):
    side_len = landed.shape[2]
    tile_len = total.shape[1]
    own_blocks = tile_len // LANES
    side_blocks = side_len // LANES
    scan, tile = neighbours(axes)
    has_left, left, has_right, right = scan
    has_up, up, has_down, down = tile
    rows = axes[1][1]
    row = lax.axis_index(axes[1][0])
    first = leads(rows, row)
    second = jnp.logical_not(first)
    after_first = jnp.logical_and(has_up, leads(rows, row - 1))
    before_first = jnp.logical_and(has_down, leads(rows, row + 1))
    barrier = pltpu.get_barrier_semaphore()

    def tell(there, sem, peer):
        @pl.when(there)
        def _():
            pl.semaphore_signal(
                sem, inc=1, device_id=peer, device_id_type=pl.DeviceIdType.MESH
            )

    tell(has_left, barrier, left)
    tell(jnp.logical_and(has_up, jnp.logical_not(after_first)), barrier, up)
    tell(jnp.logical_and(has_down, jnp.logical_not(before_first)), barrier, down)
    corner = remote(both, landed, sends, receives, 0, down)
    under = remote(dropped, from_up, sends, receives, 1, down)
    rest = remote(
        spill.at[:, :, side_len:, :], from_left.at[:, :, side_len:, :], sends, receives, 2, right
    )
    top = remote(
        spill.at[:, :, :side_len, :], from_left.at[:, :, :side_len, :], sends, receives, 3, right
    )
    spill[:, :, side_len:, :] = grown[:, own_blocks:, side_len:tile_len, :].astype(jnp.bfloat16)
    both[...] = grown[:, own_blocks:, tile_len:, :].astype(jnp.bfloat16)
    beside = has_up.astype(jnp.int32) + has_down.astype(jnp.int32)
    awaited = has_right.astype(jnp.int32) + jnp.where(second, beside, 0)

    @pl.when(awaited > 0)
    def _():
        pl.semaphore_wait(barrier, awaited)

    @pl.when(has_right)
    def _():
        rest.start()

    tell(jnp.logical_and(second, after_first), ready, up)

    @pl.when(jnp.logical_and(second, has_down))
    def _():
        corner.start()

    @pl.when(jnp.logical_not(has_up))
    def _():
        spill[:, :, :side_len, :] = grown[:, own_blocks:, :side_len, :].astype(jnp.bfloat16)

    @pl.when(jnp.logical_and(jnp.logical_not(has_up), has_right))
    def _():
        top.start()

    dropped[...] = grown[:, :own_blocks, tile_len:, :].astype(jnp.bfloat16)

    @pl.when(jnp.logical_and(second, has_down))
    def _():
        under.start()

    for c in range(2):
        for b in range(own_blocks):
            total[c, :, b * LANES : (b + 1) * LANES] = grown[c, b, :tile_len, :]

    @pl.when(jnp.logical_and(first, has_down))
    def _():
        pl.semaphore_wait(ready, 1)
        corner.start()
        under.start()

    @pl.when(has_up)
    def _():
        corner.wait_recv()
        spill[:, :, :side_len, :] = (
            grown[:, own_blocks:, :side_len, :] + landed[...].astype(jnp.float32)
        ).astype(jnp.bfloat16)

    @pl.when(jnp.logical_and(has_up, has_right))
    def _():
        top.start()

    def add(blocks, at, source):
        for c in range(2):
            for b in blocks:
                total[c, at, b * LANES : (b + 1) * LANES] += source[c, b, at, :].astype(jnp.float32)

    @pl.when(has_left)
    def _():
        rest.wait_recv()
        add(range(side_blocks), slice(side_len, tile_len), from_left)

    @pl.when(has_up)
    def _():
        under.wait_recv()
        add(range(own_blocks), slice(0, side_len), from_up)

    @pl.when(has_left)
    def _():
        top.wait_recv()
        add(range(side_blocks), slice(0, side_len), from_left)

    @pl.when(has_right)
    def _():
        rest.wait_send()
        top.wait_send()

    @pl.when(has_down)
    def _():
        corner.wait_send()
        under.wait_send()


def scatter(axes, grown, tile_len):
    span = grown.shape[2]
    side_len = span - tile_len
    own_blocks = tile_len // LANES
    side_blocks = side_len // LANES
    vmem = pl.BlockSpec(memory_space=pltpu.VMEM)
    scratch = [
        ((2, side_blocks, tile_len, LANES), jnp.bfloat16),
        ((2, own_blocks, side_len, LANES), jnp.bfloat16),
        ((2, side_blocks, side_len, LANES), jnp.bfloat16),
        ((2, side_blocks, side_len, LANES), jnp.bfloat16),
        ((2, side_blocks, tile_len, LANES), jnp.bfloat16),
        ((2, own_blocks, side_len, LANES), jnp.bfloat16),
    ]
    return pl.pallas_call(
        functools.partial(scatter_kernel, axes),
        out_shape=pltpu.VMEM((2, tile_len, tile_len), jnp.float32),
        in_specs=[vmem],
        out_specs=vmem,
        scratch_shapes=[pltpu.VMEM(*each) for each in scratch]
        + [
            pltpu.SemaphoreType.DMA((4,)),
            pltpu.SemaphoreType.DMA((4,)),
            pltpu.SemaphoreType.REGULAR,
        ],
        compiler_params=pltpu.CompilerParams(
            collective_id=1, has_side_effects=True, vmem_limit_bytes=room(scratch)
        ),
    )(grown)


def side_by_side(*blocks):
    return jnp.concatenate(blocks, axis=1)


def solve_kernel(
    live_ref,
    shift_ref,
    field,
    probes,
    tables,
    measured,
    zeros,
    grown,
    mixed,
    halves,
    misfits,
    spectra,
    backs,
):
    side_len = probes.shape[3]
    part = side_len // RADIX
    side_blocks = side_len // LANES
    lane = lax.broadcasted_iota(jnp.int32, (1, LANES), 1)
    line = lax.broadcasted_iota(jnp.int32, (GROUP, LANES), 0)

    def one_slot(slot, carry):
        row = shift_ref[0, slot]
        col = shift_ref[1, slot]
        lift = lax.rem(row, GROUP)
        turn = lax.rem(col, LANES)
        base = pl.multiple_of(row - lift, GROUP)
        block = lax.div(col, LANES)
        stay = lane >= turn
        below = line >= lift

        def table(side, kind, q):
            return side_by_side(tables[slot, side, kind, q, 0], tables[slot, side, kind, q, 1])

        def piece(c, b, at):
            def cut(b):
                start = pl.multiple_of(base + at, GROUP)
                value = field[c, block + b, pl.ds(start, GROUP), :].astype(jnp.float32)
                if at == 0:
                    start = pl.multiple_of(base + side_len, GROUP)
                    wrapped = field[c, block + b, pl.ds(start, GROUP), :].astype(jnp.float32)
                    value = jnp.where(below, value, wrapped)
                return value

            return cut(b) if b else jnp.where(stay, cut(0), cut(side_blocks))

        def exit_waves(blocks):
            for at in range(0, part, GROUP):
                for b in blocks:
                    waves = []
                    for p in range(RADIX):
                        here = at + p * part
                        re, im = piece(0, b, here), piece(1, b, here)
                        probe_re = probes[slot, 0, b, here : here + GROUP, :]
                        probe_im = probes[slot, 1, b, here : here + GROUP, :]
                        waves.append((probe_re * re - probe_im * im, probe_re * im + probe_im * re))
                    for q, (re, im) in enumerate(butterfly(waves, -1)):
                        mixed[q, b, at : at + GROUP, :] = re.astype(jnp.bfloat16)
                        mixed[q, b, at + part : at + part + GROUP, :] = im.astype(jnp.bfloat16)

        def split(value):
            return [
                (value[:part, at : at + part], value[part:, at : at + part])
                for at in range(0, value.shape[1], part)
            ]

        def left(q, blocks):
            return split(dot(table(0, 0, q), side_by_side(*(mixed[q, b] for b in blocks))))

        def far_field(other):
            return dot(side_by_side(halves[other, 0], halves[other, 1]), table(1, 1, other))

        def misfit_of(other, far):
            for q in range(RADIX):
                rows = slice(q * part, (q + 1) * part)
                far_re, far_im = far[rows, :part], far[rows, part:]
                seen = measured[slot, other, rows, :].astype(jnp.float32)
                misfit = far_re * far_re + far_im * far_im - seen
                misfits[q, other, :part, :] = (misfit * far_re).astype(jnp.bfloat16)
                misfits[q, other, part:, :] = (misfit * far_im).astype(jnp.bfloat16)

        def left_back(q, pair):
            mixture = dot(table(1, 0, q), side_by_side(*(misfits[q, other] for other in pair)))
            for i, other in enumerate(pair):
                spectra[q, other] = mixture[:, i * part : (i + 1) * part]

        def mix(ats, pair):
            for at in ats:
                for other in pair:
                    parts = [
                        (
                            spectra[q, other, at : at + GROUP, :],
                            spectra[q, other, part + at : part + at + GROUP, :],
                        )
                        for q in range(RADIX)
                    ]
                    for p, (re, im) in enumerate(butterfly(parts, 1)):
                        here = slice(at + p * part, at + p * part + GROUP)
                        backs[other, 0, here, :] = re.astype(jnp.bfloat16)
                        backs[other, 1, here, :] = im.astype(jnp.bfloat16)

        def add(c, b, at, value):
            where = pl.ds(pl.multiple_of(base + at, GROUP), value.shape[0])
            grown[c, block + b, where, :] += value

        def add_wrapped(c, b, at, value):
            if at == 0:
                add(c, b, 0, jnp.where(below, value[:GROUP], 0.0))
                add(c, b, side_len, jnp.where(below, 0.0, value[:GROUP]))
                add(c, b, GROUP, value[GROUP:])
            else:
                add(c, b, at, value)

        def right_back(at, tall):
            parts = []
            for other in range(RADIX):
                back = jnp.concatenate(
                    [
                        side_by_side(
                            backs[other, 0, here : here + tall, :],
                            backs[other, 1, here : here + tall, :],
                        )
                        for here in range(at, side_len, part)
                    ],
                    axis=0,
                )
                grad = dot(back, table(0, 1, other))
                parts.append((grad[:, :part], grad[:, part:]))
            return parts

        def accumulate(at, tall, parts):
            for p in range(RADIX):
                here = at + p * part
                rows = slice(p * tall, (p + 1) * tall)
                some = [(re[rows], im[rows]) for re, im in parts]
                for b, (re, im) in enumerate(butterfly(some, 1)):
                    probe_re = probes[slot, 0, b, here : here + tall, :]
                    probe_im = probes[slot, 1, b, here : here + tall, :]
                    values = (probe_re * re + probe_im * im, probe_re * im - probe_im * re)
                    for c, value in enumerate(values):
                        if b == 0:
                            add_wrapped(c, 0, here, jnp.where(stay, value, 0.0))
                            add_wrapped(c, side_blocks, here, jnp.where(stay, 0.0, value))
                        else:
                            add_wrapped(c, b, here, value)

        exit_waves((0, 2))
        early = [left(q, (0, 2)) for q in range(RADIX)]
        exit_waves((1, 3))
        for q in range(RADIX):
            rows = slice(q * part, (q + 1) * part)
            (r0, r2), (r1, r3) = early[q], left(q, (1, 3))
            for other, (re, im) in enumerate(butterfly([r0, r1, r2, r3], -1)):
                halves[other, 0, rows, :] = re.astype(jnp.bfloat16)
                halves[other, 1, rows, :] = im.astype(jnp.bfloat16)
        ahead = far_field(0)
        for other in range(RADIX):
            far = ahead
            if other + 1 < RADIX:
                ahead = far_field(other + 1)
            misfit_of(other, far)
            if other == 2:
                for q in range(RADIX):
                    left_back(q, (0, 1))
        tall = part // 2
        ats = [range(at, at + tall, GROUP) for at in range(0, part, tall)]
        for q in range(RADIX):
            left_back(q, (2, 3))
        mix(ats[0], (0, 1))
        mix(ats[0], (2, 3))
        first = right_back(0, tall)
        mix(ats[1], (0, 1))
        mix(ats[1], (2, 3))
        second = right_back(tall, tall)
        accumulate(0, tall, first)
        accumulate(tall, tall, second)
        return carry

    lax.fori_loop(0, live_ref[0, lax.axis_index("scan")], one_slot, 0)


def solve(live_counts, shifts, prepared, limit):
    grown = prepared[-1]
    side_len = prepared[1].shape[3]
    part = side_len // RADIX
    smem = pl.BlockSpec(memory_space=pltpu.SMEM)
    vmem = pl.BlockSpec(memory_space=pltpu.VMEM)
    wide = (RADIX, RADIX, 2 * part, part)
    tall = (RADIX, 2, side_len, part)
    scratch = [
        (wide, jnp.bfloat16),
        (tall, jnp.bfloat16),
        (wide, jnp.bfloat16),
        (wide, jnp.float32),
        (tall, jnp.bfloat16),
    ]
    return pl.pallas_call(
        solve_kernel,
        out_shape=pltpu.VMEM(grown.shape, grown.dtype),
        in_specs=[smem, smem] + [vmem] * len(prepared),
        out_specs=vmem,
        scratch_shapes=[pltpu.VMEM(*each) for each in scratch],
        input_output_aliases={1 + len(prepared): 0},
        compiler_params=pltpu.CompilerParams(vmem_limit_bytes=limit),
    )(live_counts, shifts, *prepared)


def shards(axes, object_slab, probe_field, intensities, offsets, live_count):
    tables = residue_tables(probe_field.shape[-1])
    shifts = offsets[0, 0].T
    prepared, limit = gather(axes, shifts, object_slab, intensities[0, 0], probe_field, tables)
    grown = solve(live_count.T, shifts, prepared, limit)
    return scatter(axes, grown, object_slab.shape[1])


def solution(mesh):
    placed = (
        P(None, "tile", "scan"),
        P(),
        P("scan", "tile", None, None, None),
        P("scan", "tile", None, None),
        P(None, "tile"),
    )
    axes = tuple((name, mesh.shape[name]) for name in ("scan", "tile"))
    return jax.shard_map(
        functools.partial(shards, axes), mesh=mesh, in_specs=placed, out_specs=P(None, "tile", "scan"), check_vma=False
    )
```

```python
import functools
import math

import jax
import jax.numpy as jnp
import numpy as np
from jax import lax
from jax.experimental import pallas as pl
from jax.experimental.pallas import tpu as pltpu
from jax.sharding import PartitionSpec as P

RADIX = 4
LANES = 128
GROUP = 16


def residue_tables(side_len):
    part = side_len // RADIX
    freq = np.arange(side_len).reshape(part, RADIX).T
    across = np.arange(part)
    phase = (freq[:, :, None] * across[None, None, :] % side_len) * (2.0 * math.pi / side_len)
    factor = 1.0 / math.sqrt(side_len)
    cos = np.cos(phase) * factor
    sin = np.sin(phase) * factor
    rows = np.concatenate(
        [np.concatenate([cos, sin], axis=2), np.concatenate([-sin, cos], axis=2)], axis=1
    ).astype(np.float32)
    return jnp.asarray(rows, jnp.bfloat16), jnp.asarray(rows.swapaxes(1, 2), jnp.bfloat16)


def sorted_by_residue(side_len):
    at = np.arange(side_len)
    source = at % (side_len // RADIX) * RADIX + at // (side_len // RADIX)
    sort = (source[:, None] == at[None, :]).astype(np.float32)
    return jnp.asarray(sort, jnp.bfloat16), jnp.asarray(sort.T, jnp.bfloat16)


def dot(a, b):
    return jnp.dot(a, b, preferred_element_type=jnp.float32)


def butterfly(parts, sign):
    (r0, i0), (r1, i1), (r2, i2), (r3, i3) = parts
    ar, ai, br, bi = r0 + r2, i0 + i2, r1 + r3, i1 + i3
    cr, ci, dr, di = r0 - r2, i0 - i2, r1 - r3, i1 - i3
    plus = (cr - di, ci + dr)
    minus = (cr + di, ci - dr)
    first, third = (plus, minus) if sign > 0 else (minus, plus)
    return [(ar + br, ai + bi), first, (ar - br, ai - bi), third]


def neighbours(axes):
    result = []
    for name, count in axes:
        me = lax.axis_index(name)
        result.append((me > 0, {name: me - 1}, me < count - 1, {name: me + 1}))
    return result


def greet(peers):
    barrier = pltpu.get_barrier_semaphore()
    for has_low, low, has_high, high in peers:
        for there, peer in ((has_low, low), (has_high, high)):

            @pl.when(there)
            def _(peer=peer):
                pl.semaphore_signal(
                    barrier, inc=1, device_id=peer, device_id_type=pl.DeviceIdType.MESH
                )


def all_here(peers):
    count = sum(
        there.astype(jnp.int32) for has_low, _, has_high, _ in peers for there in (has_low, has_high)
    )
    pl.semaphore_wait(pltpu.get_barrier_semaphore(), count)


def remote(source, target, sends, receives, index, peer):
    return pltpu.make_async_remote_copy(
        src_ref=source,
        dst_ref=target,
        send_sem=sends.at[index],
        recv_sem=receives.at[index],
        device_id=peer,
        device_id_type=pl.DeviceIdType.MESH,
    )


def quarter_turns(cos, sin, q):
    return ((cos, sin), (sin, -cos), (-cos, -sin), (-sin, cos))[q]


def in_place(mask, cos, sin, q):
    wrapped = quarter_turns(cos, sin, q)
    return jnp.where(mask, cos, wrapped[0]), jnp.where(mask, sin, wrapped[1])


def gather_kernel(
    axes,
    shift_ref,
    own_hbm,
    measured_hbm,
    probe_hbm,
    rows_hbm,
    cols_hbm,
    sort_hbm,
    unsort_hbm,
    field,
    probes,
    tables,
    arranged,
    grown,
    own,
    measured,
    extended,
    rows_ref,
    cols_ref,
    doubled,
    sort,
    unsort,
    sends,
    receives,
    fetches,
    freed,
):
    slots, side_len = measured.shape[:2]
    tile_len = own.shape[1]
    part = side_len // RADIX
    own_blocks = tile_len // LANES
    side_blocks = side_len // LANES
    scan, tile = neighbours(axes)
    has_left, left, has_right, _ = scan
    has_up, up, has_down, down = tile
    greet((scan, tile))
    first = pltpu.make_async_copy(
        own_hbm.at[:, :side_len, :side_len], own.at[:, :side_len, :side_len], fetches.at[0]
    )
    second = pltpu.make_async_copy(
        own_hbm.at[:, side_len:, :side_len], own.at[:, side_len:, :side_len], fetches.at[1]
    )
    third = pltpu.make_async_copy(
        own_hbm.at[:, :side_len, side_len:], own.at[:, :side_len, side_len:], fetches.at[2]
    )
    fourth = pltpu.make_async_copy(
        own_hbm.at[:, side_len:, side_len:], own.at[:, side_len:, side_len:], fetches.at[3]
    )
    constants = [
        pltpu.make_async_copy(source, target, fetches.at[4 + i])
        for i, (source, target) in enumerate(
            (
                (sort_hbm, sort),
                (unsort_hbm, unsort),
                (measured_hbm, measured),
                (rows_hbm, rows_ref),
                (cols_hbm, cols_ref),
            )
        )
    ]
    for c in range(2):
        for b in range(side_blocks):
            cols = slice(b * LANES, (b + 1) * LANES)
            for source, target in (
                (probe_hbm.at[c, :, cols], extended.at[c, b, GROUP:, :]),
                (probe_hbm.at[c, side_len - GROUP :, cols], extended.at[c, b, :GROUP, :]),
            ):
                constants.append(
                    pltpu.make_async_copy(source, target, fetches.at[4 + len(constants)])
                )
    for load in [first, second, third, fourth] + constants:
        load.start()
    near = slice(0, side_blocks)
    far = slice(own_blocks, own_blocks + side_blocks)
    halves = [
        (c, slice(at, at + side_blocks // 2))
        for c in range(2)
        for at in range(0, side_blocks, side_blocks // 2)
    ]

    def moved(blocks):
        return slice(blocks.start + own_blocks, blocks.stop + own_blocks)

    tops = [
        remote(
            field.at[c, blocks, :side_len, :],
            field.at[c, moved(blocks), :side_len, :],
            sends,
            receives,
            3 + i,
            left,
        )
        for i, (c, blocks) in enumerate(halves)
    ]
    rests = [
        remote(
            field.at[c, near, side_len:tile_len, :],
            field.at[c, far, side_len:tile_len, :],
            sends,
            receives,
            c,
            left,
        )
        for c in range(2)
    ]
    under = remote(
        field.at[:, :own_blocks, :side_len, :],
        field.at[:, :own_blocks, tile_len:, :],
        sends,
        receives,
        2,
        up,
    )
    acrosses = [
        remote(
            field.at[c, moved(blocks), :side_len, :],
            field.at[c, moved(blocks), tile_len:, :],
            sends,
            receives,
            3 + len(halves) + i,
            up,
        )
        for i, (c, blocks) in enumerate(halves)
    ]

    def narrow(blocks, at):
        for c in range(2):
            for b in blocks:
                field[c, b, at, :] = own[c, at, b * LANES : (b + 1) * LANES].astype(jnp.bfloat16)

    first.wait()
    narrow(range(side_blocks), slice(0, side_len))
    all_here((scan, tile))

    @pl.when(has_left)
    def _():
        for each in tops:
            each.start()

    second.wait()
    third.wait()
    narrow(range(side_blocks), slice(side_len, tile_len))
    narrow(range(side_blocks, own_blocks), slice(0, side_len))

    odd = lax.rem(lax.axis_index(axes[1][0]), 2) == 1
    first_turn = jnp.logical_and(has_left, jnp.logical_not(odd))
    second_turn = jnp.logical_and(has_left, odd)

    @pl.when(first_turn)
    def _():
        for each in rests:
            each.start()

    @pl.when(has_up)
    def _():
        under.start()

    @pl.when(jnp.logical_not(has_right))
    def _():
        field[:, far, :tile_len, :] = jnp.zeros(
            (2, side_blocks, tile_len, LANES), jnp.bfloat16
        )

    @pl.when(jnp.logical_not(has_down))
    def _():
        field[:, :, tile_len:, :] = jnp.zeros(
            (2, own_blocks + side_blocks, side_len, LANES), jnp.bfloat16
        )

    fourth.wait()
    narrow(range(side_blocks, own_blocks), slice(side_len, tile_len))
    for load in constants:
        load.wait()

    def sort_slot(slot, carry):
        rows = dot(sort[...], measured[slot]).astype(jnp.bfloat16)
        both = dot(rows, unsort[...]).astype(jnp.bfloat16)
        for b in range(RADIX):
            arranged[slot, b] = both[:, b * part : (b + 1) * part]
        return carry

    lax.fori_loop(0, slots, sort_slot, 0)

    grown[...] = jnp.zeros_like(grown)
    for q in range(RADIX):
        for i in range(2):
            for at in (0, part):
                doubled[q, i, at : at + part, :] = cols_ref[
                    q, i * part : (i + 1) * part, :part
                ].astype(jnp.float32)

    lane = lax.broadcasted_iota(jnp.int32, (1, LANES), 1)
    line = lax.broadcasted_iota(jnp.int32, (part, LANES), 0)
    chunk = 32

    def prepare(slot, carry):
        lift = lax.rem(shift_ref[0, slot], GROUP)
        turn = lax.rem(shift_ref[1, slot], LANES)

        def move_probe(i, carry):
            at = pl.multiple_of(i * chunk, chunk)
            for c in range(2):
                turned = [
                    pltpu.roll(extended[c, b, pl.ds(GROUP - lift + at, chunk), :], turn, 1)
                    for b in range(side_blocks)
                ]
                for b in range(side_blocks):
                    probes[slot, c, b, pl.ds(at, chunk), :] = jnp.where(
                        lane >= turn, turned[b], turned[b - 1]
                    )
            return carry

        lax.fori_loop(0, side_len // chunk, move_probe, 0)
        for k, by in enumerate((lift, turn)):
            for q in range(RADIX):
                cos = pltpu.roll(rows_ref[q, :part, :part].astype(jnp.float32), by, 1)
                sin = pltpu.roll(rows_ref[q, :part, part:].astype(jnp.float32), by, 1)
                cos, sin = in_place(lane >= by, cos, sin, q)
                tables[slot, 0, k, q, 0, :part, :] = cos.astype(jnp.bfloat16)
                tables[slot, 0, k, q, 1, :part, :] = sin.astype(jnp.bfloat16)
                tables[slot, 0, k, q, 0, part:, :] = (-sin).astype(jnp.bfloat16)
                tables[slot, 0, k, q, 1, part:, :] = cos.astype(jnp.bfloat16)
                cos = doubled[q, 0, pl.ds(part - by, part), :]
                sin = doubled[q, 1, pl.ds(part - by, part), :]
                cos, sin = in_place(line >= by, cos, sin, q)
                tables[slot, 1, k, q, 0, :part, :] = cos.astype(jnp.bfloat16)
                tables[slot, 1, k, q, 1, :part, :] = (-sin).astype(jnp.bfloat16)
                tables[slot, 1, k, q, 0, part:, :] = sin.astype(jnp.bfloat16)
                tables[slot, 1, k, q, 1, part:, :] = cos.astype(jnp.bfloat16)
        return carry

    lax.fori_loop(0, slots, prepare, 0)

    for top, across in zip(tops, acrosses):

        @pl.when(has_right)
        def _(top=top):
            top.wait_recv()

        @pl.when(has_up)
        def _(across=across):
            across.start()

    @pl.when(first_turn)
    def _():
        for each in tops + rests:
            each.wait_send()

    @pl.when(jnp.logical_and(first_turn, has_down))
    def _():
        pl.semaphore_signal(
            freed, inc=1, device_id=down, device_id_type=pl.DeviceIdType.MESH
        )

    @pl.when(second_turn)
    def _():
        pl.semaphore_wait(freed, 1)
        for each in rests:
            each.start()


    @pl.when(has_down)
    def _():
        under.wait_recv()

    @pl.when(has_right)
    def _():
        for each in rests:
            each.wait_recv()

    @pl.when(has_down)
    def _():
        for each in acrosses:
            each.wait_recv()

    @pl.when(second_turn)
    def _():
        for each in tops + rests:
            each.wait_send()

    @pl.when(has_up)
    def _():
        under.wait_send()
        for each in acrosses:
            each.wait_send()


def gather(axes, shifts, own, measured, probe, tables):
    slots, side_len = measured.shape[:2]
    tile_len = own.shape[1]
    span = tile_len + side_len
    part = side_len // RADIX
    side_blocks = side_len // LANES
    hbm = pl.BlockSpec(memory_space=pltpu.HBM)
    vmem = pl.BlockSpec(memory_space=pltpu.VMEM)
    table = (slots, 2, 2, RADIX, 2, 2 * part, part)
    scratch = [
        (own.shape, jnp.float32),
        (measured.shape, jnp.bfloat16),
        ((2, side_blocks, side_len + GROUP, LANES), jnp.float32),
        (tables[0].shape, jnp.bfloat16),
        (tables[1].shape, jnp.bfloat16),
        ((RADIX, 2, 2 * part, part), jnp.float32),
        ((side_len, side_len), jnp.bfloat16),
        ((side_len, side_len), jnp.bfloat16),
    ]
    call = pl.pallas_call(
        functools.partial(gather_kernel, axes),
        out_shape=[
            pltpu.VMEM((2, span // LANES, span, LANES), jnp.bfloat16),
            pltpu.VMEM((slots, 2, side_blocks, side_len, LANES), jnp.float32),
            pltpu.VMEM(table, jnp.bfloat16),
            pltpu.VMEM((slots, RADIX, side_len, part), jnp.bfloat16),
            pltpu.VMEM((2, span // LANES, span, LANES), jnp.float32),
        ],
        in_specs=[pl.BlockSpec(memory_space=pltpu.SMEM)] + [hbm] * 7,
        out_specs=[vmem] * 5,
        scratch_shapes=[pltpu.VMEM(*each) for each in scratch]
        + [
            pltpu.SemaphoreType.DMA((3 + 8,)),
            pltpu.SemaphoreType.DMA((3 + 8,)),
            pltpu.SemaphoreType.DMA((9 + 4 * side_blocks,)),
            pltpu.SemaphoreType.REGULAR,
        ],
        compiler_params=pltpu.CompilerParams(
            collective_id=0, has_side_effects=True, vmem_limit_bytes=room(scratch)
        ),
    )
    prepared = call(shifts, own, measured, probe, *tables, *sorted_by_residue(side_len))
    held = [pltpu.with_memory_space_constraint(each, pltpu.VMEM) for each in prepared]
    return held, room(scratch)


def room(scratch):
    return sum(math.prod(shape) * jnp.dtype(kind).itemsize for shape, kind in scratch) + (1 << 20)


def scatter_kernel(
    axes,
    grown,
    total,
    spill,
    dropped,
    both,
    landed,
    from_left,
    from_up,
    sends,
    receives,
    ready,
):
    side_len = landed.shape[2]
    tile_len = total.shape[1]
    own_blocks = tile_len // LANES
    side_blocks = side_len // LANES
    scan, tile = neighbours(axes)
    has_left, left, has_right, right = scan
    has_up, up, has_down, down = tile
    odd = lax.rem(lax.axis_index(axes[1][0]), 2) == 1
    even = jnp.logical_not(odd)
    barrier = pltpu.get_barrier_semaphore()

    def tell(there, sem, peer):
        @pl.when(there)
        def _():
            pl.semaphore_signal(
                sem, inc=1, device_id=peer, device_id_type=pl.DeviceIdType.MESH
            )

    tell(has_left, barrier, left)
    tell(jnp.logical_and(even, has_up), barrier, up)
    tell(jnp.logical_and(even, has_down), barrier, down)
    corner = remote(both, landed, sends, receives, 0, down)
    under = remote(dropped, from_up, sends, receives, 1, down)
    rest = remote(
        spill.at[:, :, side_len:, :], from_left.at[:, :, side_len:, :], sends, receives, 2, right
    )
    top = remote(
        spill.at[:, :, :side_len, :], from_left.at[:, :, :side_len, :], sends, receives, 3, right
    )
    spill[:, :, side_len:, :] = grown[:, own_blocks:, side_len:tile_len, :].astype(jnp.bfloat16)
    both[...] = grown[:, own_blocks:, tile_len:, :].astype(jnp.bfloat16)
    from_even = has_up.astype(jnp.int32) + has_down.astype(jnp.int32)
    awaited = has_right.astype(jnp.int32) + jnp.where(odd, from_even, 0)

    @pl.when(awaited > 0)
    def _():
        pl.semaphore_wait(barrier, awaited)

    @pl.when(has_right)
    def _():
        rest.start()

    tell(odd, ready, up)

    @pl.when(jnp.logical_and(odd, has_down))
    def _():
        corner.start()

    @pl.when(jnp.logical_not(has_up))
    def _():
        spill[:, :, :side_len, :] = grown[:, own_blocks:, :side_len, :].astype(jnp.bfloat16)

    @pl.when(jnp.logical_and(jnp.logical_not(has_up), has_right))
    def _():
        top.start()

    dropped[...] = grown[:, :own_blocks, tile_len:, :].astype(jnp.bfloat16)

    @pl.when(jnp.logical_and(odd, has_down))
    def _():
        under.start()

    for c in range(2):
        for b in range(own_blocks):
            total[c, :, b * LANES : (b + 1) * LANES] = grown[c, b, :tile_len, :]

    @pl.when(jnp.logical_and(even, has_down))
    def _():
        pl.semaphore_wait(ready, 1)
        corner.start()
        under.start()

    @pl.when(has_up)
    def _():
        corner.wait_recv()
        spill[:, :, :side_len, :] = (
            grown[:, own_blocks:, :side_len, :] + landed[...].astype(jnp.float32)
        ).astype(jnp.bfloat16)

    @pl.when(jnp.logical_and(has_up, has_right))
    def _():
        top.start()

    def add(blocks, at, source):
        for c in range(2):
            for b in blocks:
                total[c, at, b * LANES : (b + 1) * LANES] += source[c, b, at, :].astype(jnp.float32)

    @pl.when(has_left)
    def _():
        rest.wait_recv()
        add(range(side_blocks), slice(side_len, tile_len), from_left)

    @pl.when(has_up)
    def _():
        under.wait_recv()
        add(range(own_blocks), slice(0, side_len), from_up)

    @pl.when(has_left)
    def _():
        top.wait_recv()
        add(range(side_blocks), slice(0, side_len), from_left)

    @pl.when(has_right)
    def _():
        rest.wait_send()
        top.wait_send()

    @pl.when(has_down)
    def _():
        corner.wait_send()
        under.wait_send()


def scatter(axes, grown, tile_len):
    span = grown.shape[2]
    side_len = span - tile_len
    own_blocks = tile_len // LANES
    side_blocks = side_len // LANES
    vmem = pl.BlockSpec(memory_space=pltpu.VMEM)
    scratch = [
        ((2, side_blocks, tile_len, LANES), jnp.bfloat16),
        ((2, own_blocks, side_len, LANES), jnp.bfloat16),
        ((2, side_blocks, side_len, LANES), jnp.bfloat16),
        ((2, side_blocks, side_len, LANES), jnp.bfloat16),
        ((2, side_blocks, tile_len, LANES), jnp.bfloat16),
        ((2, own_blocks, side_len, LANES), jnp.bfloat16),
    ]
    return pl.pallas_call(
        functools.partial(scatter_kernel, axes),
        out_shape=pltpu.VMEM((2, tile_len, tile_len), jnp.float32),
        in_specs=[vmem],
        out_specs=vmem,
        scratch_shapes=[pltpu.VMEM(*each) for each in scratch]
        + [
            pltpu.SemaphoreType.DMA((4,)),
            pltpu.SemaphoreType.DMA((4,)),
            pltpu.SemaphoreType.REGULAR,
        ],
        compiler_params=pltpu.CompilerParams(
            collective_id=1, has_side_effects=True, vmem_limit_bytes=room(scratch)
        ),
    )(grown)


def side_by_side(*blocks):
    return jnp.concatenate(blocks, axis=1)


def solve_kernel(
    live_ref,
    shift_ref,
    field,
    probes,
    tables,
    measured,
    zeros,
    grown,
    mixed,
    halves,
    misfits,
    spectra,
    backs,
):
    side_len = probes.shape[3]
    part = side_len // RADIX
    side_blocks = side_len // LANES
    lane = lax.broadcasted_iota(jnp.int32, (1, LANES), 1)
    line = lax.broadcasted_iota(jnp.int32, (GROUP, LANES), 0)

    def one_slot(slot, carry):
        row = shift_ref[0, slot]
        col = shift_ref[1, slot]
        lift = lax.rem(row, GROUP)
        turn = lax.rem(col, LANES)
        base = pl.multiple_of(row - lift, GROUP)
        block = lax.div(col, LANES)
        stay = lane >= turn
        below = line >= lift

        def table(side, kind, q):
            return side_by_side(tables[slot, side, kind, q, 0], tables[slot, side, kind, q, 1])

        def piece(c, b, at):
            def cut(b):
                start = pl.multiple_of(base + at, GROUP)
                value = field[c, block + b, pl.ds(start, GROUP), :]
                if at == 0:
                    start = pl.multiple_of(base + side_len, GROUP)
                    wrapped = field[c, block + b, pl.ds(start, GROUP), :]
                    value = jnp.where(below, value, wrapped)
                return value

            value = cut(b) if b else jnp.where(stay, cut(0), cut(side_blocks))
            return value.astype(jnp.float32)

        def exit_waves(blocks):
            for at in range(0, part, GROUP):
                for b in blocks:
                    waves = []
                    for p in range(RADIX):
                        here = at + p * part
                        re, im = piece(0, b, here), piece(1, b, here)
                        probe_re = probes[slot, 0, b, here : here + GROUP, :]
                        probe_im = probes[slot, 1, b, here : here + GROUP, :]
                        waves.append((probe_re * re - probe_im * im, probe_re * im + probe_im * re))
                    for q, (re, im) in enumerate(butterfly(waves, -1)):
                        mixed[q, b, at : at + GROUP, :] = re.astype(jnp.bfloat16)
                        mixed[q, b, at + part : at + part + GROUP, :] = im.astype(jnp.bfloat16)

        def split(value):
            return [
                (value[:part, at : at + part], value[part:, at : at + part])
                for at in range(0, value.shape[1], part)
            ]

        def left(q, blocks):
            return split(dot(table(0, 0, q), side_by_side(*(mixed[q, b] for b in blocks))))

        def far_field(other):
            return dot(side_by_side(halves[other, 0], halves[other, 1]), table(1, 1, other))

        def misfit_of(other, far):
            for q in range(RADIX):
                rows = slice(q * part, (q + 1) * part)
                far_re, far_im = far[rows, :part], far[rows, part:]
                seen = measured[slot, other, rows, :].astype(jnp.float32)
                misfit = far_re * far_re + far_im * far_im - seen
                misfits[q, other, :part, :] = (misfit * far_re).astype(jnp.bfloat16)
                misfits[q, other, part:, :] = (misfit * far_im).astype(jnp.bfloat16)

        def left_back(q, pair):
            mixture = dot(table(1, 0, q), side_by_side(*(misfits[q, other] for other in pair)))
            for i, other in enumerate(pair):
                spectra[q, other] = mixture[:, i * part : (i + 1) * part]

        def mix(ats, pair):
            for at in ats:
                for other in pair:
                    parts = [
                        (
                            spectra[q, other, at : at + GROUP, :],
                            spectra[q, other, part + at : part + at + GROUP, :],
                        )
                        for q in range(RADIX)
                    ]
                    for p, (re, im) in enumerate(butterfly(parts, 1)):
                        here = slice(at + p * part, at + p * part + GROUP)
                        backs[other, 0, here, :] = re.astype(jnp.bfloat16)
                        backs[other, 1, here, :] = im.astype(jnp.bfloat16)

        def add(c, b, at, value):
            where = pl.ds(pl.multiple_of(base + at, GROUP), value.shape[0])
            grown[c, block + b, where, :] += value

        def add_wrapped(c, b, at, value):
            if at == 0:
                add(c, b, 0, jnp.where(below, value[:GROUP], 0.0))
                add(c, b, side_len, jnp.where(below, 0.0, value[:GROUP]))
                add(c, b, GROUP, value[GROUP:])
            else:
                add(c, b, at, value)

        def right_back(at, tall):
            parts = []
            for other in range(RADIX):
                back = jnp.concatenate(
                    [
                        side_by_side(
                            backs[other, 0, here : here + tall, :],
                            backs[other, 1, here : here + tall, :],
                        )
                        for here in range(at, side_len, part)
                    ],
                    axis=0,
                )
                grad = dot(back, table(0, 1, other))
                parts.append((grad[:, :part], grad[:, part:]))
            return parts

        def accumulate(at, tall, parts):
            for p in range(RADIX):
                here = at + p * part
                rows = slice(p * tall, (p + 1) * tall)
                some = [(re[rows], im[rows]) for re, im in parts]
                for b, (re, im) in enumerate(butterfly(some, 1)):
                    probe_re = probes[slot, 0, b, here : here + tall, :]
                    probe_im = probes[slot, 1, b, here : here + tall, :]
                    values = (probe_re * re + probe_im * im, probe_re * im - probe_im * re)
                    for c, value in enumerate(values):
                        if b == 0:
                            add_wrapped(c, 0, here, jnp.where(stay, value, 0.0))
                            add_wrapped(c, side_blocks, here, jnp.where(stay, 0.0, value))
                        else:
                            add_wrapped(c, b, here, value)

        exit_waves((0, 2))
        early = [left(q, (0, 2)) for q in range(RADIX)]
        exit_waves((1, 3))
        for q in range(RADIX):
            rows = slice(q * part, (q + 1) * part)
            (r0, r2), (r1, r3) = early[q], left(q, (1, 3))
            for other, (re, im) in enumerate(butterfly([r0, r1, r2, r3], -1)):
                halves[other, 0, rows, :] = re.astype(jnp.bfloat16)
                halves[other, 1, rows, :] = im.astype(jnp.bfloat16)
        ahead = far_field(0)
        for other in range(RADIX):
            far = ahead
            if other + 1 < RADIX:
                ahead = far_field(other + 1)
            misfit_of(other, far)
            if other == 2:
                for q in range(RADIX):
                    left_back(q, (0, 1))
        tall = part // 2
        ats = [range(at, at + tall, GROUP) for at in range(0, part, tall)]
        for q in range(RADIX):
            left_back(q, (2, 3))
        mix(ats[0], (0, 1))
        mix(ats[0], (2, 3))
        first = right_back(0, tall)
        mix(ats[1], (0, 1))
        mix(ats[1], (2, 3))
        second = right_back(tall, tall)
        accumulate(0, tall, first)
        accumulate(tall, tall, second)
        return carry

    lax.fori_loop(0, live_ref[0, lax.axis_index("scan")], one_slot, 0)


def solve(live_counts, shifts, prepared, limit):
    grown = prepared[-1]
    side_len = prepared[1].shape[3]
    part = side_len // RADIX
    smem = pl.BlockSpec(memory_space=pltpu.SMEM)
    vmem = pl.BlockSpec(memory_space=pltpu.VMEM)
    wide = (RADIX, RADIX, 2 * part, part)
    tall = (RADIX, 2, side_len, part)
    scratch = [
        (wide, jnp.bfloat16),
        (tall, jnp.bfloat16),
        (wide, jnp.bfloat16),
        (wide, jnp.float32),
        (tall, jnp.bfloat16),
    ]
    return pl.pallas_call(
        solve_kernel,
        out_shape=pltpu.VMEM(grown.shape, grown.dtype),
        in_specs=[smem, smem] + [vmem] * len(prepared),
        out_specs=vmem,
        scratch_shapes=[pltpu.VMEM(*each) for each in scratch],
        input_output_aliases={1 + len(prepared): 0},
        compiler_params=pltpu.CompilerParams(vmem_limit_bytes=limit),
    )(live_counts, shifts, *prepared)


def shards(axes, object_slab, probe_field, intensities, offsets, live_count):
    tables = residue_tables(probe_field.shape[-1])
    shifts = offsets[0, 0].T
    prepared, limit = gather(axes, shifts, object_slab, intensities[0, 0], probe_field, tables)
    grown = solve(live_count.T, shifts, prepared, limit)
    return scatter(axes, grown, object_slab.shape[1])


def solution(mesh):
    placed = (
        P(None, "tile", "scan"),
        P(),
        P("scan", "tile", None, None, None),
        P("scan", "tile", None, None),
        P(None, "tile"),
    )
    axes = tuple((name, mesh.shape[name]) for name in ("scan", "tile"))
    return jax.shard_map(
        functools.partial(shards, axes), mesh=mesh, in_specs=placed, out_specs=P(None, "tile", "scan"), check_vma=False
    )
```

```python
import functools
import math

import jax
import jax.numpy as jnp
import numpy as np
from jax import lax
from jax.experimental import pallas as pl
from jax.experimental.pallas import tpu as pltpu
from jax.sharding import PartitionSpec as P

RADIX = 4
LANES = 128
GROUP = 16


def residue_tables(side_len):
    part = side_len // RADIX
    freq = np.arange(side_len).reshape(part, RADIX).T
    across = np.arange(part)
    phase = (freq[:, :, None] * across[None, None, :] % side_len) * (2.0 * math.pi / side_len)
    factor = 1.0 / math.sqrt(side_len)
    cos = np.cos(phase) * factor
    sin = np.sin(phase) * factor
    rows = np.concatenate(
        [np.concatenate([cos, sin], axis=2), np.concatenate([-sin, cos], axis=2)], axis=1
    ).astype(np.float32)
    return jnp.asarray(rows, jnp.bfloat16), jnp.asarray(rows.swapaxes(1, 2), jnp.bfloat16)


def sorted_by_residue(side_len):
    at = np.arange(side_len)
    source = at % (side_len // RADIX) * RADIX + at // (side_len // RADIX)
    sort = (source[:, None] == at[None, :]).astype(np.float32)
    return jnp.asarray(sort, jnp.bfloat16), jnp.asarray(sort.T, jnp.bfloat16)


def dot(a, b):
    return jnp.dot(a, b, preferred_element_type=jnp.float32)


def butterfly(parts, sign):
    (r0, i0), (r1, i1), (r2, i2), (r3, i3) = parts
    ar, ai, br, bi = r0 + r2, i0 + i2, r1 + r3, i1 + i3
    cr, ci, dr, di = r0 - r2, i0 - i2, r1 - r3, i1 - i3
    plus = (cr - di, ci + dr)
    minus = (cr + di, ci - dr)
    first, third = (plus, minus) if sign > 0 else (minus, plus)
    return [(ar + br, ai + bi), first, (ar - br, ai - bi), third]


def neighbours(axes):
    result = []
    for name, count in axes:
        me = lax.axis_index(name)
        result.append((me > 0, {name: me - 1}, me < count - 1, {name: me + 1}))
    return result


def greet(peers):
    barrier = pltpu.get_barrier_semaphore()
    for has_low, low, has_high, high in peers:
        for there, peer in ((has_low, low), (has_high, high)):

            @pl.when(there)
            def _(peer=peer):
                pl.semaphore_signal(
                    barrier, inc=1, device_id=peer, device_id_type=pl.DeviceIdType.MESH
                )


def all_here(peers):
    count = sum(
        there.astype(jnp.int32) for has_low, _, has_high, _ in peers for there in (has_low, has_high)
    )
    pl.semaphore_wait(pltpu.get_barrier_semaphore(), count)


def remote(source, target, sends, receives, index, peer):
    return pltpu.make_async_remote_copy(
        src_ref=source,
        dst_ref=target,
        send_sem=sends.at[index],
        recv_sem=receives.at[index],
        device_id=peer,
        device_id_type=pl.DeviceIdType.MESH,
    )


def quarter_turns(cos, sin, q):
    return ((cos, sin), (sin, -cos), (-cos, -sin), (-sin, cos))[q]


def in_place(mask, cos, sin, q):
    wrapped = quarter_turns(cos, sin, q)
    return jnp.where(mask, cos, wrapped[0]), jnp.where(mask, sin, wrapped[1])


def gather_kernel(
    axes,
    shift_ref,
    own_hbm,
    measured_hbm,
    probe_hbm,
    rows_hbm,
    cols_hbm,
    sort_hbm,
    unsort_hbm,
    field,
    probes,
    tables,
    arranged,
    grown,
    own,
    measured,
    extended,
    rows_ref,
    cols_ref,
    doubled,
    sort,
    unsort,
    sends,
    receives,
    fetches,
    freed,
):
    slots, side_len = measured.shape[:2]
    tile_len = own.shape[1]
    part = side_len // RADIX
    own_blocks = tile_len // LANES
    side_blocks = side_len // LANES
    scan, tile = neighbours(axes)
    has_left, left, has_right, _ = scan
    has_up, up, has_down, down = tile
    greet((scan, tile))
    first = pltpu.make_async_copy(
        own_hbm.at[:, :side_len, :side_len], own.at[:, :side_len, :side_len], fetches.at[0]
    )
    second = pltpu.make_async_copy(
        own_hbm.at[:, side_len:, :side_len], own.at[:, side_len:, :side_len], fetches.at[1]
    )
    third = pltpu.make_async_copy(
        own_hbm.at[:, :side_len, side_len:], own.at[:, :side_len, side_len:], fetches.at[2]
    )
    fourth = pltpu.make_async_copy(
        own_hbm.at[:, side_len:, side_len:], own.at[:, side_len:, side_len:], fetches.at[3]
    )
    constants = [
        pltpu.make_async_copy(source, target, fetches.at[4 + i])
        for i, (source, target) in enumerate(
            (
                (sort_hbm, sort),
                (unsort_hbm, unsort),
                (measured_hbm, measured),
                (rows_hbm, rows_ref),
                (cols_hbm, cols_ref),
            )
        )
    ]
    for c in range(2):
        for b in range(side_blocks):
            cols = slice(b * LANES, (b + 1) * LANES)
            for source, target in (
                (probe_hbm.at[c, :, cols], extended.at[c, b, GROUP:, :]),
                (probe_hbm.at[c, side_len - GROUP :, cols], extended.at[c, b, :GROUP, :]),
            ):
                constants.append(
                    pltpu.make_async_copy(source, target, fetches.at[4 + len(constants)])
                )
    for load in [first, second, third, fourth] + constants:
        load.start()
    near = slice(0, side_blocks)
    far = slice(own_blocks, own_blocks + side_blocks)
    halves = [
        (c, slice(at, at + side_blocks // 2))
        for c in range(2)
        for at in range(0, side_blocks, side_blocks // 2)
    ]

    def moved(blocks):
        return slice(blocks.start + own_blocks, blocks.stop + own_blocks)

    tops = [
        remote(
            field.at[c, blocks, :side_len, :],
            field.at[c, moved(blocks), :side_len, :],
            sends,
            receives,
            3 + i,
            left,
        )
        for i, (c, blocks) in enumerate(halves)
    ]
    rests = [
        remote(
            field.at[c, near, side_len:tile_len, :],
            field.at[c, far, side_len:tile_len, :],
            sends,
            receives,
            c,
            left,
        )
        for c in range(2)
    ]
    under = remote(
        field.at[:, :own_blocks, :side_len, :],
        field.at[:, :own_blocks, tile_len:, :],
        sends,
        receives,
        2,
        up,
    )
    acrosses = [
        remote(
            field.at[c, moved(blocks), :side_len, :],
            field.at[c, moved(blocks), tile_len:, :],
            sends,
            receives,
            3 + len(halves) + i,
            up,
        )
        for i, (c, blocks) in enumerate(halves)
    ]

    def narrow(blocks, at):
        for c in range(2):
            for b in blocks:
                field[c, b, at, :] = own[c, at, b * LANES : (b + 1) * LANES].astype(jnp.bfloat16)

    first.wait()
    narrow(range(side_blocks), slice(0, side_len))
    all_here((scan, tile))

    @pl.when(has_left)
    def _():
        for each in tops:
            each.start()

    second.wait()
    third.wait()
    narrow(range(side_blocks), slice(side_len, tile_len))
    narrow(range(side_blocks, own_blocks), slice(0, side_len))

    odd = lax.rem(lax.axis_index(axes[1][0]), 2) == 1
    first_turn = jnp.logical_and(has_left, jnp.logical_not(odd))
    second_turn = jnp.logical_and(has_left, odd)

    @pl.when(first_turn)
    def _():
        for each in rests:
            each.start()

    @pl.when(has_up)
    def _():
        under.start()

    @pl.when(jnp.logical_not(has_right))
    def _():
        field[:, far, :tile_len, :] = jnp.zeros(
            (2, side_blocks, tile_len, LANES), jnp.bfloat16
        )

    @pl.when(jnp.logical_not(has_down))
    def _():
        field[:, :, tile_len:, :] = jnp.zeros(
            (2, own_blocks + side_blocks, side_len, LANES), jnp.bfloat16
        )

    fourth.wait()
    narrow(range(side_blocks, own_blocks), slice(side_len, tile_len))
    for load in constants:
        load.wait()

    def sort_slot(slot, carry):
        rows = dot(sort[...], measured[slot]).astype(jnp.bfloat16)
        both = dot(rows, unsort[...]).astype(jnp.bfloat16)
        for b in range(RADIX):
            arranged[slot, b] = both[:, b * part : (b + 1) * part]
        return carry

    lax.fori_loop(0, slots, sort_slot, 0)

    grown[...] = jnp.zeros_like(grown)
    for q in range(RADIX):
        for i in range(2):
            for at in (0, part):
                doubled[q, i, at : at + part, :] = cols_ref[
                    q, i * part : (i + 1) * part, :part
                ].astype(jnp.float32)

    lane = lax.broadcasted_iota(jnp.int32, (1, LANES), 1)
    line = lax.broadcasted_iota(jnp.int32, (part, LANES), 0)
    chunk = 32

    def prepare(slot, carry):
        lift = lax.rem(shift_ref[0, slot], GROUP)
        turn = lax.rem(shift_ref[1, slot], LANES)

        def move_probe(i, carry):
            at = pl.multiple_of(i * chunk, chunk)
            for c in range(2):
                turned = [
                    pltpu.roll(extended[c, b, pl.ds(GROUP - lift + at, chunk), :], turn, 1)
                    for b in range(side_blocks)
                ]
                for b in range(side_blocks):
                    probes[slot, c, b, pl.ds(at, chunk), :] = jnp.where(
                        lane >= turn, turned[b], turned[b - 1]
                    )
            return carry

        lax.fori_loop(0, side_len // chunk, move_probe, 0)
        for k, by in enumerate((lift, turn)):
            for q in range(RADIX):
                cos = pltpu.roll(rows_ref[q, :part, :part].astype(jnp.float32), by, 1)
                sin = pltpu.roll(rows_ref[q, :part, part:].astype(jnp.float32), by, 1)
                cos, sin = in_place(lane >= by, cos, sin, q)
                tables[slot, 0, k, q, 0, :part, :] = cos.astype(jnp.bfloat16)
                tables[slot, 0, k, q, 1, :part, :] = sin.astype(jnp.bfloat16)
                tables[slot, 0, k, q, 0, part:, :] = (-sin).astype(jnp.bfloat16)
                tables[slot, 0, k, q, 1, part:, :] = cos.astype(jnp.bfloat16)
                cos = doubled[q, 0, pl.ds(part - by, part), :]
                sin = doubled[q, 1, pl.ds(part - by, part), :]
                cos, sin = in_place(line >= by, cos, sin, q)
                tables[slot, 1, k, q, 0, :part, :] = cos.astype(jnp.bfloat16)
                tables[slot, 1, k, q, 1, :part, :] = (-sin).astype(jnp.bfloat16)
                tables[slot, 1, k, q, 0, part:, :] = sin.astype(jnp.bfloat16)
                tables[slot, 1, k, q, 1, part:, :] = cos.astype(jnp.bfloat16)
        return carry

    lax.fori_loop(0, slots, prepare, 0)

    for top, across in zip(tops, acrosses):

        @pl.when(has_right)
        def _(top=top):
            top.wait_recv()

        @pl.when(has_up)
        def _(across=across):
            across.start()

    @pl.when(first_turn)
    def _():
        for each in tops + rests:
            each.wait_send()

    @pl.when(jnp.logical_and(first_turn, has_down))
    def _():
        pl.semaphore_signal(
            freed, inc=1, device_id=down, device_id_type=pl.DeviceIdType.MESH
        )

    @pl.when(second_turn)
    def _():
        pl.semaphore_wait(freed, 1)
        for each in rests:
            each.start()


    @pl.when(has_down)
    def _():
        under.wait_recv()

    @pl.when(has_right)
    def _():
        for each in rests:
            each.wait_recv()

    @pl.when(has_down)
    def _():
        for each in acrosses:
            each.wait_recv()

    @pl.when(second_turn)
    def _():
        for each in tops + rests:
            each.wait_send()

    @pl.when(has_up)
    def _():
        under.wait_send()
        for each in acrosses:
            each.wait_send()


def gather(axes, shifts, own, measured, probe, tables):
    slots, side_len = measured.shape[:2]
    tile_len = own.shape[1]
    span = tile_len + side_len
    part = side_len // RADIX
    side_blocks = side_len // LANES
    hbm = pl.BlockSpec(memory_space=pltpu.HBM)
    vmem = pl.BlockSpec(memory_space=pltpu.VMEM)
    table = (slots, 2, 2, RADIX, 2, 2 * part, part)
    scratch = [
        (own.shape, jnp.float32),
        (measured.shape, jnp.bfloat16),
        ((2, side_blocks, side_len + GROUP, LANES), jnp.float32),
        (tables[0].shape, jnp.bfloat16),
        (tables[1].shape, jnp.bfloat16),
        ((RADIX, 2, 2 * part, part), jnp.float32),
        ((side_len, side_len), jnp.bfloat16),
        ((side_len, side_len), jnp.bfloat16),
    ]
    call = pl.pallas_call(
        functools.partial(gather_kernel, axes),
        out_shape=[
            pltpu.VMEM((2, span // LANES, span, LANES), jnp.bfloat16),
            pltpu.VMEM((slots, 2, side_blocks, side_len, LANES), jnp.float32),
            pltpu.VMEM(table, jnp.bfloat16),
            pltpu.VMEM((slots, RADIX, side_len, part), jnp.bfloat16),
            pltpu.VMEM((2, span // LANES, span, LANES), jnp.float32),
        ],
        in_specs=[pl.BlockSpec(memory_space=pltpu.SMEM)] + [hbm] * 7,
        out_specs=[vmem] * 5,
        scratch_shapes=[pltpu.VMEM(*each) for each in scratch]
        + [
            pltpu.SemaphoreType.DMA((3 + 8,)),
            pltpu.SemaphoreType.DMA((3 + 8,)),
            pltpu.SemaphoreType.DMA((9 + 4 * side_blocks,)),
            pltpu.SemaphoreType.REGULAR,
        ],
        compiler_params=pltpu.CompilerParams(
            collective_id=0, has_side_effects=True, vmem_limit_bytes=room(scratch)
        ),
    )
    prepared = call(shifts, own, measured, probe, *tables, *sorted_by_residue(side_len))
    held = [pltpu.with_memory_space_constraint(each, pltpu.VMEM) for each in prepared]
    return held, room(scratch)


def room(scratch):
    return sum(math.prod(shape) * jnp.dtype(kind).itemsize for shape, kind in scratch) + (1 << 20)


def scatter_kernel(
    axes,
    grown,
    total,
    from_left,
    spill,
    dropped,
    both,
    landed,
    from_up,
    sends,
    receives,
    ready,
):
    side_len = landed.shape[2]
    tile_len = total.shape[1]
    own_blocks = tile_len // LANES
    side_blocks = side_len // LANES
    scan, tile = neighbours(axes)
    has_left, left, has_right, right = scan
    has_up, up, has_down, down = tile
    odd = lax.rem(lax.axis_index(axes[1][0]), 2) == 1
    even = jnp.logical_not(odd)
    barrier = pltpu.get_barrier_semaphore()

    def tell(there, sem, peer):
        @pl.when(there)
        def _():
            pl.semaphore_signal(
                sem, inc=1, device_id=peer, device_id_type=pl.DeviceIdType.MESH
            )

    tell(has_left, barrier, left)
    tell(jnp.logical_and(even, has_up), barrier, up)
    tell(jnp.logical_and(even, has_down), barrier, down)
    corner = remote(both, landed, sends, receives, 0, down)
    under = remote(dropped, from_up, sends, receives, 1, down)
    rest = remote(
        spill.at[:, :, side_len:, :], from_left.at[:, :, side_len:, :], sends, receives, 2, right
    )
    top = remote(
        spill.at[:, :, :side_len, :], from_left.at[:, :, :side_len, :], sends, receives, 3, right
    )
    spill[:, :, side_len:, :] = grown[:, own_blocks:, side_len:tile_len, :].astype(jnp.bfloat16)
    both[...] = grown[:, own_blocks:, tile_len:, :].astype(jnp.bfloat16)
    from_even = has_up.astype(jnp.int32) + has_down.astype(jnp.int32)
    awaited = has_right.astype(jnp.int32) + jnp.where(odd, from_even, 0)

    @pl.when(awaited > 0)
    def _():
        pl.semaphore_wait(barrier, awaited)

    @pl.when(has_right)
    def _():
        rest.start()

    tell(odd, ready, up)

    @pl.when(jnp.logical_and(odd, has_down))
    def _():
        corner.start()

    @pl.when(jnp.logical_not(has_up))
    def _():
        spill[:, :, :side_len, :] = grown[:, own_blocks:, :side_len, :].astype(jnp.bfloat16)

    @pl.when(jnp.logical_and(jnp.logical_not(has_up), has_right))
    def _():
        top.start()

    dropped[...] = grown[:, :own_blocks, tile_len:, :].astype(jnp.bfloat16)

    @pl.when(jnp.logical_and(odd, has_down))
    def _():
        under.start()

    for c in range(2):
        for b in range(own_blocks):
            total[c, :, b * LANES : (b + 1) * LANES] = grown[c, b, :tile_len, :]

    @pl.when(jnp.logical_and(even, has_down))
    def _():
        pl.semaphore_wait(ready, 1)
        corner.start()
        under.start()

    @pl.when(has_up)
    def _():
        corner.wait_recv()
        spill[:, :, :side_len, :] = (
            grown[:, own_blocks:, :side_len, :] + landed[...].astype(jnp.float32)
        ).astype(jnp.bfloat16)

    @pl.when(jnp.logical_and(has_up, has_right))
    def _():
        top.start()

    def add(blocks, at, source):
        for c in range(2):
            for b in blocks:
                total[c, at, b * LANES : (b + 1) * LANES] += source[c, b, at, :].astype(jnp.float32)

    @pl.when(has_left)
    def _():
        rest.wait_recv()
        add(range(side_blocks), slice(side_len, tile_len), from_left)

    @pl.when(has_up)
    def _():
        under.wait_recv()
        add(range(own_blocks), slice(0, side_len), from_up)

    @pl.when(has_left)
    def _():
        top.wait_recv()

    @pl.when(jnp.logical_not(has_left))
    def _():
        from_left[:, :, :side_len, :] = jnp.zeros(
            (2, side_blocks, side_len, LANES), jnp.bfloat16
        )

    @pl.when(has_right)
    def _():
        rest.wait_send()
        top.wait_send()

    @pl.when(has_down)
    def _():
        corner.wait_send()
        under.wait_send()


def scatter(axes, grown, tile_len):
    span = grown.shape[2]
    side_len = span - tile_len
    own_blocks = tile_len // LANES
    side_blocks = side_len // LANES
    vmem = pl.BlockSpec(memory_space=pltpu.VMEM)
    scratch = [
        ((2, side_blocks, tile_len, LANES), jnp.bfloat16),
        ((2, own_blocks, side_len, LANES), jnp.bfloat16),
        ((2, side_blocks, side_len, LANES), jnp.bfloat16),
        ((2, side_blocks, side_len, LANES), jnp.bfloat16),
        ((2, own_blocks, side_len, LANES), jnp.bfloat16),
    ]
    summed = pl.pallas_call(
        functools.partial(scatter_kernel, axes),
        out_shape=[
            pltpu.VMEM((2, tile_len, tile_len), jnp.float32),
            pltpu.VMEM((2, side_blocks, tile_len, LANES), jnp.bfloat16),
        ],
        in_specs=[vmem],
        out_specs=[vmem] * 2,
        scratch_shapes=[pltpu.VMEM(*each) for each in scratch]
        + [
            pltpu.SemaphoreType.DMA((4,)),
            pltpu.SemaphoreType.DMA((4,)),
            pltpu.SemaphoreType.REGULAR,
        ],
        compiler_params=pltpu.CompilerParams(
            collective_id=1, has_side_effects=True, vmem_limit_bytes=room(scratch)
        ),
    )(grown)
    held = [pltpu.with_memory_space_constraint(each, pltpu.VMEM) for each in summed]
    return pl.pallas_call(
        finish_kernel,
        out_shape=jax.ShapeDtypeStruct((2, tile_len, tile_len), jnp.float32),
        in_specs=[vmem] * 2,
        out_specs=pl.BlockSpec(memory_space=pltpu.HBM),
        scratch_shapes=[
            pltpu.VMEM((2, side_len, side_len), jnp.float32),
            pltpu.SemaphoreType.DMA((2, 3)),
        ],
        compiler_params=pltpu.CompilerParams(vmem_limit_bytes=room(scratch)),
    )(*held)


def finish_kernel(total, from_left, out_hbm, head, puts):
    side_len = head.shape[1]
    copies = []
    for c in range(2):
        for i, at in enumerate(
            (
                (c, slice(side_len, None), slice(None)),
                (c, slice(0, side_len), slice(side_len, None)),
            )
        ):
            copies.append(pltpu.make_async_copy(total.at[at], out_hbm.at[at], puts.at[c, i]))
    for copy in copies:
        copy.start()
    for c in range(2):
        for b in range(side_len // LANES):
            cols = slice(b * LANES, (b + 1) * LANES)
            head[c, :, cols] = total[c, :side_len, cols] + from_left[c, b, :side_len, :].astype(
                jnp.float32
            )
        at = (c, slice(0, side_len), slice(0, side_len))
        copies.append(pltpu.make_async_copy(head.at[c], out_hbm.at[at], puts.at[c, 2]))
        copies[-1].start()
    for copy in copies:
        copy.wait()


def side_by_side(*blocks):
    return jnp.concatenate(blocks, axis=1)


def solve_kernel(
    live_ref,
    shift_ref,
    field,
    probes,
    tables,
    measured,
    zeros,
    grown,
    mixed,
    halves,
    misfits,
    spectra,
    backs,
):
    side_len = probes.shape[3]
    part = side_len // RADIX
    side_blocks = side_len // LANES
    lane = lax.broadcasted_iota(jnp.int32, (1, LANES), 1)
    line = lax.broadcasted_iota(jnp.int32, (GROUP, LANES), 0)

    def one_slot(slot, carry):
        row = shift_ref[0, slot]
        col = shift_ref[1, slot]
        lift = lax.rem(row, GROUP)
        turn = lax.rem(col, LANES)
        base = pl.multiple_of(row - lift, GROUP)
        block = lax.div(col, LANES)
        stay = lane >= turn
        below = line >= lift

        def table(side, kind, q):
            return side_by_side(tables[slot, side, kind, q, 0], tables[slot, side, kind, q, 1])

        def piece(c, b, at):
            def cut(b):
                start = pl.multiple_of(base + at, GROUP)
                value = field[c, block + b, pl.ds(start, GROUP), :]
                if at == 0:
                    start = pl.multiple_of(base + side_len, GROUP)
                    wrapped = field[c, block + b, pl.ds(start, GROUP), :]
                    value = jnp.where(below, value, wrapped)
                return value

            value = cut(b) if b else jnp.where(stay, cut(0), cut(side_blocks))
            return value.astype(jnp.float32)

        def exit_waves(blocks):
            for at in range(0, part, GROUP):
                for b in blocks:
                    waves = []
                    for p in range(RADIX):
                        here = at + p * part
                        re, im = piece(0, b, here), piece(1, b, here)
                        probe_re = probes[slot, 0, b, here : here + GROUP, :]
                        probe_im = probes[slot, 1, b, here : here + GROUP, :]
                        waves.append((probe_re * re - probe_im * im, probe_re * im + probe_im * re))
                    for q, (re, im) in enumerate(butterfly(waves, -1)):
                        mixed[q, b, at : at + GROUP, :] = re.astype(jnp.bfloat16)
                        mixed[q, b, at + part : at + part + GROUP, :] = im.astype(jnp.bfloat16)

        def split(value):
            return [
                (value[:part, at : at + part], value[part:, at : at + part])
                for at in range(0, value.shape[1], part)
            ]

        def left(q, blocks):
            return split(dot(table(0, 0, q), side_by_side(*(mixed[q, b] for b in blocks))))

        def far_field(other):
            return dot(side_by_side(halves[other, 0], halves[other, 1]), table(1, 1, other))

        def misfit_of(other, far):
            for q in range(RADIX):
                rows = slice(q * part, (q + 1) * part)
                far_re, far_im = far[rows, :part], far[rows, part:]
                seen = measured[slot, other, rows, :].astype(jnp.float32)
                misfit = far_re * far_re + far_im * far_im - seen
                misfits[q, other, :part, :] = (misfit * far_re).astype(jnp.bfloat16)
                misfits[q, other, part:, :] = (misfit * far_im).astype(jnp.bfloat16)

        def left_back(q, pair):
            mixture = dot(table(1, 0, q), side_by_side(*(misfits[q, other] for other in pair)))
            for i, other in enumerate(pair):
                spectra[q, other] = mixture[:, i * part : (i + 1) * part]

        def mix(ats, pair):
            for at in ats:
                for other in pair:
                    parts = [
                        (
                            spectra[q, other, at : at + GROUP, :],
                            spectra[q, other, part + at : part + at + GROUP, :],
                        )
                        for q in range(RADIX)
                    ]
                    for p, (re, im) in enumerate(butterfly(parts, 1)):
                        here = slice(at + p * part, at + p * part + GROUP)
                        backs[other, 0, here, :] = re.astype(jnp.bfloat16)
                        backs[other, 1, here, :] = im.astype(jnp.bfloat16)

        def add(c, b, at, value, mask=None):
            where = pl.ds(pl.multiple_of(base + at, GROUP), value.shape[0])
            if mask is None:
                grown[c, block + b, where, :] += value
            else:
                spot = grown.at[c, block + b, where, :]
                mask = jnp.broadcast_to(mask, value.shape)
                pltpu.store(spot, spot[...] + value, mask=mask)

        def add_wrapped(c, b, at, value, mask=None):
            if at == 0:
                add(c, b, 0, jnp.where(below, value[:GROUP], 0.0), mask)
                add(c, b, side_len, jnp.where(below, 0.0, value[:GROUP]), mask)
                add(c, b, GROUP, value[GROUP:], mask)
            else:
                add(c, b, at, value, mask)

        def right_back(at, tall):
            parts = []
            for other in range(RADIX):
                back = jnp.concatenate(
                    [
                        side_by_side(
                            backs[other, 0, here : here + tall, :],
                            backs[other, 1, here : here + tall, :],
                        )
                        for here in range(at, side_len, part)
                    ],
                    axis=0,
                )
                grad = dot(back, table(0, 1, other))
                parts.append((grad[:, :part], grad[:, part:]))
            return parts

        def accumulate(at, tall, parts):
            for p in range(RADIX):
                here = at + p * part
                rows = slice(p * tall, (p + 1) * tall)
                some = [(re[rows], im[rows]) for re, im in parts]
                for b, (re, im) in enumerate(butterfly(some, 1)):
                    probe_re = probes[slot, 0, b, here : here + tall, :]
                    probe_im = probes[slot, 1, b, here : here + tall, :]
                    values = (probe_re * re + probe_im * im, probe_re * im - probe_im * re)
                    for c, value in enumerate(values):
                        if b == 0:
                            add_wrapped(c, 0, here, value, stay)
                            add_wrapped(c, side_blocks, here, value, jnp.logical_not(stay))
                        else:
                            add_wrapped(c, b, here, value)

        exit_waves((0, 2))
        early = [left(q, (0, 2)) for q in range(RADIX)]
        exit_waves((1, 3))
        for q in range(RADIX):
            rows = slice(q * part, (q + 1) * part)
            (r0, r2), (r1, r3) = early[q], left(q, (1, 3))
            for other, (re, im) in enumerate(butterfly([r0, r1, r2, r3], -1)):
                halves[other, 0, rows, :] = re.astype(jnp.bfloat16)
                halves[other, 1, rows, :] = im.astype(jnp.bfloat16)
        ahead = far_field(0)
        for other in range(RADIX):
            far = ahead
            if other + 1 < RADIX:
                ahead = far_field(other + 1)
            misfit_of(other, far)
            if other == 2:
                for q in range(RADIX):
                    left_back(q, (0, 1))
        tall = part // 2
        ats = [range(at, at + tall, GROUP) for at in range(0, part, tall)]
        for q in range(RADIX):
            left_back(q, (2, 3))
        mix(ats[0], range(RADIX))
        mix(ats[1], range(RADIX))
        first = right_back(0, tall)
        second = right_back(tall, tall)
        accumulate(0, tall, first)
        accumulate(tall, tall, second)
        return carry

    lax.fori_loop(0, live_ref[0, lax.axis_index("scan")], one_slot, 0)


def solve(live_counts, shifts, prepared, limit):
    grown = prepared[-1]
    side_len = prepared[1].shape[3]
    part = side_len // RADIX
    smem = pl.BlockSpec(memory_space=pltpu.SMEM)
    vmem = pl.BlockSpec(memory_space=pltpu.VMEM)
    wide = (RADIX, RADIX, 2 * part, part)
    tall = (RADIX, 2, side_len, part)
    scratch = [
        (wide, jnp.bfloat16),
        (tall, jnp.bfloat16),
        (wide, jnp.bfloat16),
        (wide, jnp.float32),
        (tall, jnp.bfloat16),
    ]
    return pl.pallas_call(
        solve_kernel,
        out_shape=pltpu.VMEM(grown.shape, grown.dtype),
        in_specs=[smem, smem] + [vmem] * len(prepared),
        out_specs=vmem,
        scratch_shapes=[pltpu.VMEM(*each) for each in scratch],
        input_output_aliases={1 + len(prepared): 0},
        compiler_params=pltpu.CompilerParams(vmem_limit_bytes=limit),
    )(live_counts, shifts, *prepared)


def shards(axes, object_slab, probe_field, intensities, offsets, live_count):
    tables = residue_tables(probe_field.shape[-1])
    shifts = offsets[0, 0].T
    prepared, limit = gather(axes, shifts, object_slab, intensities[0, 0], probe_field, tables)
    grown = solve(live_count.T, shifts, prepared, limit)
    return scatter(axes, grown, object_slab.shape[1])


def solution(mesh):
    placed = (
        P(None, "tile", "scan"),
        P(),
        P("scan", "tile", None, None, None),
        P("scan", "tile", None, None),
        P(None, "tile"),
    )
    axes = tuple((name, mesh.shape[name]) for name in ("scan", "tile"))
    return jax.shard_map(
        functools.partial(shards, axes), mesh=mesh, in_specs=placed, out_specs=P(None, "tile", "scan"), check_vma=False
    )
```

```python
import functools
import math

import jax
import jax.numpy as jnp
import numpy as np
from jax import lax
from jax.experimental import pallas as pl
from jax.experimental.pallas import tpu as pltpu
from jax.sharding import PartitionSpec as P

RADIX = 4
LANES = 128
GROUP = 16


def residue_tables(side_len):
    part = side_len // RADIX
    freq = np.arange(side_len).reshape(part, RADIX).T
    across = np.arange(part)
    phase = (freq[:, :, None] * across[None, None, :] % side_len) * (2.0 * math.pi / side_len)
    factor = 1.0 / math.sqrt(side_len)
    cos = np.cos(phase) * factor
    sin = np.sin(phase) * factor
    rows = np.concatenate(
        [np.concatenate([cos, sin], axis=2), np.concatenate([-sin, cos], axis=2)], axis=1
    ).astype(np.float32)
    return jnp.asarray(rows, jnp.bfloat16), jnp.asarray(rows.swapaxes(1, 2), jnp.bfloat16)


def sorted_by_residue(side_len):
    at = np.arange(side_len)
    source = at % (side_len // RADIX) * RADIX + at // (side_len // RADIX)
    sort = (source[:, None] == at[None, :]).astype(np.float32)
    return jnp.asarray(sort, jnp.bfloat16), jnp.asarray(sort.T, jnp.bfloat16)


def dot(a, b):
    return jnp.dot(a, b, preferred_element_type=jnp.float32)


def butterfly(parts, sign):
    (r0, i0), (r1, i1), (r2, i2), (r3, i3) = parts
    ar, ai, br, bi = r0 + r2, i0 + i2, r1 + r3, i1 + i3
    cr, ci, dr, di = r0 - r2, i0 - i2, r1 - r3, i1 - i3
    plus = (cr - di, ci + dr)
    minus = (cr + di, ci - dr)
    first, third = (plus, minus) if sign > 0 else (minus, plus)
    return [(ar + br, ai + bi), first, (ar - br, ai - bi), third]


def neighbours(axes):
    result = []
    for name, count in axes:
        me = lax.axis_index(name)
        result.append((me > 0, {name: me - 1}, me < count - 1, {name: me + 1}))
    return result


def greet(peers):
    barrier = pltpu.get_barrier_semaphore()
    for has_low, low, has_high, high in peers:
        for there, peer in ((has_low, low), (has_high, high)):

            @pl.when(there)
            def _(peer=peer):
                pl.semaphore_signal(
                    barrier, inc=1, device_id=peer, device_id_type=pl.DeviceIdType.MESH
                )


def all_here(peers):
    count = sum(
        there.astype(jnp.int32) for has_low, _, has_high, _ in peers for there in (has_low, has_high)
    )
    pl.semaphore_wait(pltpu.get_barrier_semaphore(), count)


def remote(source, target, sends, receives, index, peer):
    return pltpu.make_async_remote_copy(
        src_ref=source,
        dst_ref=target,
        send_sem=sends.at[index],
        recv_sem=receives.at[index],
        device_id=peer,
        device_id_type=pl.DeviceIdType.MESH,
    )


def quarter_turns(cos, sin, q):
    return ((cos, sin), (sin, -cos), (-cos, -sin), (-sin, cos))[q]


def in_place(mask, cos, sin, q):
    wrapped = quarter_turns(cos, sin, q)
    return jnp.where(mask, cos, wrapped[0]), jnp.where(mask, sin, wrapped[1])


def gather_kernel(
    axes,
    shift_ref,
    own_hbm,
    measured_hbm,
    probe_hbm,
    rows_hbm,
    cols_hbm,
    sort_hbm,
    unsort_hbm,
    field,
    probes,
    tables,
    arranged,
    grown,
    own,
    measured,
    extended,
    rows_ref,
    cols_ref,
    doubled,
    sort,
    unsort,
    sends,
    receives,
    fetches,
    freed,
):
    slots, side_len = measured.shape[:2]
    tile_len = own.shape[1]
    part = side_len // RADIX
    own_blocks = tile_len // LANES
    side_blocks = side_len // LANES
    scan, tile = neighbours(axes)
    has_left, left, has_right, _ = scan
    has_up, up, has_down, down = tile
    greet((scan, tile))
    firsts = [
        pltpu.make_async_copy(
            own_hbm.at[c, :side_len, :side_len],
            own.at[c, :side_len, :side_len],
            fetches.at[4 * c],
        )
        for c in range(2)
    ]
    second = pltpu.make_async_copy(
        own_hbm.at[:, side_len:, :side_len], own.at[:, side_len:, :side_len], fetches.at[1]
    )
    third = pltpu.make_async_copy(
        own_hbm.at[:, :side_len, side_len:], own.at[:, :side_len, side_len:], fetches.at[2]
    )
    fourth = pltpu.make_async_copy(
        own_hbm.at[:, side_len:, side_len:], own.at[:, side_len:, side_len:], fetches.at[3]
    )
    constants = [
        pltpu.make_async_copy(source, target, fetches.at[5 + i])
        for i, (source, target) in enumerate(
            (
                (sort_hbm, sort),
                (unsort_hbm, unsort),
                (measured_hbm, measured),
                (rows_hbm, rows_ref),
                (cols_hbm, cols_ref),
            )
        )
    ]
    for c in range(2):
        for b in range(side_blocks):
            cols = slice(b * LANES, (b + 1) * LANES)
            for source, target in (
                (probe_hbm.at[c, :, cols], extended.at[c, b, GROUP:, :]),
                (probe_hbm.at[c, side_len - GROUP :, cols], extended.at[c, b, :GROUP, :]),
            ):
                constants.append(
                    pltpu.make_async_copy(source, target, fetches.at[5 + len(constants)])
                )
    for load in firsts + [third, second, fourth] + constants:
        load.start()
    near = slice(0, side_blocks)
    far = slice(own_blocks, own_blocks + side_blocks)
    halves = [
        (c, slice(at, at + side_blocks // 2))
        for c in range(2)
        for at in range(0, side_blocks, side_blocks // 2)
    ]

    def moved(blocks):
        return slice(blocks.start + own_blocks, blocks.stop + own_blocks)

    tops = [
        remote(
            field.at[c, blocks, :side_len, :],
            field.at[c, moved(blocks), :side_len, :],
            sends,
            receives,
            3 + i,
            left,
        )
        for i, (c, blocks) in enumerate(halves)
    ]
    rests = [
        remote(
            field.at[c, near, side_len:tile_len, :],
            field.at[c, far, side_len:tile_len, :],
            sends,
            receives,
            c,
            left,
        )
        for c in range(2)
    ]
    unders = [
        remote(
            field.at[:, blocks, :side_len, :],
            field.at[:, blocks, tile_len:, :],
            sends,
            receives,
            index,
            up,
        )
        for blocks, index in (
            (near, 2),
            (slice(side_blocks, own_blocks), 3 + 2 * len(halves)),
        )
    ]
    acrosses = [
        remote(
            field.at[c, moved(blocks), :side_len, :],
            field.at[c, moved(blocks), tile_len:, :],
            sends,
            receives,
            3 + len(halves) + i,
            up,
        )
        for i, (c, blocks) in enumerate(halves)
    ]

    def narrow(blocks, at, planes=range(2)):
        for c in planes:
            for b in blocks:
                field[c, b, at, :] = own[c, at, b * LANES : (b + 1) * LANES].astype(jnp.bfloat16)

    firsts[0].wait()
    narrow(range(side_blocks), slice(0, side_len), range(1))
    all_here((scan, tile))

    @pl.when(has_left)
    def _():
        for each in tops[:2]:
            each.start()

    firsts[1].wait()
    narrow(range(side_blocks), slice(0, side_len), range(1, 2))

    @pl.when(has_left)
    def _():
        for each in tops[2:]:
            each.start()

    @pl.when(has_up)
    def _():
        unders[0].start()

    third.wait()
    narrow(range(side_blocks, own_blocks), slice(0, side_len))

    @pl.when(has_up)
    def _():
        unders[1].start()

    second.wait()
    narrow(range(side_blocks), slice(side_len, tile_len))

    odd = lax.rem(lax.axis_index(axes[1][0]), 2) == 1
    first_turn = jnp.logical_and(has_left, jnp.logical_not(odd))
    second_turn = jnp.logical_and(has_left, odd)

    @pl.when(first_turn)
    def _():
        for each in rests:
            each.start()

    @pl.when(jnp.logical_not(has_right))
    def _():
        field[:, far, :tile_len, :] = jnp.zeros(
            (2, side_blocks, tile_len, LANES), jnp.bfloat16
        )

    @pl.when(jnp.logical_not(has_down))
    def _():
        field[:, :, tile_len:, :] = jnp.zeros(
            (2, own_blocks + side_blocks, side_len, LANES), jnp.bfloat16
        )

    fourth.wait()
    narrow(range(side_blocks, own_blocks), slice(side_len, tile_len))
    for load in constants:
        load.wait()

    def sort_slot(slot, carry):
        rows = dot(sort[...], measured[slot]).astype(jnp.bfloat16)
        both = dot(rows, unsort[...]).astype(jnp.bfloat16)
        for b in range(RADIX):
            arranged[slot, b] = both[:, b * part : (b + 1) * part]
        return carry

    lax.fori_loop(0, slots, sort_slot, 0)

    grown[...] = jnp.zeros_like(grown)
    for q in range(RADIX):
        for i in range(2):
            for at in (0, part):
                doubled[q, i, at : at + part, :] = cols_ref[
                    q, i * part : (i + 1) * part, :part
                ].astype(jnp.float32)

    lane = lax.broadcasted_iota(jnp.int32, (1, LANES), 1)
    line = lax.broadcasted_iota(jnp.int32, (part, LANES), 0)
    chunk = 32

    def prepare(slot, carry):
        lift = lax.rem(shift_ref[0, slot], GROUP)
        turn = lax.rem(shift_ref[1, slot], LANES)

        def move_probe(i, carry):
            at = pl.multiple_of(i * chunk, chunk)
            for c in range(2):
                turned = [
                    pltpu.roll(extended[c, b, pl.ds(GROUP - lift + at, chunk), :], turn, 1)
                    for b in range(side_blocks)
                ]
                for b in range(side_blocks):
                    probes[slot, c, b, pl.ds(at, chunk), :] = jnp.where(
                        lane >= turn, turned[b], turned[b - 1]
                    )
            return carry

        lax.fori_loop(0, side_len // chunk, move_probe, 0)
        for k, by in enumerate((lift, turn)):
            for q in range(RADIX):
                cos = pltpu.roll(rows_ref[q, :part, :part].astype(jnp.float32), by, 1)
                sin = pltpu.roll(rows_ref[q, :part, part:].astype(jnp.float32), by, 1)
                cos, sin = in_place(lane >= by, cos, sin, q)
                tables[slot, 0, k, q, 0, :part, :] = cos.astype(jnp.bfloat16)
                tables[slot, 0, k, q, 1, :part, :] = sin.astype(jnp.bfloat16)
                tables[slot, 0, k, q, 0, part:, :] = (-sin).astype(jnp.bfloat16)
                tables[slot, 0, k, q, 1, part:, :] = cos.astype(jnp.bfloat16)
                cos = doubled[q, 0, pl.ds(part - by, part), :]
                sin = doubled[q, 1, pl.ds(part - by, part), :]
                cos, sin = in_place(line >= by, cos, sin, q)
                tables[slot, 1, k, q, 0, :part, :] = cos.astype(jnp.bfloat16)
                tables[slot, 1, k, q, 1, :part, :] = (-sin).astype(jnp.bfloat16)
                tables[slot, 1, k, q, 0, part:, :] = sin.astype(jnp.bfloat16)
                tables[slot, 1, k, q, 1, part:, :] = cos.astype(jnp.bfloat16)
        return carry

    lax.fori_loop(0, slots, prepare, 0)

    for top, across in zip(tops, acrosses):

        @pl.when(has_right)
        def _(top=top):
            top.wait_recv()

        @pl.when(has_up)
        def _(across=across):
            across.start()

    @pl.when(first_turn)
    def _():
        for each in tops + rests:
            each.wait_send()

    @pl.when(jnp.logical_and(first_turn, has_down))
    def _():
        pl.semaphore_signal(
            freed, inc=1, device_id=down, device_id_type=pl.DeviceIdType.MESH
        )

    @pl.when(second_turn)
    def _():
        pl.semaphore_wait(freed, 1)
        for each in rests:
            each.start()


    @pl.when(has_down)
    def _():
        for each in unders:
            each.wait_recv()

    @pl.when(has_right)
    def _():
        for each in rests:
            each.wait_recv()

    @pl.when(has_down)
    def _():
        for each in acrosses:
            each.wait_recv()

    @pl.when(second_turn)
    def _():
        for each in tops + rests:
            each.wait_send()

    @pl.when(has_up)
    def _():
        for each in unders:
            each.wait_send()
        for each in acrosses:
            each.wait_send()


def gather(axes, shifts, own, measured, probe, tables):
    slots, side_len = measured.shape[:2]
    tile_len = own.shape[1]
    span = tile_len + side_len
    part = side_len // RADIX
    side_blocks = side_len // LANES
    hbm = pl.BlockSpec(memory_space=pltpu.HBM)
    vmem = pl.BlockSpec(memory_space=pltpu.VMEM)
    table = (slots, 2, 2, RADIX, 2, 2 * part, part)
    scratch = [
        (own.shape, jnp.float32),
        (measured.shape, jnp.bfloat16),
        ((2, side_blocks, side_len + GROUP, LANES), jnp.float32),
        (tables[0].shape, jnp.bfloat16),
        (tables[1].shape, jnp.bfloat16),
        ((RADIX, 2, 2 * part, part), jnp.float32),
        ((side_len, side_len), jnp.bfloat16),
        ((side_len, side_len), jnp.bfloat16),
    ]
    call = pl.pallas_call(
        functools.partial(gather_kernel, axes),
        out_shape=[
            pltpu.VMEM((2, span // LANES, span, LANES), jnp.bfloat16),
            pltpu.VMEM((slots, 2, side_blocks, side_len, LANES), jnp.float32),
            pltpu.VMEM(table, jnp.bfloat16),
            pltpu.VMEM((slots, RADIX, side_len, part), jnp.bfloat16),
            pltpu.VMEM((2, span // LANES, span, LANES), jnp.float32),
        ],
        in_specs=[pl.BlockSpec(memory_space=pltpu.SMEM)] + [hbm] * 7,
        out_specs=[vmem] * 5,
        scratch_shapes=[pltpu.VMEM(*each) for each in scratch]
        + [
            pltpu.SemaphoreType.DMA((4 + 8,)),
            pltpu.SemaphoreType.DMA((4 + 8,)),
            pltpu.SemaphoreType.DMA((10 + 4 * side_blocks,)),
            pltpu.SemaphoreType.REGULAR,
        ],
        compiler_params=pltpu.CompilerParams(
            collective_id=0, has_side_effects=True, vmem_limit_bytes=room(scratch)
        ),
    )
    prepared = call(shifts, own, measured, probe, *tables, *sorted_by_residue(side_len))
    held = [pltpu.with_memory_space_constraint(each, pltpu.VMEM) for each in prepared]
    return held, room(scratch)


def room(scratch):
    return sum(math.prod(shape) * jnp.dtype(kind).itemsize for shape, kind in scratch) + (1 << 20)


def scatter_kernel(
    axes,
    grown,
    total,
    from_left,
    spill,
    dropped,
    both,
    landed,
    from_up,
    sends,
    receives,
    ready,
):
    side_len = landed.shape[2]
    tile_len = total.shape[1]
    own_blocks = tile_len // LANES
    side_blocks = side_len // LANES
    scan, tile = neighbours(axes)
    has_left, left, has_right, right = scan
    has_up, up, has_down, down = tile
    odd = lax.rem(lax.axis_index(axes[1][0]), 2) == 1
    even = jnp.logical_not(odd)
    barrier = pltpu.get_barrier_semaphore()

    def tell(there, sem, peer):
        @pl.when(there)
        def _():
            pl.semaphore_signal(
                sem, inc=1, device_id=peer, device_id_type=pl.DeviceIdType.MESH
            )

    tell(has_left, barrier, left)
    tell(jnp.logical_and(even, has_up), barrier, up)
    tell(jnp.logical_and(even, has_down), barrier, down)
    corner = remote(both, landed, sends, receives, 0, down)
    under = remote(dropped, from_up, sends, receives, 1, down)
    rest = remote(
        spill.at[:, :, side_len:, :], from_left.at[:, :, side_len:, :], sends, receives, 2, right
    )
    top = remote(
        spill.at[:, :, :side_len, :], from_left.at[:, :, :side_len, :], sends, receives, 3, right
    )
    spill[:, :, side_len:, :] = grown[:, own_blocks:, side_len:tile_len, :].astype(jnp.bfloat16)
    both[...] = grown[:, own_blocks:, tile_len:, :].astype(jnp.bfloat16)
    from_even = has_up.astype(jnp.int32) + has_down.astype(jnp.int32)
    awaited = has_right.astype(jnp.int32) + jnp.where(odd, from_even, 0)

    @pl.when(awaited > 0)
    def _():
        pl.semaphore_wait(barrier, awaited)

    @pl.when(has_right)
    def _():
        rest.start()

    tell(odd, ready, up)

    @pl.when(jnp.logical_and(odd, has_down))
    def _():
        corner.start()

    @pl.when(jnp.logical_not(has_up))
    def _():
        spill[:, :, :side_len, :] = grown[:, own_blocks:, :side_len, :].astype(jnp.bfloat16)

    @pl.when(jnp.logical_and(jnp.logical_not(has_up), has_right))
    def _():
        top.start()

    dropped[...] = grown[:, :own_blocks, tile_len:, :].astype(jnp.bfloat16)

    @pl.when(jnp.logical_and(odd, has_down))
    def _():
        under.start()

    for c in range(2):
        for b in range(own_blocks):
            total[c, :, b * LANES : (b + 1) * LANES] = grown[c, b, :tile_len, :]

    @pl.when(jnp.logical_and(even, has_down))
    def _():
        pl.semaphore_wait(ready, 1)
        corner.start()
        under.start()

    @pl.when(has_up)
    def _():
        corner.wait_recv()
        spill[:, :, :side_len, :] = (
            grown[:, own_blocks:, :side_len, :] + landed[...].astype(jnp.float32)
        ).astype(jnp.bfloat16)

    @pl.when(jnp.logical_and(has_up, has_right))
    def _():
        top.start()

    def add(blocks, at, source):
        for c in range(2):
            for b in blocks:
                total[c, at, b * LANES : (b + 1) * LANES] += source[c, b, at, :].astype(jnp.float32)

    @pl.when(has_left)
    def _():
        rest.wait_recv()
        add(range(side_blocks), slice(side_len, tile_len), from_left)

    @pl.when(has_up)
    def _():
        under.wait_recv()
        add(range(own_blocks), slice(0, side_len), from_up)

    @pl.when(has_left)
    def _():
        top.wait_recv()

    @pl.when(jnp.logical_not(has_left))
    def _():
        from_left[:, :, :side_len, :] = jnp.zeros(
            (2, side_blocks, side_len, LANES), jnp.bfloat16
        )

    @pl.when(has_right)
    def _():
        rest.wait_send()
        top.wait_send()

    @pl.when(has_down)
    def _():
        corner.wait_send()
        under.wait_send()


def scatter(axes, grown, tile_len):
    span = grown.shape[2]
    side_len = span - tile_len
    own_blocks = tile_len // LANES
    side_blocks = side_len // LANES
    vmem = pl.BlockSpec(memory_space=pltpu.VMEM)
    scratch = [
        ((2, side_blocks, tile_len, LANES), jnp.bfloat16),
        ((2, own_blocks, side_len, LANES), jnp.bfloat16),
        ((2, side_blocks, side_len, LANES), jnp.bfloat16),
        ((2, side_blocks, side_len, LANES), jnp.bfloat16),
        ((2, own_blocks, side_len, LANES), jnp.bfloat16),
    ]
    summed = pl.pallas_call(
        functools.partial(scatter_kernel, axes),
        out_shape=[
            pltpu.VMEM((2, tile_len, tile_len), jnp.float32),
            pltpu.VMEM((2, side_blocks, tile_len, LANES), jnp.bfloat16),
        ],
        in_specs=[vmem],
        out_specs=[vmem] * 2,
        scratch_shapes=[pltpu.VMEM(*each) for each in scratch]
        + [
            pltpu.SemaphoreType.DMA((4,)),
            pltpu.SemaphoreType.DMA((4,)),
            pltpu.SemaphoreType.REGULAR,
        ],
        compiler_params=pltpu.CompilerParams(
            collective_id=1, has_side_effects=True, vmem_limit_bytes=room(scratch)
        ),
    )(grown)
    held = [pltpu.with_memory_space_constraint(each, pltpu.VMEM) for each in summed]
    return pl.pallas_call(
        finish_kernel,
        out_shape=jax.ShapeDtypeStruct((2, tile_len, tile_len), jnp.float32),
        in_specs=[vmem] * 2,
        out_specs=pl.BlockSpec(memory_space=pltpu.HBM),
        scratch_shapes=[
            pltpu.VMEM((2, side_len, side_len), jnp.float32),
            pltpu.SemaphoreType.DMA((2, 3)),
        ],
        compiler_params=pltpu.CompilerParams(vmem_limit_bytes=room(scratch)),
    )(*held)


def finish_kernel(total, from_left, out_hbm, head, puts):
    side_len = head.shape[1]
    copies = []
    for c in range(2):
        for i, at in enumerate(
            (
                (c, slice(side_len, None), slice(None)),
                (c, slice(0, side_len), slice(side_len, None)),
            )
        ):
            copies.append(pltpu.make_async_copy(total.at[at], out_hbm.at[at], puts.at[c, i]))
    for copy in copies:
        copy.start()
    for c in range(2):
        for b in range(side_len // LANES):
            cols = slice(b * LANES, (b + 1) * LANES)
            head[c, :, cols] = total[c, :side_len, cols] + from_left[c, b, :side_len, :].astype(
                jnp.float32
            )
        at = (c, slice(0, side_len), slice(0, side_len))
        copies.append(pltpu.make_async_copy(head.at[c], out_hbm.at[at], puts.at[c, 2]))
        copies[-1].start()
    for copy in copies:
        copy.wait()


def side_by_side(*blocks):
    return jnp.concatenate(blocks, axis=1)


def solve_kernel(
    live_ref,
    shift_ref,
    field,
    probes,
    tables,
    measured,
    zeros,
    grown,
    mixed,
    halves,
    misfits,
    spectra,
    backs,
):
    side_len = probes.shape[3]
    part = side_len // RADIX
    side_blocks = side_len // LANES
    lane = lax.broadcasted_iota(jnp.int32, (1, LANES), 1)
    line = lax.broadcasted_iota(jnp.int32, (GROUP, LANES), 0)

    def one_slot(slot, carry):
        row = shift_ref[0, slot]
        col = shift_ref[1, slot]
        lift = lax.rem(row, GROUP)
        turn = lax.rem(col, LANES)
        base = pl.multiple_of(row - lift, GROUP)
        block = lax.div(col, LANES)
        stay = lane >= turn
        below = line >= lift

        def table(side, kind, q):
            return side_by_side(tables[slot, side, kind, q, 0], tables[slot, side, kind, q, 1])

        def piece(c, b, at):
            def cut(b):
                start = pl.multiple_of(base + at, GROUP)
                value = field[c, block + b, pl.ds(start, GROUP), :]
                if at == 0:
                    start = pl.multiple_of(base + side_len, GROUP)
                    wrapped = field[c, block + b, pl.ds(start, GROUP), :]
                    value = jnp.where(below, value, wrapped)
                return value

            value = cut(b) if b else jnp.where(stay, cut(0), cut(side_blocks))
            return value.astype(jnp.float32)

        def exit_waves(blocks):
            for at in range(0, part, GROUP):
                for b in blocks:
                    waves = []
                    for p in range(RADIX):
                        here = at + p * part
                        re, im = piece(0, b, here), piece(1, b, here)
                        probe_re = probes[slot, 0, b, here : here + GROUP, :]
                        probe_im = probes[slot, 1, b, here : here + GROUP, :]
                        waves.append((probe_re * re - probe_im * im, probe_re * im + probe_im * re))
                    for q, (re, im) in enumerate(butterfly(waves, -1)):
                        mixed[q, b, at : at + GROUP, :] = re.astype(jnp.bfloat16)
                        mixed[q, b, at + part : at + part + GROUP, :] = im.astype(jnp.bfloat16)

        def split(value):
            return [
                (value[:part, at : at + part], value[part:, at : at + part])
                for at in range(0, value.shape[1], part)
            ]

        def left(q, blocks):
            return split(dot(table(0, 0, q), side_by_side(*(mixed[q, b] for b in blocks))))

        def far_field(other):
            return dot(side_by_side(halves[other, 0], halves[other, 1]), table(1, 1, other))

        def misfit_of(other, far):
            for q in range(RADIX):
                rows = slice(q * part, (q + 1) * part)
                far_re, far_im = far[rows, :part], far[rows, part:]
                seen = measured[slot, other, rows, :].astype(jnp.float32)
                misfit = far_re * far_re + far_im * far_im - seen
                misfits[q, other, :part, :] = (misfit * far_re).astype(jnp.bfloat16)
                misfits[q, other, part:, :] = (misfit * far_im).astype(jnp.bfloat16)

        def left_back(q, pair):
            mixture = dot(table(1, 0, q), side_by_side(*(misfits[q, other] for other in pair)))
            for i, other in enumerate(pair):
                spectra[q, other] = mixture[:, i * part : (i + 1) * part]

        def mix(ats, pair):
            for at in ats:
                for other in pair:
                    parts = [
                        (
                            spectra[q, other, at : at + GROUP, :],
                            spectra[q, other, part + at : part + at + GROUP, :],
                        )
                        for q in range(RADIX)
                    ]
                    for p, (re, im) in enumerate(butterfly(parts, 1)):
                        here = slice(at + p * part, at + p * part + GROUP)
                        backs[other, 0, here, :] = re.astype(jnp.bfloat16)
                        backs[other, 1, here, :] = im.astype(jnp.bfloat16)

        def add(c, b, at, value, mask=None):
            where = pl.ds(pl.multiple_of(base + at, GROUP), value.shape[0])
            if mask is None:
                grown[c, block + b, where, :] += value
            else:
                spot = grown.at[c, block + b, where, :]
                mask = jnp.broadcast_to(mask, value.shape)
                pltpu.store(spot, spot[...] + value, mask=mask)

        def add_wrapped(c, b, at, value, mask=None):
            if at == 0:
                add(c, b, 0, jnp.where(below, value[:GROUP], 0.0), mask)
                add(c, b, side_len, jnp.where(below, 0.0, value[:GROUP]), mask)
                add(c, b, GROUP, value[GROUP:], mask)
            else:
                add(c, b, at, value, mask)

        def right_back(at, tall):
            parts = []
            for other in range(RADIX):
                back = jnp.concatenate(
                    [
                        side_by_side(
                            backs[other, 0, here : here + tall, :],
                            backs[other, 1, here : here + tall, :],
                        )
                        for here in range(at, side_len, part)
                    ],
                    axis=0,
                )
                grad = dot(back, table(0, 1, other))
                parts.append((grad[:, :part], grad[:, part:]))
            return parts

        def accumulate(at, tall, parts):
            for p in range(RADIX):
                here = at + p * part
                rows = slice(p * tall, (p + 1) * tall)
                some = [(re[rows], im[rows]) for re, im in parts]
                for b, (re, im) in enumerate(butterfly(some, 1)):
                    probe_re = probes[slot, 0, b, here : here + tall, :]
                    probe_im = probes[slot, 1, b, here : here + tall, :]
                    values = (probe_re * re + probe_im * im, probe_re * im - probe_im * re)
                    for c, value in enumerate(values):
                        if b == 0:
                            add_wrapped(c, 0, here, value, stay)
                            add_wrapped(c, side_blocks, here, value, jnp.logical_not(stay))
                        else:
                            add_wrapped(c, b, here, value)

        exit_waves((0, 2))
        early = [left(q, (0, 2)) for q in range(RADIX)]
        exit_waves((1, 3))
        for q in range(RADIX):
            rows = slice(q * part, (q + 1) * part)
            (r0, r2), (r1, r3) = early[q], left(q, (1, 3))
            for other, (re, im) in enumerate(butterfly([r0, r1, r2, r3], -1)):
                halves[other, 0, rows, :] = re.astype(jnp.bfloat16)
                halves[other, 1, rows, :] = im.astype(jnp.bfloat16)
        ahead = far_field(0)
        for other in range(RADIX):
            far = ahead
            if other + 1 < RADIX:
                ahead = far_field(other + 1)
            misfit_of(other, far)
            if other == 2:
                for q in range(RADIX):
                    left_back(q, (0, 1))
        tall = part // 2
        ats = [range(at, at + tall, GROUP) for at in range(0, part, tall)]
        for q in range(RADIX):
            left_back(q, (2, 3))
        mix(ats[0], range(RADIX))
        mix(ats[1], range(RADIX))
        first = right_back(0, tall)
        second = right_back(tall, tall)
        accumulate(0, tall, first)
        accumulate(tall, tall, second)
        return carry

    lax.fori_loop(0, live_ref[0, lax.axis_index("scan")], one_slot, 0)


def solve(live_counts, shifts, prepared, limit):
    grown = prepared[-1]
    side_len = prepared[1].shape[3]
    part = side_len // RADIX
    smem = pl.BlockSpec(memory_space=pltpu.SMEM)
    vmem = pl.BlockSpec(memory_space=pltpu.VMEM)
    wide = (RADIX, RADIX, 2 * part, part)
    tall = (RADIX, 2, side_len, part)
    scratch = [
        (wide, jnp.bfloat16),
        (tall, jnp.bfloat16),
        (wide, jnp.bfloat16),
        (wide, jnp.float32),
        (tall, jnp.bfloat16),
    ]
    return pl.pallas_call(
        solve_kernel,
        out_shape=pltpu.VMEM(grown.shape, grown.dtype),
        in_specs=[smem, smem] + [vmem] * len(prepared),
        out_specs=vmem,
        scratch_shapes=[pltpu.VMEM(*each) for each in scratch],
        input_output_aliases={1 + len(prepared): 0},
        compiler_params=pltpu.CompilerParams(vmem_limit_bytes=limit),
    )(live_counts, shifts, *prepared)


def shards(axes, object_slab, probe_field, intensities, offsets, live_count):
    tables = residue_tables(probe_field.shape[-1])
    shifts = offsets[0, 0].T
    prepared, limit = gather(axes, shifts, object_slab, intensities[0, 0], probe_field, tables)
    grown = solve(live_count.T, shifts, prepared, limit)
    return scatter(axes, grown, object_slab.shape[1])


def solution(mesh):
    placed = (
        P(None, "tile", "scan"),
        P(),
        P("scan", "tile", None, None, None),
        P("scan", "tile", None, None),
        P(None, "tile"),
    )
    axes = tuple((name, mesh.shape[name]) for name in ("scan", "tile"))
    return jax.shard_map(
        functools.partial(shards, axes), mesh=mesh, in_specs=placed, out_specs=P(None, "tile", "scan"), check_vma=False
    )
```

```python
import functools
import math

import jax
import jax.numpy as jnp
import numpy as np
from jax import lax
from jax.experimental import pallas as pl
from jax.experimental.pallas import tpu as pltpu
from jax.sharding import PartitionSpec as P

RADIX = 4
LANES = 128
GROUP = 16


def residue_tables(side_len):
    part = side_len // RADIX
    freq = np.arange(side_len).reshape(part, RADIX).T
    across = np.arange(part)
    phase = (freq[:, :, None] * across[None, None, :] % side_len) * (2.0 * math.pi / side_len)
    factor = 1.0 / math.sqrt(side_len)
    cos = np.cos(phase) * factor
    sin = np.sin(phase) * factor
    rows = np.concatenate(
        [np.concatenate([cos, sin], axis=2), np.concatenate([-sin, cos], axis=2)], axis=1
    ).astype(np.float32)
    return jnp.asarray(rows, jnp.bfloat16), jnp.asarray(rows.swapaxes(1, 2), jnp.bfloat16)


def sorted_by_residue(side_len):
    at = np.arange(side_len)
    source = at % (side_len // RADIX) * RADIX + at // (side_len // RADIX)
    sort = (source[:, None] == at[None, :]).astype(np.float32)
    return jnp.asarray(sort, jnp.bfloat16), jnp.asarray(sort.T, jnp.bfloat16)


def dot(a, b):
    return jnp.dot(a, b, preferred_element_type=jnp.float32)


def butterfly(parts, sign):
    (r0, i0), (r1, i1), (r2, i2), (r3, i3) = parts
    ar, ai, br, bi = r0 + r2, i0 + i2, r1 + r3, i1 + i3
    cr, ci, dr, di = r0 - r2, i0 - i2, r1 - r3, i1 - i3
    plus = (cr - di, ci + dr)
    minus = (cr + di, ci - dr)
    first, third = (plus, minus) if sign > 0 else (minus, plus)
    return [(ar + br, ai + bi), first, (ar - br, ai - bi), third]


def neighbours(axes):
    result = []
    for name, count in axes:
        me = lax.axis_index(name)
        result.append((me > 0, {name: me - 1}, me < count - 1, {name: me + 1}))
    return result


def greet(peers):
    barrier = pltpu.get_barrier_semaphore()
    for has_low, low, has_high, high in peers:
        for there, peer in ((has_low, low), (has_high, high)):

            @pl.when(there)
            def _(peer=peer):
                pl.semaphore_signal(
                    barrier, inc=1, device_id=peer, device_id_type=pl.DeviceIdType.MESH
                )


def all_here(peers):
    count = sum(
        there.astype(jnp.int32) for has_low, _, has_high, _ in peers for there in (has_low, has_high)
    )
    pl.semaphore_wait(pltpu.get_barrier_semaphore(), count)


def remote(source, target, sends, receives, index, peer):
    return pltpu.make_async_remote_copy(
        src_ref=source,
        dst_ref=target,
        send_sem=sends.at[index],
        recv_sem=receives.at[index],
        device_id=peer,
        device_id_type=pl.DeviceIdType.MESH,
    )


def quarter_turns(cos, sin, q):
    return ((cos, sin), (sin, -cos), (-cos, -sin), (-sin, cos))[q]


def in_place(mask, cos, sin, q):
    wrapped = quarter_turns(cos, sin, q)
    return jnp.where(mask, cos, wrapped[0]), jnp.where(mask, sin, wrapped[1])


def gather_kernel(
    axes,
    shift_ref,
    own_hbm,
    measured_hbm,
    probe_hbm,
    rows_hbm,
    cols_hbm,
    sort_hbm,
    unsort_hbm,
    field,
    probes,
    tables,
    arranged,
    grown,
    own,
    measured,
    extended,
    rows_ref,
    cols_ref,
    doubled,
    sort,
    unsort,
    carried,
    sends,
    receives,
    fetches,
    freed,
):
    slots, side_len = measured.shape[:2]
    tile_len = own.shape[1]
    part = side_len // RADIX
    own_blocks = tile_len // LANES
    side_blocks = side_len // LANES
    scan, tile = neighbours(axes)
    has_left, left, has_right, _ = scan
    has_up, up, has_down, down = tile
    name, count = axes[1]
    row = lax.axis_index(name)
    odd = lax.rem(row, 2) == 1
    past_up = jnp.logical_and(odd, row >= 2)
    past_down = jnp.logical_and(odd, row + 2 < count)
    beyond = (past_up, {name: row - 2}, past_down, {name: row + 2})
    hands_off = jnp.logical_and(jnp.logical_not(odd), jnp.logical_and(has_up, has_down))
    greet((scan, tile, beyond))
    firsts = [
        pltpu.make_async_copy(
            own_hbm.at[c, :side_len, :side_len],
            own.at[c, :side_len, :side_len],
            fetches.at[4 * c],
        )
        for c in range(2)
    ]
    second = pltpu.make_async_copy(
        own_hbm.at[:, side_len:, :side_len], own.at[:, side_len:, :side_len], fetches.at[1]
    )
    third = pltpu.make_async_copy(
        own_hbm.at[:, :side_len, side_len:], own.at[:, :side_len, side_len:], fetches.at[2]
    )
    fourth = pltpu.make_async_copy(
        own_hbm.at[:, side_len:, side_len:], own.at[:, side_len:, side_len:], fetches.at[3]
    )
    constants = [
        pltpu.make_async_copy(source, target, fetches.at[5 + i])
        for i, (source, target) in enumerate(
            (
                (sort_hbm, sort),
                (unsort_hbm, unsort),
                (measured_hbm, measured),
                (rows_hbm, rows_ref),
                (cols_hbm, cols_ref),
            )
        )
    ]
    for c in range(2):
        for b in range(side_blocks):
            cols = slice(b * LANES, (b + 1) * LANES)
            for source, target in (
                (probe_hbm.at[c, :, cols], extended.at[c, b, GROUP:, :]),
                (probe_hbm.at[c, side_len - GROUP :, cols], extended.at[c, b, :GROUP, :]),
            ):
                constants.append(
                    pltpu.make_async_copy(source, target, fetches.at[5 + len(constants)])
                )
    for load in firsts + [third, second, fourth] + constants:
        load.start()
    near = slice(0, side_blocks)
    far = slice(own_blocks, own_blocks + side_blocks)
    halves = [
        (c, slice(at, at + side_blocks // 2))
        for c in range(2)
        for at in range(0, side_blocks, side_blocks // 2)
    ]

    def moved(blocks):
        return slice(blocks.start + own_blocks, blocks.stop + own_blocks)

    tops = [
        remote(
            field.at[c, blocks, :side_len, :],
            field.at[c, moved(blocks), :side_len, :],
            sends,
            receives,
            3 + i,
            left,
        )
        for i, (c, blocks) in enumerate(halves)
    ]
    rests = [
        remote(
            field.at[c, near, side_len:tile_len, :],
            field.at[c, far, side_len:tile_len, :],
            sends,
            receives,
            c,
            left,
        )
        for c in range(2)
    ]
    unders = [
        remote(
            field.at[:, blocks, :side_len, :],
            field.at[:, blocks, tile_len:, :],
            sends,
            receives,
            index,
            up,
        )
        for blocks, index in (
            (near, 2),
            (slice(side_blocks, own_blocks), 3 + 2 * len(halves)),
        )
    ]
    beside = (field.at[:, side_blocks:own_blocks, :side_len, :], carried)
    lent = remote(*beside, sends, receives, 4 + 2 * len(halves), down)
    passed_on = pltpu.make_async_remote_copy(
        src_ref=carried,
        dst_ref=field.at[:, side_blocks:own_blocks, tile_len:, :],
        send_sem=sends.at[5 + 2 * len(halves)],
        recv_sem=receives.at[3 + 2 * len(halves)],
        device_id=beyond[1],
        device_id_type=pl.DeviceIdType.MESH,
    )
    acrosses = [
        remote(
            field.at[c, moved(blocks), :side_len, :],
            field.at[c, moved(blocks), tile_len:, :],
            sends,
            receives,
            3 + len(halves) + i,
            up,
        )
        for i, (c, blocks) in enumerate(halves)
    ]

    def narrow(blocks, at, planes=range(2)):
        for c in planes:
            for b in blocks:
                field[c, b, at, :] = own[c, at, b * LANES : (b + 1) * LANES].astype(jnp.bfloat16)

    firsts[0].wait()
    narrow(range(side_blocks), slice(0, side_len), range(1))
    all_here((scan, tile, beyond))

    @pl.when(has_left)
    def _():
        for each in tops[:2]:
            each.start()

    firsts[1].wait()
    narrow(range(side_blocks), slice(0, side_len), range(1, 2))

    @pl.when(has_left)
    def _():
        for each in tops[2:]:
            each.start()

    @pl.when(has_up)
    def _():
        unders[0].start()

    third.wait()
    narrow(range(side_blocks, own_blocks), slice(0, side_len))

    @pl.when(jnp.logical_and(has_up, jnp.logical_not(hands_off)))
    def _():
        unders[1].start()

    @pl.when(hands_off)
    def _():
        lent.start()

    second.wait()
    narrow(range(side_blocks), slice(side_len, tile_len))

    first_turn = jnp.logical_and(has_left, jnp.logical_not(odd))
    second_turn = jnp.logical_and(has_left, odd)

    @pl.when(first_turn)
    def _():
        for each in rests:
            each.start()

    @pl.when(jnp.logical_not(has_right))
    def _():
        field[:, far, :tile_len, :] = jnp.zeros(
            (2, side_blocks, tile_len, LANES), jnp.bfloat16
        )

    @pl.when(jnp.logical_not(has_down))
    def _():
        field[:, :, tile_len:, :] = jnp.zeros(
            (2, own_blocks + side_blocks, side_len, LANES), jnp.bfloat16
        )

    fourth.wait()
    narrow(range(side_blocks, own_blocks), slice(side_len, tile_len))
    for load in constants:
        load.wait()

    def sort_slot(slot, carry):
        rows = dot(sort[...], measured[slot]).astype(jnp.bfloat16)
        both = dot(rows, unsort[...]).astype(jnp.bfloat16)
        for b in range(RADIX):
            arranged[slot, b] = both[:, b * part : (b + 1) * part]
        return carry

    lax.fori_loop(0, slots, sort_slot, 0)

    grown[...] = jnp.zeros_like(grown)
    for q in range(RADIX):
        for i in range(2):
            for at in (0, part):
                doubled[q, i, at : at + part, :] = cols_ref[
                    q, i * part : (i + 1) * part, :part
                ].astype(jnp.float32)

    lane = lax.broadcasted_iota(jnp.int32, (1, LANES), 1)
    line = lax.broadcasted_iota(jnp.int32, (part, LANES), 0)
    chunk = 32

    def prepare(slot, carry):
        lift = lax.rem(shift_ref[0, slot], GROUP)
        turn = lax.rem(shift_ref[1, slot], LANES)

        def move_probe(i, carry):
            at = pl.multiple_of(i * chunk, chunk)
            for c in range(2):
                turned = [
                    pltpu.roll(extended[c, b, pl.ds(GROUP - lift + at, chunk), :], turn, 1)
                    for b in range(side_blocks)
                ]
                for b in range(side_blocks):
                    probes[slot, c, b, pl.ds(at, chunk), :] = jnp.where(
                        lane >= turn, turned[b], turned[b - 1]
                    )
            return carry

        lax.fori_loop(0, side_len // chunk, move_probe, 0)
        for k, by in enumerate((lift, turn)):
            for q in range(RADIX):
                cos = pltpu.roll(rows_ref[q, :part, :part].astype(jnp.float32), by, 1)
                sin = pltpu.roll(rows_ref[q, :part, part:].astype(jnp.float32), by, 1)
                cos, sin = in_place(lane >= by, cos, sin, q)
                tables[slot, 0, k, q, 0, :part, :] = cos.astype(jnp.bfloat16)
                tables[slot, 0, k, q, 1, :part, :] = sin.astype(jnp.bfloat16)
                tables[slot, 0, k, q, 0, part:, :] = (-sin).astype(jnp.bfloat16)
                tables[slot, 0, k, q, 1, part:, :] = cos.astype(jnp.bfloat16)
                cos = doubled[q, 0, pl.ds(part - by, part), :]
                sin = doubled[q, 1, pl.ds(part - by, part), :]
                cos, sin = in_place(line >= by, cos, sin, q)
                tables[slot, 1, k, q, 0, :part, :] = cos.astype(jnp.bfloat16)
                tables[slot, 1, k, q, 1, :part, :] = (-sin).astype(jnp.bfloat16)
                tables[slot, 1, k, q, 0, part:, :] = sin.astype(jnp.bfloat16)
                tables[slot, 1, k, q, 1, part:, :] = cos.astype(jnp.bfloat16)
        return carry

    lax.fori_loop(0, slots, prepare, 0)

    for top, across in zip(tops, acrosses):

        @pl.when(has_right)
        def _(top=top):
            top.wait_recv()

        @pl.when(has_up)
        def _(across=across):
            across.start()

    @pl.when(past_up)
    def _():
        lent.wait_recv()
        passed_on.start()

    @pl.when(first_turn)
    def _():
        for each in tops + rests:
            each.wait_send()

    @pl.when(jnp.logical_and(first_turn, has_down))
    def _():
        pl.semaphore_signal(
            freed, inc=1, device_id=down, device_id_type=pl.DeviceIdType.MESH
        )

    @pl.when(second_turn)
    def _():
        pl.semaphore_wait(freed, 1)
        for each in rests:
            each.start()


    @pl.when(has_down)
    def _():
        for each in unders:
            each.wait_recv()

    @pl.when(has_right)
    def _():
        for each in rests:
            each.wait_recv()

    @pl.when(has_down)
    def _():
        for each in acrosses:
            each.wait_recv()

    @pl.when(second_turn)
    def _():
        for each in tops + rests:
            each.wait_send()

    @pl.when(has_up)
    def _():
        unders[0].wait_send()
        for each in acrosses:
            each.wait_send()

    @pl.when(jnp.logical_and(has_up, jnp.logical_not(hands_off)))
    def _():
        unders[1].wait_send()

    @pl.when(hands_off)
    def _():
        lent.wait_send()

    @pl.when(past_up)
    def _():
        passed_on.wait_send()


def gather(axes, shifts, own, measured, probe, tables):
    slots, side_len = measured.shape[:2]
    tile_len = own.shape[1]
    span = tile_len + side_len
    part = side_len // RADIX
    side_blocks = side_len // LANES
    hbm = pl.BlockSpec(memory_space=pltpu.HBM)
    vmem = pl.BlockSpec(memory_space=pltpu.VMEM)
    table = (slots, 2, 2, RADIX, 2, 2 * part, part)
    scratch = [
        (own.shape, jnp.float32),
        (measured.shape, jnp.bfloat16),
        ((2, side_blocks, side_len + GROUP, LANES), jnp.float32),
        (tables[0].shape, jnp.bfloat16),
        (tables[1].shape, jnp.bfloat16),
        ((RADIX, 2, 2 * part, part), jnp.float32),
        ((side_len, side_len), jnp.bfloat16),
        ((side_len, side_len), jnp.bfloat16),
        ((2, tile_len // LANES - side_blocks, side_len, LANES), jnp.bfloat16),
    ]
    call = pl.pallas_call(
        functools.partial(gather_kernel, axes),
        out_shape=[
            pltpu.VMEM((2, span // LANES, span, LANES), jnp.bfloat16),
            pltpu.VMEM((slots, 2, side_blocks, side_len, LANES), jnp.float32),
            pltpu.VMEM(table, jnp.bfloat16),
            pltpu.VMEM((slots, RADIX, side_len, part), jnp.bfloat16),
            pltpu.VMEM((2, span // LANES, span, LANES), jnp.float32),
        ],
        in_specs=[pl.BlockSpec(memory_space=pltpu.SMEM)] + [hbm] * 7,
        out_specs=[vmem] * 5,
        scratch_shapes=[pltpu.VMEM(*each) for each in scratch]
        + [
            pltpu.SemaphoreType.DMA((6 + 8,)),
            pltpu.SemaphoreType.DMA((6 + 8,)),
            pltpu.SemaphoreType.DMA((10 + 4 * side_blocks,)),
            pltpu.SemaphoreType.REGULAR,
        ],
        compiler_params=pltpu.CompilerParams(
            collective_id=0, has_side_effects=True, vmem_limit_bytes=room(scratch)
        ),
    )
    prepared = call(shifts, own, measured, probe, *tables, *sorted_by_residue(side_len))
    held = [pltpu.with_memory_space_constraint(each, pltpu.VMEM) for each in prepared]
    return held, room(scratch)


def room(scratch):
    return sum(math.prod(shape) * jnp.dtype(kind).itemsize for shape, kind in scratch) + (1 << 20)


def scatter_kernel(
    axes,
    grown,
    total,
    from_left,
    spill,
    dropped,
    both,
    landed,
    from_up,
    sends,
    receives,
    ready,
):
    side_len = landed.shape[2]
    tile_len = total.shape[1]
    own_blocks = tile_len // LANES
    side_blocks = side_len // LANES
    scan, tile = neighbours(axes)
    has_left, left, has_right, right = scan
    has_up, up, has_down, down = tile
    odd = lax.rem(lax.axis_index(axes[1][0]), 2) == 1
    even = jnp.logical_not(odd)
    barrier = pltpu.get_barrier_semaphore()

    def tell(there, sem, peer):
        @pl.when(there)
        def _():
            pl.semaphore_signal(
                sem, inc=1, device_id=peer, device_id_type=pl.DeviceIdType.MESH
            )

    tell(has_left, barrier, left)
    tell(jnp.logical_and(even, has_up), barrier, up)
    tell(jnp.logical_and(even, has_down), barrier, down)
    corner = remote(both, landed, sends, receives, 0, down)
    under = remote(dropped, from_up, sends, receives, 1, down)
    rest = remote(
        spill.at[:, :, side_len:, :], from_left.at[:, :, side_len:, :], sends, receives, 2, right
    )
    top = remote(
        spill.at[:, :, :side_len, :], from_left.at[:, :, :side_len, :], sends, receives, 3, right
    )
    spill[:, :, side_len:, :] = grown[:, own_blocks:, side_len:tile_len, :].astype(jnp.bfloat16)
    both[...] = grown[:, own_blocks:, tile_len:, :].astype(jnp.bfloat16)
    from_even = has_up.astype(jnp.int32) + has_down.astype(jnp.int32)
    awaited = has_right.astype(jnp.int32) + jnp.where(odd, from_even, 0)

    @pl.when(awaited > 0)
    def _():
        pl.semaphore_wait(barrier, awaited)

    @pl.when(has_right)
    def _():
        rest.start()

    tell(odd, ready, up)

    @pl.when(jnp.logical_and(odd, has_down))
    def _():
        corner.start()

    @pl.when(jnp.logical_not(has_up))
    def _():
        spill[:, :, :side_len, :] = grown[:, own_blocks:, :side_len, :].astype(jnp.bfloat16)

    @pl.when(jnp.logical_and(jnp.logical_not(has_up), has_right))
    def _():
        top.start()

    dropped[...] = grown[:, :own_blocks, tile_len:, :].astype(jnp.bfloat16)

    @pl.when(jnp.logical_and(odd, has_down))
    def _():
        under.start()

    for c in range(2):
        for b in range(own_blocks):
            total[c, :, b * LANES : (b + 1) * LANES] = grown[c, b, :tile_len, :]

    @pl.when(jnp.logical_and(even, has_down))
    def _():
        pl.semaphore_wait(ready, 1)
        corner.start()
        under.start()

    @pl.when(has_up)
    def _():
        corner.wait_recv()
        spill[:, :, :side_len, :] = (
            grown[:, own_blocks:, :side_len, :] + landed[...].astype(jnp.float32)
        ).astype(jnp.bfloat16)

    @pl.when(jnp.logical_and(has_up, has_right))
    def _():
        top.start()

    def add(blocks, at, source):
        for c in range(2):
            for b in blocks:
                total[c, at, b * LANES : (b + 1) * LANES] += source[c, b, at, :].astype(jnp.float32)

    @pl.when(has_left)
    def _():
        rest.wait_recv()
        add(range(side_blocks), slice(side_len, tile_len), from_left)

    @pl.when(has_up)
    def _():
        under.wait_recv()
        add(range(own_blocks), slice(0, side_len), from_up)

    @pl.when(has_left)
    def _():
        top.wait_recv()

    @pl.when(jnp.logical_not(has_left))
    def _():
        from_left[:, :, :side_len, :] = jnp.zeros(
            (2, side_blocks, side_len, LANES), jnp.bfloat16
        )

    @pl.when(has_right)
    def _():
        rest.wait_send()
        top.wait_send()

    @pl.when(has_down)
    def _():
        corner.wait_send()
        under.wait_send()


def scatter(axes, grown, tile_len):
    span = grown.shape[2]
    side_len = span - tile_len
    own_blocks = tile_len // LANES
    side_blocks = side_len // LANES
    vmem = pl.BlockSpec(memory_space=pltpu.VMEM)
    scratch = [
        ((2, side_blocks, tile_len, LANES), jnp.bfloat16),
        ((2, own_blocks, side_len, LANES), jnp.bfloat16),
        ((2, side_blocks, side_len, LANES), jnp.bfloat16),
        ((2, side_blocks, side_len, LANES), jnp.bfloat16),
        ((2, own_blocks, side_len, LANES), jnp.bfloat16),
    ]
    summed = pl.pallas_call(
        functools.partial(scatter_kernel, axes),
        out_shape=[
            pltpu.VMEM((2, tile_len, tile_len), jnp.float32),
            pltpu.VMEM((2, side_blocks, tile_len, LANES), jnp.bfloat16),
        ],
        in_specs=[vmem],
        out_specs=[vmem] * 2,
        scratch_shapes=[pltpu.VMEM(*each) for each in scratch]
        + [
            pltpu.SemaphoreType.DMA((4,)),
            pltpu.SemaphoreType.DMA((4,)),
            pltpu.SemaphoreType.REGULAR,
        ],
        compiler_params=pltpu.CompilerParams(
            collective_id=1, has_side_effects=True, vmem_limit_bytes=room(scratch)
        ),
    )(grown)
    held = [pltpu.with_memory_space_constraint(each, pltpu.VMEM) for each in summed]
    return pl.pallas_call(
        finish_kernel,
        out_shape=jax.ShapeDtypeStruct((2, tile_len, tile_len), jnp.float32),
        in_specs=[vmem] * 2,
        out_specs=pl.BlockSpec(memory_space=pltpu.HBM),
        scratch_shapes=[
            pltpu.VMEM((2, side_len, side_len), jnp.float32),
            pltpu.SemaphoreType.DMA((2, 3)),
        ],
        compiler_params=pltpu.CompilerParams(vmem_limit_bytes=room(scratch)),
    )(*held)


def finish_kernel(total, from_left, out_hbm, head, puts):
    side_len = head.shape[1]
    copies = []
    for c in range(2):
        for i, at in enumerate(
            (
                (c, slice(side_len, None), slice(None)),
                (c, slice(0, side_len), slice(side_len, None)),
            )
        ):
            copies.append(pltpu.make_async_copy(total.at[at], out_hbm.at[at], puts.at[c, i]))
    for copy in copies:
        copy.start()
    for c in range(2):
        for b in range(side_len // LANES):
            cols = slice(b * LANES, (b + 1) * LANES)
            head[c, :, cols] = total[c, :side_len, cols] + from_left[c, b, :side_len, :].astype(
                jnp.float32
            )
        at = (c, slice(0, side_len), slice(0, side_len))
        copies.append(pltpu.make_async_copy(head.at[c], out_hbm.at[at], puts.at[c, 2]))
        copies[-1].start()
    for copy in copies:
        copy.wait()


def side_by_side(*blocks):
    return jnp.concatenate(blocks, axis=1)


def solve_kernel(
    live_ref,
    shift_ref,
    field,
    probes,
    tables,
    measured,
    zeros,
    grown,
    mixed,
    halves,
    misfits,
    spectra,
    backs,
):
    side_len = probes.shape[3]
    part = side_len // RADIX
    side_blocks = side_len // LANES
    lane = lax.broadcasted_iota(jnp.int32, (1, LANES), 1)
    line = lax.broadcasted_iota(jnp.int32, (GROUP, LANES), 0)

    def one_slot(slot, carry):
        row = shift_ref[0, slot]
        col = shift_ref[1, slot]
        lift = lax.rem(row, GROUP)
        turn = lax.rem(col, LANES)
        base = pl.multiple_of(row - lift, GROUP)
        block = lax.div(col, LANES)
        stay = lane >= turn
        below = line >= lift

        def table(side, kind, q):
            return side_by_side(tables[slot, side, kind, q, 0], tables[slot, side, kind, q, 1])

        def piece(c, b, at):
            def cut(b):
                start = pl.multiple_of(base + at, GROUP)
                value = field[c, block + b, pl.ds(start, GROUP), :]
                if at == 0:
                    start = pl.multiple_of(base + side_len, GROUP)
                    wrapped = field[c, block + b, pl.ds(start, GROUP), :]
                    value = jnp.where(below, value, wrapped)
                return value

            value = cut(b) if b else jnp.where(stay, cut(0), cut(side_blocks))
            return value.astype(jnp.float32)

        def exit_waves(blocks):
            for at in range(0, part, GROUP):
                for b in blocks:
                    waves = []
                    for p in range(RADIX):
                        here = at + p * part
                        re, im = piece(0, b, here), piece(1, b, here)
                        probe_re = probes[slot, 0, b, here : here + GROUP, :]
                        probe_im = probes[slot, 1, b, here : here + GROUP, :]
                        waves.append((probe_re * re - probe_im * im, probe_re * im + probe_im * re))
                    for q, (re, im) in enumerate(butterfly(waves, -1)):
                        mixed[q, b, at : at + GROUP, :] = re.astype(jnp.bfloat16)
                        mixed[q, b, at + part : at + part + GROUP, :] = im.astype(jnp.bfloat16)

        def split(value):
            return [
                (value[:part, at : at + part], value[part:, at : at + part])
                for at in range(0, value.shape[1], part)
            ]

        def left(q, blocks):
            return split(dot(table(0, 0, q), side_by_side(*(mixed[q, b] for b in blocks))))

        def far_field(other):
            return dot(side_by_side(halves[other, 0], halves[other, 1]), table(1, 1, other))

        def misfit_of(other, far):
            for q in range(RADIX):
                rows = slice(q * part, (q + 1) * part)
                far_re, far_im = far[rows, :part], far[rows, part:]
                seen = measured[slot, other, rows, :].astype(jnp.float32)
                misfit = far_re * far_re + far_im * far_im - seen
                misfits[q, other, :part, :] = (misfit * far_re).astype(jnp.bfloat16)
                misfits[q, other, part:, :] = (misfit * far_im).astype(jnp.bfloat16)

        def left_back(q, pair):
            mixture = dot(table(1, 0, q), side_by_side(*(misfits[q, other] for other in pair)))
            for i, other in enumerate(pair):
                spectra[q, other] = mixture[:, i * part : (i + 1) * part]

        def mix(ats, pair):
            for at in ats:
                for other in pair:
                    parts = [
                        (
                            spectra[q, other, at : at + GROUP, :],
                            spectra[q, other, part + at : part + at + GROUP, :],
                        )
                        for q in range(RADIX)
                    ]
                    for p, (re, im) in enumerate(butterfly(parts, 1)):
                        here = slice(at + p * part, at + p * part + GROUP)
                        backs[other, 0, here, :] = re.astype(jnp.bfloat16)
                        backs[other, 1, here, :] = im.astype(jnp.bfloat16)

        def add(c, b, at, value, mask=None):
            where = pl.ds(pl.multiple_of(base + at, GROUP), value.shape[0])
            if mask is None:
                grown[c, block + b, where, :] += value
            else:
                spot = grown.at[c, block + b, where, :]
                mask = jnp.broadcast_to(mask, value.shape)
                pltpu.store(spot, spot[...] + value, mask=mask)

        def add_wrapped(c, b, at, value, mask=None):
            if at == 0:
                add(c, b, 0, jnp.where(below, value[:GROUP], 0.0), mask)
                add(c, b, side_len, jnp.where(below, 0.0, value[:GROUP]), mask)
                add(c, b, GROUP, value[GROUP:], mask)
            else:
                add(c, b, at, value, mask)

        def right_back(at, tall):
            parts = []
            for other in range(RADIX):
                back = jnp.concatenate(
                    [
                        side_by_side(
                            backs[other, 0, here : here + tall, :],
                            backs[other, 1, here : here + tall, :],
                        )
                        for here in range(at, side_len, part)
                    ],
                    axis=0,
                )
                grad = dot(back, table(0, 1, other))
                parts.append((grad[:, :part], grad[:, part:]))
            return parts

        def accumulate(at, tall, parts):
            for p in range(RADIX):
                here = at + p * part
                rows = slice(p * tall, (p + 1) * tall)
                some = [(re[rows], im[rows]) for re, im in parts]
                for b, (re, im) in enumerate(butterfly(some, 1)):
                    probe_re = probes[slot, 0, b, here : here + tall, :]
                    probe_im = probes[slot, 1, b, here : here + tall, :]
                    values = (probe_re * re + probe_im * im, probe_re * im - probe_im * re)
                    for c, value in enumerate(values):
                        if b == 0:
                            add_wrapped(c, 0, here, value, stay)
                            add_wrapped(c, side_blocks, here, value, jnp.logical_not(stay))
                        else:
                            add_wrapped(c, b, here, value)

        exit_waves((0, 2))
        early = [left(q, (0, 2)) for q in range(RADIX)]
        exit_waves((1, 3))
        for q in range(RADIX):
            rows = slice(q * part, (q + 1) * part)
            (r0, r2), (r1, r3) = early[q], left(q, (1, 3))
            for other, (re, im) in enumerate(butterfly([r0, r1, r2, r3], -1)):
                halves[other, 0, rows, :] = re.astype(jnp.bfloat16)
                halves[other, 1, rows, :] = im.astype(jnp.bfloat16)
        ahead = far_field(0)
        for other in range(RADIX):
            far = ahead
            if other + 1 < RADIX:
                ahead = far_field(other + 1)
            misfit_of(other, far)
            if other == 2:
                for q in range(RADIX):
                    left_back(q, (0, 1))
        tall = part // 2
        ats = [range(at, at + tall, GROUP) for at in range(0, part, tall)]
        for q in range(RADIX):
            left_back(q, (2, 3))
        mix(ats[0], range(RADIX))
        mix(ats[1], range(RADIX))
        first = right_back(0, tall)
        second = right_back(tall, tall)
        accumulate(0, tall, first)
        accumulate(tall, tall, second)
        return carry

    lax.fori_loop(0, live_ref[0, lax.axis_index("scan")], one_slot, 0)


def solve(live_counts, shifts, prepared, limit):
    grown = prepared[-1]
    side_len = prepared[1].shape[3]
    part = side_len // RADIX
    smem = pl.BlockSpec(memory_space=pltpu.SMEM)
    vmem = pl.BlockSpec(memory_space=pltpu.VMEM)
    wide = (RADIX, RADIX, 2 * part, part)
    tall = (RADIX, 2, side_len, part)
    scratch = [
        (wide, jnp.bfloat16),
        (tall, jnp.bfloat16),
        (wide, jnp.bfloat16),
        (wide, jnp.float32),
        (tall, jnp.bfloat16),
    ]
    return pl.pallas_call(
        solve_kernel,
        out_shape=pltpu.VMEM(grown.shape, grown.dtype),
        in_specs=[smem, smem] + [vmem] * len(prepared),
        out_specs=vmem,
        scratch_shapes=[pltpu.VMEM(*each) for each in scratch],
        input_output_aliases={1 + len(prepared): 0},
        compiler_params=pltpu.CompilerParams(vmem_limit_bytes=limit),
    )(live_counts, shifts, *prepared)


def shards(axes, object_slab, probe_field, intensities, offsets, live_count):
    tables = residue_tables(probe_field.shape[-1])
    shifts = offsets[0, 0].T
    prepared, limit = gather(axes, shifts, object_slab, intensities[0, 0], probe_field, tables)
    grown = solve(live_count.T, shifts, prepared, limit)
    return scatter(axes, grown, object_slab.shape[1])


def solution(mesh):
    placed = (
        P(None, "tile", "scan"),
        P(),
        P("scan", "tile", None, None, None),
        P("scan", "tile", None, None),
        P(None, "tile"),
    )
    axes = tuple((name, mesh.shape[name]) for name in ("scan", "tile"))
    return jax.shard_map(
        functools.partial(shards, axes), mesh=mesh, in_specs=placed, out_specs=P(None, "tile", "scan"), check_vma=False
    )
```

```python
import functools
import math

import jax
import jax.numpy as jnp
import numpy as np
from jax import lax
from jax.experimental import pallas as pl
from jax.experimental.pallas import tpu as pltpu
from jax.sharding import PartitionSpec as P

RADIX = 4
LANES = 128
GROUP = 16


def residue_tables(side_len):
    part = side_len // RADIX
    freq = np.arange(side_len).reshape(part, RADIX).T
    across = np.arange(part)
    phase = (freq[:, :, None] * across[None, None, :] % side_len) * (2.0 * math.pi / side_len)
    factor = 1.0 / math.sqrt(side_len)
    cos = np.cos(phase) * factor
    sin = np.sin(phase) * factor
    rows = np.concatenate(
        [np.concatenate([cos, sin], axis=2), np.concatenate([-sin, cos], axis=2)], axis=1
    ).astype(np.float32)
    return jnp.asarray(rows, jnp.bfloat16), jnp.asarray(rows.swapaxes(1, 2), jnp.bfloat16)


def sorted_by_residue(side_len):
    at = np.arange(side_len)
    source = at % (side_len // RADIX) * RADIX + at // (side_len // RADIX)
    sort = (source[:, None] == at[None, :]).astype(np.float32)
    return jnp.asarray(sort, jnp.bfloat16), jnp.asarray(sort.T, jnp.bfloat16)


def dot(a, b):
    return jnp.dot(a, b, preferred_element_type=jnp.float32)


def butterfly(parts, sign):
    (r0, i0), (r1, i1), (r2, i2), (r3, i3) = parts
    ar, ai, br, bi = r0 + r2, i0 + i2, r1 + r3, i1 + i3
    cr, ci, dr, di = r0 - r2, i0 - i2, r1 - r3, i1 - i3
    plus = (cr - di, ci + dr)
    minus = (cr + di, ci - dr)
    first, third = (plus, minus) if sign > 0 else (minus, plus)
    return [(ar + br, ai + bi), first, (ar - br, ai - bi), third]


def neighbours(axes):
    result = []
    for name, count in axes:
        me = lax.axis_index(name)
        result.append((me > 0, {name: me - 1}, me < count - 1, {name: me + 1}))
    return result


def greet(peers):
    barrier = pltpu.get_barrier_semaphore()
    for has_low, low, has_high, high in peers:
        for there, peer in ((has_low, low), (has_high, high)):

            @pl.when(there)
            def _(peer=peer):
                pl.semaphore_signal(
                    barrier, inc=1, device_id=peer, device_id_type=pl.DeviceIdType.MESH
                )


def all_here(peers):
    count = sum(
        there.astype(jnp.int32) for has_low, _, has_high, _ in peers for there in (has_low, has_high)
    )
    pl.semaphore_wait(pltpu.get_barrier_semaphore(), count)


def remote(source, target, sends, receives, index, peer):
    return pltpu.make_async_remote_copy(
        src_ref=source,
        dst_ref=target,
        send_sem=sends.at[index],
        recv_sem=receives.at[index],
        device_id=peer,
        device_id_type=pl.DeviceIdType.MESH,
    )


def quarter_turns(cos, sin, q):
    return ((cos, sin), (sin, -cos), (-cos, -sin), (-sin, cos))[q]


def in_place(mask, cos, sin, q):
    wrapped = quarter_turns(cos, sin, q)
    return jnp.where(mask, cos, wrapped[0]), jnp.where(mask, sin, wrapped[1])


def gather_kernel(
    axes,
    shift_ref,
    own_hbm,
    measured_hbm,
    probe_hbm,
    rows_hbm,
    cols_hbm,
    sort_hbm,
    unsort_hbm,
    field,
    probes,
    tables,
    arranged,
    grown,
    own,
    measured,
    extended,
    rows_ref,
    cols_ref,
    doubled,
    sort,
    unsort,
    sends,
    receives,
    fetches,
    freed,
):
    slots, side_len = measured.shape[:2]
    tile_len = own.shape[1]
    part = side_len // RADIX
    own_blocks = tile_len // LANES
    side_blocks = side_len // LANES
    scan, tile = neighbours(axes)
    has_left, left, has_right, _ = scan
    has_up, up, has_down, down = tile
    greet((scan, tile))
    firsts = [
        pltpu.make_async_copy(
            own_hbm.at[c, :side_len, :side_len],
            own.at[c, :side_len, :side_len],
            fetches.at[4 * c],
        )
        for c in range(2)
    ]
    second = pltpu.make_async_copy(
        own_hbm.at[:, side_len:, :side_len], own.at[:, side_len:, :side_len], fetches.at[1]
    )
    third = pltpu.make_async_copy(
        own_hbm.at[:, :side_len, side_len:], own.at[:, :side_len, side_len:], fetches.at[2]
    )
    fourth = pltpu.make_async_copy(
        own_hbm.at[:, side_len:, side_len:], own.at[:, side_len:, side_len:], fetches.at[3]
    )
    constants = [
        pltpu.make_async_copy(source, target, fetches.at[5 + i])
        for i, (source, target) in enumerate(
            (
                (sort_hbm, sort),
                (unsort_hbm, unsort),
                (measured_hbm, measured),
                (rows_hbm, rows_ref),
                (cols_hbm, cols_ref),
            )
        )
    ]
    for c in range(2):
        for b in range(side_blocks):
            cols = slice(b * LANES, (b + 1) * LANES)
            for source, target in (
                (probe_hbm.at[c, :, cols], extended.at[c, b, GROUP:, :]),
                (probe_hbm.at[c, side_len - GROUP :, cols], extended.at[c, b, :GROUP, :]),
            ):
                constants.append(
                    pltpu.make_async_copy(source, target, fetches.at[5 + len(constants)])
                )
    for load in firsts + [third, second, fourth] + constants:
        load.start()
    near = slice(0, side_blocks)
    far = slice(own_blocks, own_blocks + side_blocks)
    halves = [
        (c, slice(at, at + side_blocks // 2))
        for c in range(2)
        for at in range(0, side_blocks, side_blocks // 2)
    ]

    def moved(blocks):
        return slice(blocks.start + own_blocks, blocks.stop + own_blocks)

    tops = [
        remote(
            field.at[c, blocks, :side_len, :],
            field.at[c, moved(blocks), :side_len, :],
            sends,
            receives,
            3 + i,
            left,
        )
        for i, (c, blocks) in enumerate(halves)
    ]
    rests = [
        remote(
            field.at[c, near, side_len:tile_len, :],
            field.at[c, far, side_len:tile_len, :],
            sends,
            receives,
            c,
            left,
        )
        for c in range(2)
    ]
    unders = [
        remote(
            field.at[:, blocks, :side_len, :],
            field.at[:, blocks, tile_len:, :],
            sends,
            receives,
            index,
            up,
        )
        for blocks, index in (
            (near, 2),
            (slice(side_blocks, own_blocks), 3 + 2 * len(halves)),
        )
    ]
    acrosses = [
        remote(
            field.at[c, moved(blocks), :side_len, :],
            field.at[c, moved(blocks), tile_len:, :],
            sends,
            receives,
            3 + len(halves) + i,
            up,
        )
        for i, (c, blocks) in enumerate(halves)
    ]

    def narrow(blocks, at, planes=range(2)):
        for c in planes:
            for b in blocks:
                field[c, b, at, :] = own[c, at, b * LANES : (b + 1) * LANES].astype(jnp.bfloat16)

    firsts[0].wait()
    narrow(range(side_blocks), slice(0, side_len), range(1))
    all_here((scan, tile))

    @pl.when(has_left)
    def _():
        for each in tops[:2]:
            each.start()

    firsts[1].wait()
    narrow(range(side_blocks), slice(0, side_len), range(1, 2))

    @pl.when(has_left)
    def _():
        for each in tops[2:]:
            each.start()

    @pl.when(has_up)
    def _():
        unders[0].start()

    third.wait()
    narrow(range(side_blocks, own_blocks), slice(0, side_len))

    @pl.when(has_up)
    def _():
        unders[1].start()

    second.wait()
    narrow(range(side_blocks), slice(side_len, tile_len))

    odd = lax.rem(lax.axis_index(axes[1][0]), 2) == 1
    first_turn = jnp.logical_and(has_left, jnp.logical_not(odd))
    second_turn = jnp.logical_and(has_left, odd)

    @pl.when(first_turn)
    def _():
        for each in rests:
            each.start()

    @pl.when(jnp.logical_not(has_right))
    def _():
        field[:, far, :tile_len, :] = jnp.zeros(
            (2, side_blocks, tile_len, LANES), jnp.bfloat16
        )

    @pl.when(jnp.logical_not(has_down))
    def _():
        field[:, :, tile_len:, :] = jnp.zeros(
            (2, own_blocks + side_blocks, side_len, LANES), jnp.bfloat16
        )

    fourth.wait()
    narrow(range(side_blocks, own_blocks), slice(side_len, tile_len))
    for load in constants:
        load.wait()

    def sort_slot(slot, carry):
        rows = dot(sort[...], measured[slot]).astype(jnp.bfloat16)
        both = dot(rows, unsort[...]).astype(jnp.bfloat16)
        for b in range(RADIX):
            arranged[slot, b] = both[:, b * part : (b + 1) * part]
        return carry

    lax.fori_loop(0, slots, sort_slot, 0)

    grown[...] = jnp.zeros_like(grown)
    for q in range(RADIX):
        for i in range(2):
            for at in (0, part):
                doubled[q, i, at : at + part, :] = cols_ref[
                    q, i * part : (i + 1) * part, :part
                ].astype(jnp.float32)

    lane = lax.broadcasted_iota(jnp.int32, (1, LANES), 1)
    line = lax.broadcasted_iota(jnp.int32, (part, LANES), 0)
    chunk = 32

    def prepare(slot, carry):
        lift = lax.rem(shift_ref[0, slot], GROUP)
        turn = lax.rem(shift_ref[1, slot], LANES)

        def move_probe(i, carry):
            at = pl.multiple_of(i * chunk, chunk)
            for c in range(2):
                turned = [
                    pltpu.roll(extended[c, b, pl.ds(GROUP - lift + at, chunk), :], turn, 1)
                    for b in range(side_blocks)
                ]
                for b in range(side_blocks):
                    probes[slot, c, b, pl.ds(at, chunk), :] = jnp.where(
                        lane >= turn, turned[b], turned[b - 1]
                    )
            return carry

        lax.fori_loop(0, side_len // chunk, move_probe, 0)
        for k, by in enumerate((lift, turn)):
            for q in range(RADIX):
                cos = pltpu.roll(rows_ref[q, :part, :part].astype(jnp.float32), by, 1)
                sin = pltpu.roll(rows_ref[q, :part, part:].astype(jnp.float32), by, 1)
                cos, sin = in_place(lane >= by, cos, sin, q)
                tables[slot, 0, k, q, 0, :part, :] = cos.astype(jnp.bfloat16)
                tables[slot, 0, k, q, 1, :part, :] = sin.astype(jnp.bfloat16)
                tables[slot, 0, k, q, 0, part:, :] = (-sin).astype(jnp.bfloat16)
                tables[slot, 0, k, q, 1, part:, :] = cos.astype(jnp.bfloat16)
                cos = doubled[q, 0, pl.ds(part - by, part), :]
                sin = doubled[q, 1, pl.ds(part - by, part), :]
                cos, sin = in_place(line >= by, cos, sin, q)
                tables[slot, 1, k, q, 0, :part, :] = cos.astype(jnp.bfloat16)
                tables[slot, 1, k, q, 1, :part, :] = (-sin).astype(jnp.bfloat16)
                tables[slot, 1, k, q, 0, part:, :] = sin.astype(jnp.bfloat16)
                tables[slot, 1, k, q, 1, part:, :] = cos.astype(jnp.bfloat16)
        return carry

    lax.fori_loop(0, slots, prepare, 0)

    for top, across in zip(tops, acrosses):

        @pl.when(has_right)
        def _(top=top):
            top.wait_recv()

        @pl.when(has_up)
        def _(across=across):
            across.start()

    @pl.when(first_turn)
    def _():
        for each in tops + rests:
            each.wait_send()

    @pl.when(jnp.logical_and(first_turn, has_down))
    def _():
        pl.semaphore_signal(
            freed, inc=1, device_id=down, device_id_type=pl.DeviceIdType.MESH
        )

    @pl.when(second_turn)
    def _():
        pl.semaphore_wait(freed, 1)
        for each in rests:
            each.start()


    @pl.when(has_down)
    def _():
        for each in unders:
            each.wait_recv()

    @pl.when(has_right)
    def _():
        for each in rests:
            each.wait_recv()

    @pl.when(has_down)
    def _():
        for each in acrosses:
            each.wait_recv()

    @pl.when(second_turn)
    def _():
        for each in tops + rests:
            each.wait_send()

    @pl.when(has_up)
    def _():
        for each in unders:
            each.wait_send()
        for each in acrosses:
            each.wait_send()


def gather(axes, shifts, own, measured, probe, tables):
    slots, side_len = measured.shape[:2]
    tile_len = own.shape[1]
    span = tile_len + side_len
    part = side_len // RADIX
    side_blocks = side_len // LANES
    hbm = pl.BlockSpec(memory_space=pltpu.HBM)
    vmem = pl.BlockSpec(memory_space=pltpu.VMEM)
    table = (slots, 2, 2, RADIX, 2, 2 * part, part)
    scratch = [
        (own.shape, jnp.float32),
        (measured.shape, jnp.bfloat16),
        ((2, side_blocks, side_len + GROUP, LANES), jnp.float32),
        (tables[0].shape, jnp.bfloat16),
        (tables[1].shape, jnp.bfloat16),
        ((RADIX, 2, 2 * part, part), jnp.float32),
        ((side_len, side_len), jnp.bfloat16),
        ((side_len, side_len), jnp.bfloat16),
    ]
    call = pl.pallas_call(
        functools.partial(gather_kernel, axes),
        out_shape=[
            pltpu.VMEM((2, span // LANES, span, LANES), jnp.bfloat16),
            pltpu.VMEM((slots, 2, side_blocks, side_len, LANES), jnp.float32),
            pltpu.VMEM(table, jnp.bfloat16),
            pltpu.VMEM((slots, RADIX, side_len, part), jnp.bfloat16),
            pltpu.VMEM((2, span // LANES, span, LANES), jnp.float32),
        ],
        in_specs=[pl.BlockSpec(memory_space=pltpu.SMEM)] + [hbm] * 7,
        out_specs=[vmem] * 5,
        scratch_shapes=[pltpu.VMEM(*each) for each in scratch]
        + [
            pltpu.SemaphoreType.DMA((4 + 8,)),
            pltpu.SemaphoreType.DMA((4 + 8,)),
            pltpu.SemaphoreType.DMA((10 + 4 * side_blocks,)),
            pltpu.SemaphoreType.REGULAR,
        ],
        compiler_params=pltpu.CompilerParams(
            collective_id=0, has_side_effects=True, vmem_limit_bytes=room(scratch)
        ),
    )
    prepared = call(shifts, own, measured, probe, *tables, *sorted_by_residue(side_len))
    held = [pltpu.with_memory_space_constraint(each, pltpu.VMEM) for each in prepared]
    return held, room(scratch)


def room(scratch):
    return sum(math.prod(shape) * jnp.dtype(kind).itemsize for shape, kind in scratch) + (1 << 20)


def scatter_kernel(
    axes,
    grown,
    total,
    from_left,
    spill,
    dropped,
    both,
    landed,
    from_up,
    sends,
    receives,
    ready,
):
    side_len = landed.shape[2]
    tile_len = total.shape[1]
    own_blocks = tile_len // LANES
    side_blocks = side_len // LANES
    scan, tile = neighbours(axes)
    has_left, left, has_right, right = scan
    has_up, up, has_down, down = tile
    odd = lax.rem(lax.axis_index(axes[1][0]), 2) == 1
    even = jnp.logical_not(odd)
    barrier = pltpu.get_barrier_semaphore()

    def tell(there, sem, peer):
        @pl.when(there)
        def _():
            pl.semaphore_signal(
                sem, inc=1, device_id=peer, device_id_type=pl.DeviceIdType.MESH
            )

    tell(has_left, barrier, left)
    tell(jnp.logical_and(even, has_up), barrier, up)
    tell(jnp.logical_and(even, has_down), barrier, down)
    corner = remote(both, landed, sends, receives, 0, down)
    under = remote(dropped, from_up, sends, receives, 1, down)
    rest = remote(
        spill.at[:, :, side_len:, :], from_left.at[:, :, side_len:, :], sends, receives, 2, right
    )
    top = remote(
        spill.at[:, :, :side_len, :], from_left.at[:, :, :side_len, :], sends, receives, 3, right
    )
    spill[:, :, side_len:, :] = grown[:, own_blocks:, side_len:tile_len, :].astype(jnp.bfloat16)
    from_even = has_up.astype(jnp.int32) + has_down.astype(jnp.int32)
    awaited = has_right.astype(jnp.int32) + jnp.where(odd, from_even, 0)

    @pl.when(awaited > 0)
    def _():
        pl.semaphore_wait(barrier, awaited)

    @pl.when(has_right)
    def _():
        rest.start()

    tell(odd, ready, up)

    both[...] = grown[:, own_blocks:, tile_len:, :].astype(jnp.bfloat16)

    @pl.when(jnp.logical_and(odd, has_down))
    def _():
        corner.start()

    @pl.when(jnp.logical_not(has_up))
    def _():
        spill[:, :, :side_len, :] = grown[:, own_blocks:, :side_len, :].astype(jnp.bfloat16)

    @pl.when(jnp.logical_and(jnp.logical_not(has_up), has_right))
    def _():
        top.start()

    dropped[...] = grown[:, :own_blocks, tile_len:, :].astype(jnp.bfloat16)

    @pl.when(jnp.logical_and(odd, has_down))
    def _():
        under.start()

    for c in range(2):
        for b in range(own_blocks):
            total[c, :, b * LANES : (b + 1) * LANES] = grown[c, b, :tile_len, :]

    @pl.when(jnp.logical_and(even, has_down))
    def _():
        pl.semaphore_wait(ready, 1)
        corner.start()
        under.start()

    @pl.when(has_up)
    def _():
        corner.wait_recv()
        spill[:, :, :side_len, :] = (
            grown[:, own_blocks:, :side_len, :] + landed[...].astype(jnp.float32)
        ).astype(jnp.bfloat16)

    @pl.when(jnp.logical_and(has_up, has_right))
    def _():
        top.start()

    def add(blocks, at, source):
        for c in range(2):
            for b in blocks:
                total[c, at, b * LANES : (b + 1) * LANES] += source[c, b, at, :].astype(jnp.float32)

    @pl.when(has_left)
    def _():
        rest.wait_recv()
        add(range(side_blocks), slice(side_len, tile_len), from_left)

    @pl.when(has_up)
    def _():
        under.wait_recv()
        add(range(own_blocks), slice(0, side_len), from_up)

    @pl.when(has_left)
    def _():
        top.wait_recv()

    @pl.when(jnp.logical_not(has_left))
    def _():
        from_left[:, :, :side_len, :] = jnp.zeros(
            (2, side_blocks, side_len, LANES), jnp.bfloat16
        )

    @pl.when(has_right)
    def _():
        rest.wait_send()
        top.wait_send()

    @pl.when(has_down)
    def _():
        corner.wait_send()
        under.wait_send()


def scatter(axes, grown, tile_len):
    span = grown.shape[2]
    side_len = span - tile_len
    own_blocks = tile_len // LANES
    side_blocks = side_len // LANES
    vmem = pl.BlockSpec(memory_space=pltpu.VMEM)
    scratch = [
        ((2, side_blocks, tile_len, LANES), jnp.bfloat16),
        ((2, own_blocks, side_len, LANES), jnp.bfloat16),
        ((2, side_blocks, side_len, LANES), jnp.bfloat16),
        ((2, side_blocks, side_len, LANES), jnp.bfloat16),
        ((2, own_blocks, side_len, LANES), jnp.bfloat16),
    ]
    summed = pl.pallas_call(
        functools.partial(scatter_kernel, axes),
        out_shape=[
            pltpu.VMEM((2, tile_len, tile_len), jnp.float32),
            pltpu.VMEM((2, side_blocks, tile_len, LANES), jnp.bfloat16),
        ],
        in_specs=[vmem],
        out_specs=[vmem] * 2,
        scratch_shapes=[pltpu.VMEM(*each) for each in scratch]
        + [
            pltpu.SemaphoreType.DMA((4,)),
            pltpu.SemaphoreType.DMA((4,)),
            pltpu.SemaphoreType.REGULAR,
        ],
        compiler_params=pltpu.CompilerParams(
            collective_id=1, has_side_effects=True, vmem_limit_bytes=room(scratch)
        ),
    )(grown)
    held = [pltpu.with_memory_space_constraint(each, pltpu.VMEM) for each in summed]
    return pl.pallas_call(
        finish_kernel,
        out_shape=jax.ShapeDtypeStruct((2, tile_len, tile_len), jnp.float32),
        in_specs=[vmem] * 2,
        out_specs=pl.BlockSpec(memory_space=pltpu.HBM),
        scratch_shapes=[
            pltpu.VMEM((2, side_len, side_len), jnp.float32),
            pltpu.SemaphoreType.DMA((2, 3)),
        ],
        compiler_params=pltpu.CompilerParams(vmem_limit_bytes=room(scratch)),
    )(*held)


def finish_kernel(total, from_left, out_hbm, head, puts):
    side_len = head.shape[1]
    copies = []
    for c in range(2):
        for i, at in enumerate(
            (
                (c, slice(side_len, None), slice(None)),
                (c, slice(0, side_len), slice(side_len, None)),
            )
        ):
            copies.append(pltpu.make_async_copy(total.at[at], out_hbm.at[at], puts.at[c, i]))
    for copy in copies:
        copy.start()
    for c in range(2):
        for b in range(side_len // LANES):
            cols = slice(b * LANES, (b + 1) * LANES)
            head[c, :, cols] = total[c, :side_len, cols] + from_left[c, b, :side_len, :].astype(
                jnp.float32
            )
        at = (c, slice(0, side_len), slice(0, side_len))
        copies.append(pltpu.make_async_copy(head.at[c], out_hbm.at[at], puts.at[c, 2]))
        copies[-1].start()
    for copy in copies:
        copy.wait()


def side_by_side(*blocks):
    return jnp.concatenate(blocks, axis=1)


def solve_kernel(
    live_ref,
    shift_ref,
    field,
    probes,
    tables,
    measured,
    zeros,
    grown,
    mixed,
    halves,
    misfits,
    spectra,
    backs,
    fence,
):
    side_len = probes.shape[3]
    part = side_len // RADIX
    side_blocks = side_len // LANES
    lane = lax.broadcasted_iota(jnp.int32, (1, LANES), 1)
    line = lax.broadcasted_iota(jnp.int32, (GROUP, LANES), 0)

    def one_slot(slot, carry):
        row = shift_ref[0, slot]
        col = shift_ref[1, slot]
        lift = lax.rem(row, GROUP)
        turn = lax.rem(col, LANES)
        base = pl.multiple_of(row - lift, GROUP)
        block = lax.div(col, LANES)
        stay = lane >= turn
        below = line >= lift

        def table(side, kind, q):
            return side_by_side(tables[slot, side, kind, q, 0], tables[slot, side, kind, q, 1])

        def piece(c, b, at):
            def cut(b):
                start = pl.multiple_of(base + at, GROUP)
                value = field[c, block + b, pl.ds(start, GROUP), :]
                if at == 0:
                    start = pl.multiple_of(base + side_len, GROUP)
                    wrapped = field[c, block + b, pl.ds(start, GROUP), :]
                    value = jnp.where(below, value, wrapped)
                return value

            value = cut(b) if b else jnp.where(stay, cut(0), cut(side_blocks))
            return value.astype(jnp.float32)

        def exit_waves(blocks):
            for at in range(0, part, GROUP):
                for b in blocks:
                    waves = []
                    for p in range(RADIX):
                        here = at + p * part
                        re, im = piece(0, b, here), piece(1, b, here)
                        probe_re = probes[slot, 0, b, here : here + GROUP, :]
                        probe_im = probes[slot, 1, b, here : here + GROUP, :]
                        waves.append((probe_re * re - probe_im * im, probe_re * im + probe_im * re))
                    for q, (re, im) in enumerate(butterfly(waves, -1)):
                        mixed[q, b, at : at + GROUP, :] = re.astype(jnp.bfloat16)
                        mixed[q, b, at + part : at + part + GROUP, :] = im.astype(jnp.bfloat16)

        def split(value):
            return [
                (value[:part, at : at + part], value[part:, at : at + part])
                for at in range(0, value.shape[1], part)
            ]

        def left(q, blocks):
            return split(dot(table(0, 0, q), side_by_side(*(mixed[q, b] for b in blocks))))

        def far_field(other):
            return dot(side_by_side(halves[other, 0], halves[other, 1]), table(1, 1, other))

        def misfit_of(other, far):
            for q in range(RADIX):
                rows = slice(q * part, (q + 1) * part)
                far_re, far_im = far[rows, :part], far[rows, part:]
                seen = measured[slot, other, rows, :].astype(jnp.float32)
                misfit = far_re * far_re + far_im * far_im - seen
                misfits[q, other, :part, :] = (misfit * far_re).astype(jnp.bfloat16)
                misfits[q, other, part:, :] = (misfit * far_im).astype(jnp.bfloat16)

        def left_back(q, pair):
            mixture = dot(table(1, 0, q), side_by_side(*(misfits[q, other] for other in pair)))
            for i, other in enumerate(pair):
                spectra[q, other] = mixture[:, i * part : (i + 1) * part]

        def mix(ats, pair):
            for at in ats:
                for other in pair:
                    parts = [
                        (
                            spectra[q, other, at : at + GROUP, :],
                            spectra[q, other, part + at : part + at + GROUP, :],
                        )
                        for q in range(RADIX)
                    ]
                    for p, (re, im) in enumerate(butterfly(parts, 1)):
                        here = slice(at + p * part, at + p * part + GROUP)
                        backs[other, 0, here, :] = re.astype(jnp.bfloat16)
                        backs[other, 1, here, :] = im.astype(jnp.bfloat16)

        def add(c, b, at, value, mask=None):
            where = pl.ds(pl.multiple_of(base + at, GROUP), value.shape[0])
            if mask is None:
                grown[c, block + b, where, :] += value
            else:
                spot = grown.at[c, block + b, where, :]
                mask = jnp.broadcast_to(mask, value.shape)
                pltpu.store(spot, spot[...] + value, mask=mask)

        def add_wrapped(c, b, at, value, mask=None):
            if at == 0:
                add(c, b, 0, jnp.where(below, value[:GROUP], 0.0), mask)
                add(c, b, side_len, jnp.where(below, 0.0, value[:GROUP]), mask)
                add(c, b, GROUP, value[GROUP:], mask)
            else:
                add(c, b, at, value, mask)

        def right_back(at, tall):
            parts = []
            for other in range(RADIX):
                back = jnp.concatenate(
                    [
                        side_by_side(
                            backs[other, 0, here : here + tall, :],
                            backs[other, 1, here : here + tall, :],
                        )
                        for here in range(at, side_len, part)
                    ],
                    axis=0,
                )
                grad = dot(back, table(0, 1, other))
                parts.append((grad[:, :part], grad[:, part:]))
            return parts

        def accumulate(at, tall, parts):
            for p in range(RADIX):
                here = at + p * part
                rows = slice(p * tall, (p + 1) * tall)
                some = [(re[rows], im[rows]) for re, im in parts]
                for b, (re, im) in enumerate(butterfly(some, 1)):
                    probe_re = probes[slot, 0, b, here : here + tall, :]
                    probe_im = probes[slot, 1, b, here : here + tall, :]
                    values = (probe_re * re + probe_im * im, probe_re * im - probe_im * re)
                    for c, value in enumerate(values):
                        if b == 0:
                            add_wrapped(c, 0, here, value, stay)
                            add_wrapped(c, side_blocks, here, value, jnp.logical_not(stay))
                        else:
                            add_wrapped(c, b, here, value)

        exit_waves((0, 2))
        exit_waves((1, 3))
        pl.semaphore_signal(fence, 1)
        pl.semaphore_wait(fence, 1)
        early = [left(q, (0, 2)) for q in range(RADIX)]
        for q in range(RADIX):
            rows = slice(q * part, (q + 1) * part)
            (r0, r2), (r1, r3) = early[q], left(q, (1, 3))
            for other, (re, im) in enumerate(butterfly([r0, r1, r2, r3], -1)):
                halves[other, 0, rows, :] = re.astype(jnp.bfloat16)
                halves[other, 1, rows, :] = im.astype(jnp.bfloat16)
        ahead = far_field(0)
        for other in range(RADIX):
            far = ahead
            if other + 1 < RADIX:
                ahead = far_field(other + 1)
            misfit_of(other, far)
            if other == 2:
                for q in range(RADIX):
                    left_back(q, (0, 1))
        tall = part // 2
        ats = [range(at, at + tall, GROUP) for at in range(0, part, tall)]
        for q in range(RADIX):
            left_back(q, (2, 3))
        mix(ats[0], range(RADIX))
        mix(ats[1], range(RADIX))
        first = right_back(0, tall)
        second = right_back(tall, tall)
        accumulate(0, tall, first)
        accumulate(tall, tall, second)
        return carry

    lax.fori_loop(0, live_ref[0, lax.axis_index("scan")], one_slot, 0)


def solve(live_counts, shifts, prepared, limit):
    grown = prepared[-1]
    side_len = prepared[1].shape[3]
    part = side_len // RADIX
    smem = pl.BlockSpec(memory_space=pltpu.SMEM)
    vmem = pl.BlockSpec(memory_space=pltpu.VMEM)
    wide = (RADIX, RADIX, 2 * part, part)
    tall = (RADIX, 2, side_len, part)
    scratch = [
        (wide, jnp.bfloat16),
        (tall, jnp.bfloat16),
        (wide, jnp.bfloat16),
        (wide, jnp.float32),
        (tall, jnp.bfloat16),
    ]
    return pl.pallas_call(
        solve_kernel,
        out_shape=pltpu.VMEM(grown.shape, grown.dtype),
        in_specs=[smem, smem] + [vmem] * len(prepared),
        out_specs=vmem,
        scratch_shapes=[pltpu.VMEM(*each) for each in scratch] + [pltpu.SemaphoreType.REGULAR],
        input_output_aliases={1 + len(prepared): 0},
        compiler_params=pltpu.CompilerParams(vmem_limit_bytes=limit),
    )(live_counts, shifts, *prepared)


def shards(axes, object_slab, probe_field, intensities, offsets, live_count):
    tables = residue_tables(probe_field.shape[-1])
    shifts = offsets[0, 0].T
    prepared, limit = gather(axes, shifts, object_slab, intensities[0, 0], probe_field, tables)
    grown = solve(live_count.T, shifts, prepared, limit)
    return scatter(axes, grown, object_slab.shape[1])


def solution(mesh):
    placed = (
        P(None, "tile", "scan"),
        P(),
        P("scan", "tile", None, None, None),
        P("scan", "tile", None, None),
        P(None, "tile"),
    )
    axes = tuple((name, mesh.shape[name]) for name in ("scan", "tile"))
    return jax.shard_map(
        functools.partial(shards, axes), mesh=mesh, in_specs=placed, out_specs=P(None, "tile", "scan"), check_vma=False
    )
```

```python
import functools
import math

import jax
import jax.numpy as jnp
import numpy as np
from jax import lax
from jax.experimental import pallas as pl
from jax.experimental.pallas import tpu as pltpu
from jax.sharding import PartitionSpec as P

RADIX = 4
LANES = 128
GROUP = 16


def residue_tables(side_len):
    part = side_len // RADIX
    freq = np.arange(side_len).reshape(part, RADIX).T
    across = np.arange(part)
    phase = (freq[:, :, None] * across[None, None, :] % side_len) * (2.0 * math.pi / side_len)
    factor = 1.0 / math.sqrt(side_len)
    cos = np.cos(phase) * factor
    sin = np.sin(phase) * factor
    rows = np.concatenate(
        [np.concatenate([cos, sin], axis=2), np.concatenate([-sin, cos], axis=2)], axis=1
    ).astype(np.float32)
    return jnp.asarray(rows, jnp.bfloat16), jnp.asarray(rows.swapaxes(1, 2), jnp.bfloat16)


def sorted_by_residue(side_len):
    at = np.arange(side_len)
    source = at % (side_len // RADIX) * RADIX + at // (side_len // RADIX)
    sort = (source[:, None] == at[None, :]).astype(np.float32)
    return jnp.asarray(sort, jnp.bfloat16), jnp.asarray(sort.T, jnp.bfloat16)


def dot(a, b):
    return jnp.dot(a, b, preferred_element_type=jnp.float32)


def butterfly(parts, sign):
    (r0, i0), (r1, i1), (r2, i2), (r3, i3) = parts
    ar, ai, br, bi = r0 + r2, i0 + i2, r1 + r3, i1 + i3
    cr, ci, dr, di = r0 - r2, i0 - i2, r1 - r3, i1 - i3
    plus = (cr - di, ci + dr)
    minus = (cr + di, ci - dr)
    first, third = (plus, minus) if sign > 0 else (minus, plus)
    return [(ar + br, ai + bi), first, (ar - br, ai - bi), third]


def neighbours(axes):
    result = []
    for name, count in axes:
        me = lax.axis_index(name)
        result.append((me > 0, {name: me - 1}, me < count - 1, {name: me + 1}))
    return result


def greet(peers):
    barrier = pltpu.get_barrier_semaphore()
    for has_low, low, has_high, high in peers:
        for there, peer in ((has_low, low), (has_high, high)):

            @pl.when(there)
            def _(peer=peer):
                pl.semaphore_signal(
                    barrier, inc=1, device_id=peer, device_id_type=pl.DeviceIdType.MESH
                )


def all_here(peers):
    count = sum(
        there.astype(jnp.int32) for has_low, _, has_high, _ in peers for there in (has_low, has_high)
    )
    pl.semaphore_wait(pltpu.get_barrier_semaphore(), count)


def remote(source, target, sends, receives, index, peer):
    return pltpu.make_async_remote_copy(
        src_ref=source,
        dst_ref=target,
        send_sem=sends.at[index],
        recv_sem=receives.at[index],
        device_id=peer,
        device_id_type=pl.DeviceIdType.MESH,
    )


def quarter_turns(cos, sin, q):
    return ((cos, sin), (sin, -cos), (-cos, -sin), (-sin, cos))[q]


def in_place(mask, cos, sin, q):
    wrapped = quarter_turns(cos, sin, q)
    return jnp.where(mask, cos, wrapped[0]), jnp.where(mask, sin, wrapped[1])


def gather_kernel(
    axes,
    shift_ref,
    own_hbm,
    measured_hbm,
    probe_hbm,
    rows_hbm,
    cols_hbm,
    sort_hbm,
    unsort_hbm,
    field,
    probes,
    tables,
    arranged,
    grown,
    own,
    measured,
    extended,
    rows_ref,
    cols_ref,
    doubled,
    sort,
    unsort,
    sends,
    receives,
    fetches,
    freed,
):
    slots, side_len = measured.shape[:2]
    tile_len = own.shape[1]
    part = side_len // RADIX
    own_blocks = tile_len // LANES
    side_blocks = side_len // LANES
    scan, tile = neighbours(axes)
    has_left, left, has_right, _ = scan
    has_up, up, has_down, down = tile
    greet((scan, tile))
    firsts = [
        pltpu.make_async_copy(
            own_hbm.at[c, :side_len, :side_len],
            own.at[c, :side_len, :side_len],
            fetches.at[4 * c],
        )
        for c in range(2)
    ]
    second = pltpu.make_async_copy(
        own_hbm.at[:, side_len:, :side_len], own.at[:, side_len:, :side_len], fetches.at[1]
    )
    third = pltpu.make_async_copy(
        own_hbm.at[:, :side_len, side_len:], own.at[:, :side_len, side_len:], fetches.at[2]
    )
    fourth = pltpu.make_async_copy(
        own_hbm.at[:, side_len:, side_len:], own.at[:, side_len:, side_len:], fetches.at[3]
    )
    constants = [
        pltpu.make_async_copy(source, target, fetches.at[5 + i])
        for i, (source, target) in enumerate(
            (
                (sort_hbm, sort),
                (unsort_hbm, unsort),
                (measured_hbm, measured),
                (rows_hbm, rows_ref),
                (cols_hbm, cols_ref),
            )
        )
    ]
    for c in range(2):
        for b in range(side_blocks):
            cols = slice(b * LANES, (b + 1) * LANES)
            for source, target in (
                (probe_hbm.at[c, :, cols], extended.at[c, b, GROUP:, :]),
                (probe_hbm.at[c, side_len - GROUP :, cols], extended.at[c, b, :GROUP, :]),
            ):
                constants.append(
                    pltpu.make_async_copy(source, target, fetches.at[5 + len(constants)])
                )
    for load in firsts + [third, second, fourth] + constants:
        load.start()
    near = slice(0, side_blocks)
    far = slice(own_blocks, own_blocks + side_blocks)
    halves = [
        (c, slice(at, at + side_blocks // 2))
        for c in range(2)
        for at in range(0, side_blocks, side_blocks // 2)
    ]

    def moved(blocks):
        return slice(blocks.start + own_blocks, blocks.stop + own_blocks)

    tops = [
        remote(
            field.at[c, blocks, :side_len, :],
            field.at[c, moved(blocks), :side_len, :],
            sends,
            receives,
            3 + i,
            left,
        )
        for i, (c, blocks) in enumerate(halves)
    ]
    rests = [
        remote(
            field.at[c, near, side_len:tile_len, :],
            field.at[c, far, side_len:tile_len, :],
            sends,
            receives,
            c,
            left,
        )
        for c in range(2)
    ]
    unders = [
        remote(
            field.at[:, blocks, :side_len, :],
            field.at[:, blocks, tile_len:, :],
            sends,
            receives,
            index,
            up,
        )
        for blocks, index in (
            (near, 2),
            (slice(side_blocks, own_blocks), 3 + 2 * len(halves)),
        )
    ]
    acrosses = [
        remote(
            field.at[c, moved(blocks), :side_len, :],
            field.at[c, moved(blocks), tile_len:, :],
            sends,
            receives,
            3 + len(halves) + i,
            up,
        )
        for i, (c, blocks) in enumerate(halves)
    ]

    def narrow(blocks, at, planes=range(2)):
        for c in planes:
            for b in blocks:
                field[c, b, at, :] = own[c, at, b * LANES : (b + 1) * LANES].astype(jnp.bfloat16)

    firsts[0].wait()
    narrow(range(side_blocks), slice(0, side_len), range(1))
    all_here((scan, tile))

    @pl.when(has_left)
    def _():
        for each in tops[:2]:
            each.start()

    firsts[1].wait()
    narrow(range(side_blocks), slice(0, side_len), range(1, 2))

    @pl.when(has_left)
    def _():
        for each in tops[2:]:
            each.start()

    @pl.when(has_up)
    def _():
        unders[0].start()

    third.wait()
    narrow(range(side_blocks, own_blocks), slice(0, side_len))

    @pl.when(has_up)
    def _():
        unders[1].start()

    second.wait()
    narrow(range(side_blocks), slice(side_len, tile_len))

    odd = lax.rem(lax.axis_index(axes[1][0]), 2) == 1
    first_turn = jnp.logical_and(has_left, jnp.logical_not(odd))
    second_turn = jnp.logical_and(has_left, odd)

    @pl.when(first_turn)
    def _():
        for each in rests:
            each.start()

    @pl.when(jnp.logical_not(has_right))
    def _():
        field[:, far, :tile_len, :] = jnp.zeros(
            (2, side_blocks, tile_len, LANES), jnp.bfloat16
        )

    @pl.when(jnp.logical_not(has_down))
    def _():
        field[:, :, tile_len:, :] = jnp.zeros(
            (2, own_blocks + side_blocks, side_len, LANES), jnp.bfloat16
        )

    fourth.wait()
    narrow(range(side_blocks, own_blocks), slice(side_len, tile_len))
    for load in constants:
        load.wait()

    def sort_slot(slot, carry):
        rows = dot(sort[...], measured[slot]).astype(jnp.bfloat16)
        both = dot(rows, unsort[...]).astype(jnp.bfloat16)
        for b in range(RADIX):
            arranged[slot, b] = both[:, b * part : (b + 1) * part]
        return carry

    lax.fori_loop(0, slots, sort_slot, 0)

    grown[...] = jnp.zeros_like(grown)
    for q in range(RADIX):
        for i in range(2):
            for at in (0, part):
                doubled[q, i, at : at + part, :] = cols_ref[
                    q, i * part : (i + 1) * part, :part
                ].astype(jnp.float32)

    lane = lax.broadcasted_iota(jnp.int32, (1, LANES), 1)
    line = lax.broadcasted_iota(jnp.int32, (part, LANES), 0)
    chunk = 32

    def prepare(slot, carry):
        lift = lax.rem(shift_ref[0, slot], GROUP)
        turn = lax.rem(shift_ref[1, slot], LANES)

        def move_probe(i, carry):
            at = pl.multiple_of(i * chunk, chunk)
            for c in range(2):
                turned = [
                    pltpu.roll(extended[c, b, pl.ds(GROUP - lift + at, chunk), :], turn, 1)
                    for b in range(side_blocks)
                ]
                for b in range(side_blocks):
                    probes[slot, c, b, pl.ds(at, chunk), :] = jnp.where(
                        lane >= turn, turned[b], turned[b - 1]
                    )
            return carry

        lax.fori_loop(0, side_len // chunk, move_probe, 0)
        for k, by in enumerate((lift, turn)):
            for q in range(RADIX):
                cos = pltpu.roll(rows_ref[q, :part, :part].astype(jnp.float32), by, 1)
                sin = pltpu.roll(rows_ref[q, :part, part:].astype(jnp.float32), by, 1)
                cos, sin = in_place(lane >= by, cos, sin, q)
                tables[slot, 0, k, q, 0, :part, :] = cos.astype(jnp.bfloat16)
                tables[slot, 0, k, q, 1, :part, :] = sin.astype(jnp.bfloat16)
                tables[slot, 0, k, q, 0, part:, :] = (-sin).astype(jnp.bfloat16)
                tables[slot, 0, k, q, 1, part:, :] = cos.astype(jnp.bfloat16)
                cos = doubled[q, 0, pl.ds(part - by, part), :]
                sin = doubled[q, 1, pl.ds(part - by, part), :]
                cos, sin = in_place(line >= by, cos, sin, q)
                tables[slot, 1, k, q, 0, :part, :] = cos.astype(jnp.bfloat16)
                tables[slot, 1, k, q, 1, :part, :] = (-sin).astype(jnp.bfloat16)
                tables[slot, 1, k, q, 0, part:, :] = sin.astype(jnp.bfloat16)
                tables[slot, 1, k, q, 1, part:, :] = cos.astype(jnp.bfloat16)
        return carry

    lax.fori_loop(0, slots, prepare, 0)

    for top, across in zip(tops, acrosses):

        @pl.when(has_right)
        def _(top=top):
            top.wait_recv()

        @pl.when(has_up)
        def _(across=across):
            across.start()

    @pl.when(first_turn)
    def _():
        for each in tops + rests:
            each.wait_send()

    @pl.when(jnp.logical_and(first_turn, has_down))
    def _():
        pl.semaphore_signal(
            freed, inc=1, device_id=down, device_id_type=pl.DeviceIdType.MESH
        )

    @pl.when(second_turn)
    def _():
        pl.semaphore_wait(freed, 1)
        for each in rests:
            each.start()


    @pl.when(has_down)
    def _():
        for each in unders:
            each.wait_recv()

    @pl.when(has_right)
    def _():
        for each in rests:
            each.wait_recv()

    @pl.when(has_down)
    def _():
        for each in acrosses:
            each.wait_recv()

    @pl.when(second_turn)
    def _():
        for each in tops + rests:
            each.wait_send()

    @pl.when(has_up)
    def _():
        for each in unders:
            each.wait_send()
        for each in acrosses:
            each.wait_send()


def gather(axes, shifts, own, measured, probe, tables):
    slots, side_len = measured.shape[:2]
    tile_len = own.shape[1]
    span = tile_len + side_len
    part = side_len // RADIX
    side_blocks = side_len // LANES
    hbm = pl.BlockSpec(memory_space=pltpu.HBM)
    vmem = pl.BlockSpec(memory_space=pltpu.VMEM)
    table = (slots, 2, 2, RADIX, 2, 2 * part, part)
    scratch = [
        (own.shape, jnp.float32),
        (measured.shape, jnp.bfloat16),
        ((2, side_blocks, side_len + GROUP, LANES), jnp.float32),
        (tables[0].shape, jnp.bfloat16),
        (tables[1].shape, jnp.bfloat16),
        ((RADIX, 2, 2 * part, part), jnp.float32),
        ((side_len, side_len), jnp.bfloat16),
        ((side_len, side_len), jnp.bfloat16),
    ]
    call = pl.pallas_call(
        functools.partial(gather_kernel, axes),
        out_shape=[
            pltpu.VMEM((2, span // LANES, span, LANES), jnp.bfloat16),
            pltpu.VMEM((slots, 2, side_blocks, side_len, LANES), jnp.float32),
            pltpu.VMEM(table, jnp.bfloat16),
            pltpu.VMEM((slots, RADIX, side_len, part), jnp.bfloat16),
            pltpu.VMEM((2, span // LANES, span, LANES), jnp.float32),
        ],
        in_specs=[pl.BlockSpec(memory_space=pltpu.SMEM)] + [hbm] * 7,
        out_specs=[vmem] * 5,
        scratch_shapes=[pltpu.VMEM(*each) for each in scratch]
        + [
            pltpu.SemaphoreType.DMA((4 + 8,)),
            pltpu.SemaphoreType.DMA((4 + 8,)),
            pltpu.SemaphoreType.DMA((10 + 4 * side_blocks,)),
            pltpu.SemaphoreType.REGULAR,
        ],
        compiler_params=pltpu.CompilerParams(
            collective_id=0, has_side_effects=True, vmem_limit_bytes=room(scratch)
        ),
    )
    prepared = call(shifts, own, measured, probe, *tables, *sorted_by_residue(side_len))
    held = [pltpu.with_memory_space_constraint(each, pltpu.VMEM) for each in prepared]
    return held, room(scratch)


def room(scratch):
    return sum(math.prod(shape) * jnp.dtype(kind).itemsize for shape, kind in scratch) + (1 << 20)


def scatter_kernel(
    axes,
    grown,
    total,
    from_left,
    spill,
    dropped,
    both,
    landed,
    from_up,
    sends,
    receives,
    ready,
):
    side_len = landed.shape[2]
    tile_len = total.shape[1]
    own_blocks = tile_len // LANES
    side_blocks = side_len // LANES
    scan, tile = neighbours(axes)
    has_left, left, has_right, right = scan
    has_up, up, has_down, down = tile
    odd = lax.rem(lax.axis_index(axes[1][0]), 2) == 1
    even = jnp.logical_not(odd)
    barrier = pltpu.get_barrier_semaphore()

    def tell(there, sem, peer):
        @pl.when(there)
        def _():
            pl.semaphore_signal(
                sem, inc=1, device_id=peer, device_id_type=pl.DeviceIdType.MESH
            )

    tell(has_left, barrier, left)
    tell(jnp.logical_and(even, has_up), barrier, up)
    tell(jnp.logical_and(even, has_down), barrier, down)
    corner = remote(both, landed, sends, receives, 0, down)
    under = remote(dropped, from_up, sends, receives, 1, down)
    rest = remote(
        spill.at[:, :, side_len:, :], from_left.at[:, :, side_len:, :], sends, receives, 2, right
    )
    top = remote(
        spill.at[:, :, :side_len, :], from_left.at[:, :, :side_len, :], sends, receives, 3, right
    )
    spill[:, :, side_len:, :] = grown[:, own_blocks:, side_len:tile_len, :].astype(jnp.bfloat16)
    from_even = has_up.astype(jnp.int32) + has_down.astype(jnp.int32)
    awaited = has_right.astype(jnp.int32) + jnp.where(odd, from_even, 0)

    @pl.when(awaited > 0)
    def _():
        pl.semaphore_wait(barrier, awaited)

    @pl.when(has_right)
    def _():
        rest.start()

    tell(odd, ready, up)

    both[...] = grown[:, own_blocks:, tile_len:, :].astype(jnp.bfloat16)

    @pl.when(jnp.logical_and(odd, has_down))
    def _():
        corner.start()

    @pl.when(jnp.logical_not(has_up))
    def _():
        spill[:, :, :side_len, :] = grown[:, own_blocks:, :side_len, :].astype(jnp.bfloat16)

    @pl.when(jnp.logical_and(jnp.logical_not(has_up), has_right))
    def _():
        top.start()

    dropped[...] = grown[:, :own_blocks, tile_len:, :].astype(jnp.bfloat16)

    @pl.when(jnp.logical_and(odd, has_down))
    def _():
        under.start()

    for c in range(2):
        for b in range(own_blocks):
            total[c, :, b * LANES : (b + 1) * LANES] = grown[c, b, :tile_len, :]

    @pl.when(jnp.logical_and(even, has_down))
    def _():
        pl.semaphore_wait(ready, 1)
        corner.start()
        under.start()

    @pl.when(has_up)
    def _():
        corner.wait_recv()
        spill[:, :, :side_len, :] = (
            grown[:, own_blocks:, :side_len, :] + landed[...].astype(jnp.float32)
        ).astype(jnp.bfloat16)

    @pl.when(jnp.logical_and(has_up, has_right))
    def _():
        top.start()

    def add(blocks, at, source):
        for c in range(2):
            for b in blocks:
                total[c, at, b * LANES : (b + 1) * LANES] += source[c, b, at, :].astype(jnp.float32)

    @pl.when(has_left)
    def _():
        rest.wait_recv()
        add(range(side_blocks), slice(side_len, tile_len), from_left)

    @pl.when(has_up)
    def _():
        under.wait_recv()
        add(range(own_blocks), slice(0, side_len), from_up)

    @pl.when(has_left)
    def _():
        top.wait_recv()

    @pl.when(jnp.logical_not(has_left))
    def _():
        from_left[:, :, :side_len, :] = jnp.zeros(
            (2, side_blocks, side_len, LANES), jnp.bfloat16
        )

    @pl.when(has_right)
    def _():
        rest.wait_send()
        top.wait_send()

    @pl.when(has_down)
    def _():
        corner.wait_send()
        under.wait_send()


def scatter(axes, grown, tile_len):
    span = grown.shape[2]
    side_len = span - tile_len
    own_blocks = tile_len // LANES
    side_blocks = side_len // LANES
    vmem = pl.BlockSpec(memory_space=pltpu.VMEM)
    scratch = [
        ((2, side_blocks, tile_len, LANES), jnp.bfloat16),
        ((2, own_blocks, side_len, LANES), jnp.bfloat16),
        ((2, side_blocks, side_len, LANES), jnp.bfloat16),
        ((2, side_blocks, side_len, LANES), jnp.bfloat16),
        ((2, own_blocks, side_len, LANES), jnp.bfloat16),
    ]
    summed = pl.pallas_call(
        functools.partial(scatter_kernel, axes),
        out_shape=[
            pltpu.VMEM((2, tile_len, tile_len), jnp.float32),
            pltpu.VMEM((2, side_blocks, tile_len, LANES), jnp.bfloat16),
        ],
        in_specs=[vmem],
        out_specs=[vmem] * 2,
        scratch_shapes=[pltpu.VMEM(*each) for each in scratch]
        + [
            pltpu.SemaphoreType.DMA((4,)),
            pltpu.SemaphoreType.DMA((4,)),
            pltpu.SemaphoreType.REGULAR,
        ],
        compiler_params=pltpu.CompilerParams(
            collective_id=1, has_side_effects=True, vmem_limit_bytes=room(scratch)
        ),
    )(grown)
    held = [pltpu.with_memory_space_constraint(each, pltpu.VMEM) for each in summed]
    return pl.pallas_call(
        finish_kernel,
        out_shape=jax.ShapeDtypeStruct((2, tile_len, tile_len), jnp.float32),
        in_specs=[vmem] * 2,
        out_specs=pl.BlockSpec(memory_space=pltpu.HBM),
        scratch_shapes=[
            pltpu.VMEM((2, side_len, side_len), jnp.float32),
            pltpu.SemaphoreType.DMA((2, 3)),
        ],
        compiler_params=pltpu.CompilerParams(vmem_limit_bytes=room(scratch)),
    )(*held)


def finish_kernel(total, from_left, out_hbm, head, puts):
    side_len = head.shape[1]
    copies = []
    for c in range(2):
        for i, at in enumerate(
            (
                (c, slice(side_len, None), slice(None)),
                (c, slice(0, side_len), slice(side_len, None)),
            )
        ):
            copies.append(pltpu.make_async_copy(total.at[at], out_hbm.at[at], puts.at[c, i]))
    for copy in copies:
        copy.start()
    for c in range(2):
        for b in range(side_len // LANES):
            cols = slice(b * LANES, (b + 1) * LANES)
            head[c, :, cols] = total[c, :side_len, cols] + from_left[c, b, :side_len, :].astype(
                jnp.float32
            )
        at = (c, slice(0, side_len), slice(0, side_len))
        copies.append(pltpu.make_async_copy(head.at[c], out_hbm.at[at], puts.at[c, 2]))
        copies[-1].start()
    for copy in copies:
        copy.wait()


def side_by_side(*blocks):
    return jnp.concatenate(blocks, axis=1)


def solve_kernel(
    live_ref,
    shift_ref,
    field,
    probes,
    tables,
    measured,
    zeros,
    grown,
    mixed,
    halves,
    misfits,
    spectra,
    backs,
    fence,
):
    side_len = probes.shape[3]
    part = side_len // RADIX
    side_blocks = side_len // LANES
    lane = lax.broadcasted_iota(jnp.int32, (1, LANES), 1)
    line = lax.broadcasted_iota(jnp.int32, (GROUP, LANES), 0)

    def one_slot(slot, carry):
        row = shift_ref[0, slot]
        col = shift_ref[1, slot]
        lift = lax.rem(row, GROUP)
        turn = lax.rem(col, LANES)
        base = pl.multiple_of(row - lift, GROUP)
        block = lax.div(col, LANES)
        stay = lane >= turn
        below = line >= lift

        def table(side, kind, q):
            return side_by_side(tables[slot, side, kind, q, 0], tables[slot, side, kind, q, 1])

        def piece(c, b, at):
            def cut(b):
                start = pl.multiple_of(base + at, GROUP)
                value = field[c, block + b, pl.ds(start, GROUP), :]
                if at == 0:
                    start = pl.multiple_of(base + side_len, GROUP)
                    wrapped = field[c, block + b, pl.ds(start, GROUP), :]
                    value = jnp.where(below, value, wrapped)
                return value

            value = cut(b) if b else jnp.where(stay, cut(0), cut(side_blocks))
            return value.astype(jnp.float32)

        def exit_waves(blocks):
            for at in range(0, part, GROUP):
                for b in blocks:
                    waves = []
                    for p in range(RADIX):
                        here = at + p * part
                        re, im = piece(0, b, here), piece(1, b, here)
                        probe_re = probes[slot, 0, b, here : here + GROUP, :]
                        probe_im = probes[slot, 1, b, here : here + GROUP, :]
                        waves.append((probe_re * re - probe_im * im, probe_re * im + probe_im * re))
                    for q, (re, im) in enumerate(butterfly(waves, -1)):
                        mixed[q, b, at : at + GROUP, :] = re.astype(jnp.bfloat16)
                        mixed[q, b, at + part : at + part + GROUP, :] = im.astype(jnp.bfloat16)

        def split(value):
            return [
                (value[:part, at : at + part], value[part:, at : at + part])
                for at in range(0, value.shape[1], part)
            ]

        def left(q, blocks):
            return split(dot(table(0, 0, q), side_by_side(*(mixed[q, b] for b in blocks))))

        def far_field(other):
            return dot(side_by_side(halves[other, 0], halves[other, 1]), table(1, 1, other))

        def misfit_of(other, far):
            for q in range(RADIX):
                rows = slice(q * part, (q + 1) * part)
                far_re, far_im = far[rows, :part], far[rows, part:]
                seen = measured[slot, other, rows, :].astype(jnp.float32)
                misfit = far_re * far_re + far_im * far_im - seen
                misfits[q, other, :part, :] = (misfit * far_re).astype(jnp.bfloat16)
                misfits[q, other, part:, :] = (misfit * far_im).astype(jnp.bfloat16)

        def left_back(q, pair):
            mixture = dot(table(1, 0, q), side_by_side(*(misfits[q, other] for other in pair)))
            for i, other in enumerate(pair):
                spectra[q, other] = mixture[:, i * part : (i + 1) * part]

        def mix(ats, pair):
            for at in ats:
                for other in pair:
                    parts = [
                        (
                            spectra[q, other, at : at + GROUP, :],
                            spectra[q, other, part + at : part + at + GROUP, :],
                        )
                        for q in range(RADIX)
                    ]
                    for p, (re, im) in enumerate(butterfly(parts, 1)):
                        here = slice(at + p * part, at + p * part + GROUP)
                        backs[other, 0, here, :] = re.astype(jnp.bfloat16)
                        backs[other, 1, here, :] = im.astype(jnp.bfloat16)

        def add(c, b, at, value, mask=None):
            where = pl.ds(pl.multiple_of(base + at, GROUP), value.shape[0])
            if mask is None:
                grown[c, block + b, where, :] += value
            else:
                spot = grown.at[c, block + b, where, :]
                mask = jnp.broadcast_to(mask, value.shape)
                pltpu.store(spot, spot[...] + value, mask=mask)

        def add_wrapped(c, b, at, value, mask=None):
            if at == 0:
                add(c, b, 0, jnp.where(below, value[:GROUP], 0.0), mask)
                add(c, b, side_len, jnp.where(below, 0.0, value[:GROUP]), mask)
                add(c, b, GROUP, value[GROUP:], mask)
            else:
                add(c, b, at, value, mask)

        def right_back(at, tall):
            parts = []
            for other in range(RADIX):
                back = jnp.concatenate(
                    [
                        side_by_side(
                            backs[other, 0, here : here + tall, :],
                            backs[other, 1, here : here + tall, :],
                        )
                        for here in range(at, side_len, part)
                    ],
                    axis=0,
                )
                grad = dot(back, table(0, 1, other))
                parts.append((grad[:, :part], grad[:, part:]))
            return parts

        def accumulate(at, tall, parts):
            for p in range(RADIX):
                here = at + p * part
                rows = slice(p * tall, (p + 1) * tall)
                some = [(re[rows], im[rows]) for re, im in parts]
                for b, (re, im) in enumerate(butterfly(some, 1)):
                    probe_re = probes[slot, 0, b, here : here + tall, :]
                    probe_im = probes[slot, 1, b, here : here + tall, :]
                    values = (probe_re * re + probe_im * im, probe_re * im - probe_im * re)
                    for c, value in enumerate(values):
                        if b == 0:
                            add_wrapped(c, 0, here, value, stay)
                            add_wrapped(c, side_blocks, here, value, jnp.logical_not(stay))
                        else:
                            add_wrapped(c, b, here, value)

        exit_waves((0, 2))
        exit_waves((1, 3))
        pl.semaphore_signal(fence, 1)
        pl.semaphore_wait(fence, 1)
        for q in range(RADIX):
            rows = slice(q * part, (q + 1) * part)
            for other, (re, im) in enumerate(butterfly(left(q, range(RADIX)), -1)):
                halves[other, 0, rows, :] = re.astype(jnp.bfloat16)
                halves[other, 1, rows, :] = im.astype(jnp.bfloat16)
        ahead = far_field(0)
        for other in range(RADIX):
            far = ahead
            if other + 1 < RADIX:
                ahead = far_field(other + 1)
            misfit_of(other, far)
            if other == 2:
                for q in range(RADIX):
                    left_back(q, (0, 1))
        tall = part // 2
        ats = [range(at, at + tall, GROUP) for at in range(0, part, tall)]
        for q in range(RADIX):
            left_back(q, (2, 3))
        mix(ats[0], range(RADIX))
        mix(ats[1], range(RADIX))
        first = right_back(0, tall)
        second = right_back(tall, tall)
        accumulate(0, tall, first)
        accumulate(tall, tall, second)
        return carry

    lax.fori_loop(0, live_ref[0, lax.axis_index("scan")], one_slot, 0)


def solve(live_counts, shifts, prepared, limit):
    grown = prepared[-1]
    side_len = prepared[1].shape[3]
    part = side_len // RADIX
    smem = pl.BlockSpec(memory_space=pltpu.SMEM)
    vmem = pl.BlockSpec(memory_space=pltpu.VMEM)
    wide = (RADIX, RADIX, 2 * part, part)
    tall = (RADIX, 2, side_len, part)
    scratch = [
        (wide, jnp.bfloat16),
        (tall, jnp.bfloat16),
        (wide, jnp.bfloat16),
        (wide, jnp.float32),
        (tall, jnp.bfloat16),
    ]
    return pl.pallas_call(
        solve_kernel,
        out_shape=pltpu.VMEM(grown.shape, grown.dtype),
        in_specs=[smem, smem] + [vmem] * len(prepared),
        out_specs=vmem,
        scratch_shapes=[pltpu.VMEM(*each) for each in scratch] + [pltpu.SemaphoreType.REGULAR],
        input_output_aliases={1 + len(prepared): 0},
        compiler_params=pltpu.CompilerParams(vmem_limit_bytes=limit),
    )(live_counts, shifts, *prepared)


def shards(axes, object_slab, probe_field, intensities, offsets, live_count):
    tables = residue_tables(probe_field.shape[-1])
    shifts = offsets[0, 0].T
    prepared, limit = gather(axes, shifts, object_slab, intensities[0, 0], probe_field, tables)
    grown = solve(live_count.T, shifts, prepared, limit)
    return scatter(axes, grown, object_slab.shape[1])


def solution(mesh):
    placed = (
        P(None, "tile", "scan"),
        P(),
        P("scan", "tile", None, None, None),
        P("scan", "tile", None, None),
        P(None, "tile"),
    )
    axes = tuple((name, mesh.shape[name]) for name in ("scan", "tile"))
    return jax.shard_map(
        functools.partial(shards, axes), mesh=mesh, in_specs=placed, out_specs=P(None, "tile", "scan"), check_vma=False
    )
```

```python
import functools
import math

import jax
import jax.numpy as jnp
import numpy as np
from jax import lax
from jax.experimental import pallas as pl
from jax.experimental.pallas import tpu as pltpu
from jax.sharding import PartitionSpec as P

RADIX = 4
LANES = 128
GROUP = 16


def residue_tables(side_len):
    part = side_len // RADIX
    freq = np.arange(side_len).reshape(part, RADIX).T
    across = np.arange(part)
    phase = (freq[:, :, None] * across[None, None, :] % side_len) * (2.0 * math.pi / side_len)
    factor = 1.0 / math.sqrt(side_len)
    cos = np.cos(phase) * factor
    sin = np.sin(phase) * factor
    rows = np.concatenate(
        [np.concatenate([cos, sin], axis=2), np.concatenate([-sin, cos], axis=2)], axis=1
    ).astype(np.float32)
    return jnp.asarray(rows, jnp.bfloat16), jnp.asarray(rows.swapaxes(1, 2), jnp.bfloat16)


def sorted_by_residue(side_len):
    at = np.arange(side_len)
    source = at % (side_len // RADIX) * RADIX + at // (side_len // RADIX)
    sort = (source[:, None] == at[None, :]).astype(np.float32)
    return jnp.asarray(sort, jnp.bfloat16), jnp.asarray(sort.T, jnp.bfloat16)


def dot(a, b):
    return jnp.dot(a, b, preferred_element_type=jnp.float32)


def butterfly(parts, sign):
    (r0, i0), (r1, i1), (r2, i2), (r3, i3) = parts
    ar, ai, br, bi = r0 + r2, i0 + i2, r1 + r3, i1 + i3
    cr, ci, dr, di = r0 - r2, i0 - i2, r1 - r3, i1 - i3
    plus = (cr - di, ci + dr)
    minus = (cr + di, ci - dr)
    first, third = (plus, minus) if sign > 0 else (minus, plus)
    return [(ar + br, ai + bi), first, (ar - br, ai - bi), third]


def neighbours(axes):
    result = []
    for name, count in axes:
        me = lax.axis_index(name)
        result.append((me > 0, {name: me - 1}, me < count - 1, {name: me + 1}))
    return result


def greet(peers):
    barrier = pltpu.get_barrier_semaphore()
    for has_low, low, has_high, high in peers:
        for there, peer in ((has_low, low), (has_high, high)):

            @pl.when(there)
            def _(peer=peer):
                pl.semaphore_signal(
                    barrier, inc=1, device_id=peer, device_id_type=pl.DeviceIdType.MESH
                )


def all_here(peers):
    count = sum(
        there.astype(jnp.int32) for has_low, _, has_high, _ in peers for there in (has_low, has_high)
    )
    pl.semaphore_wait(pltpu.get_barrier_semaphore(), count)


def remote(source, target, sends, receives, index, peer):
    return pltpu.make_async_remote_copy(
        src_ref=source,
        dst_ref=target,
        send_sem=sends.at[index],
        recv_sem=receives.at[index],
        device_id=peer,
        device_id_type=pl.DeviceIdType.MESH,
    )


def quarter_turns(cos, sin, q):
    return ((cos, sin), (sin, -cos), (-cos, -sin), (-sin, cos))[q]


def in_place(mask, cos, sin, q):
    wrapped = quarter_turns(cos, sin, q)
    return jnp.where(mask, cos, wrapped[0]), jnp.where(mask, sin, wrapped[1])


def gather_kernel(
    axes,
    shift_ref,
    own_hbm,
    measured_hbm,
    probe_hbm,
    rows_hbm,
    cols_hbm,
    sort_hbm,
    unsort_hbm,
    field,
    probes,
    tables,
    arranged,
    grown,
    own,
    measured,
    extended,
    rows_ref,
    cols_ref,
    doubled,
    sort,
    unsort,
    sends,
    receives,
    fetches,
    freed,
):
    slots, side_len = measured.shape[:2]
    tile_len = own.shape[1]
    part = side_len // RADIX
    own_blocks = tile_len // LANES
    side_blocks = side_len // LANES
    scan, tile = neighbours(axes)
    has_left, left, has_right, _ = scan
    has_up, up, has_down, down = tile
    greet((scan, tile))
    firsts = [
        pltpu.make_async_copy(
            own_hbm.at[c, :side_len, :side_len],
            own.at[c, :side_len, :side_len],
            fetches.at[4 * c],
        )
        for c in range(2)
    ]
    second = pltpu.make_async_copy(
        own_hbm.at[:, side_len:, :side_len], own.at[:, side_len:, :side_len], fetches.at[1]
    )
    third = pltpu.make_async_copy(
        own_hbm.at[:, :side_len, side_len:], own.at[:, :side_len, side_len:], fetches.at[2]
    )
    fourth = pltpu.make_async_copy(
        own_hbm.at[:, side_len:, side_len:], own.at[:, side_len:, side_len:], fetches.at[3]
    )
    constants = [
        pltpu.make_async_copy(source, target, fetches.at[5 + i])
        for i, (source, target) in enumerate(
            (
                (sort_hbm, sort),
                (unsort_hbm, unsort),
                (measured_hbm, measured),
                (rows_hbm, rows_ref),
                (cols_hbm, cols_ref),
            )
        )
    ]
    for c in range(2):
        for b in range(side_blocks):
            cols = slice(b * LANES, (b + 1) * LANES)
            for source, target in (
                (probe_hbm.at[c, :, cols], extended.at[c, b, GROUP:, :]),
                (probe_hbm.at[c, side_len - GROUP :, cols], extended.at[c, b, :GROUP, :]),
            ):
                constants.append(
                    pltpu.make_async_copy(source, target, fetches.at[5 + len(constants)])
                )
    for load in firsts + [third, second, fourth] + constants:
        load.start()
    near = slice(0, side_blocks)
    far = slice(own_blocks, own_blocks + side_blocks)
    halves = [
        (c, slice(at, at + side_blocks // 2))
        for c in range(2)
        for at in range(0, side_blocks, side_blocks // 2)
    ]

    def moved(blocks):
        return slice(blocks.start + own_blocks, blocks.stop + own_blocks)

    tops = [
        remote(
            field.at[c, blocks, :side_len, :],
            field.at[c, moved(blocks), :side_len, :],
            sends,
            receives,
            3 + i,
            left,
        )
        for i, (c, blocks) in enumerate(halves)
    ]
    rests = [
        remote(
            field.at[c, near, side_len:tile_len, :],
            field.at[c, far, side_len:tile_len, :],
            sends,
            receives,
            c,
            left,
        )
        for c in range(2)
    ]
    unders = [
        remote(
            field.at[:, blocks, :side_len, :],
            field.at[:, blocks, tile_len:, :],
            sends,
            receives,
            index,
            up,
        )
        for blocks, index in (
            (near, 2),
            (slice(side_blocks, own_blocks), 3 + 2 * len(halves)),
        )
    ]
    acrosses = [
        remote(
            field.at[c, moved(blocks), :side_len, :],
            field.at[c, moved(blocks), tile_len:, :],
            sends,
            receives,
            3 + len(halves) + i,
            up,
        )
        for i, (c, blocks) in enumerate(halves)
    ]

    def narrow(blocks, at, planes=range(2)):
        for c in planes:
            for b in blocks:
                field[c, b, at, :] = own[c, at, b * LANES : (b + 1) * LANES].astype(jnp.bfloat16)

    firsts[0].wait()
    narrow(range(side_blocks), slice(0, side_len), range(1))
    all_here((scan, tile))

    @pl.when(has_left)
    def _():
        for each in tops[:2]:
            each.start()

    firsts[1].wait()
    narrow(range(side_blocks), slice(0, side_len), range(1, 2))

    @pl.when(has_left)
    def _():
        for each in tops[2:]:
            each.start()

    @pl.when(has_up)
    def _():
        unders[0].start()

    third.wait()
    narrow(range(side_blocks, own_blocks), slice(0, side_len))

    @pl.when(has_up)
    def _():
        unders[1].start()

    second.wait()
    narrow(range(side_blocks), slice(side_len, tile_len))

    odd = lax.rem(lax.axis_index(axes[1][0]), 2) == 1
    first_turn = jnp.logical_and(has_left, jnp.logical_not(odd))
    second_turn = jnp.logical_and(has_left, odd)

    @pl.when(first_turn)
    def _():
        for each in rests:
            each.start()

    @pl.when(jnp.logical_not(has_right))
    def _():
        field[:, far, :tile_len, :] = jnp.zeros(
            (2, side_blocks, tile_len, LANES), jnp.bfloat16
        )

    @pl.when(jnp.logical_not(has_down))
    def _():
        field[:, :, tile_len:, :] = jnp.zeros(
            (2, own_blocks + side_blocks, side_len, LANES), jnp.bfloat16
        )

    fourth.wait()
    narrow(range(side_blocks, own_blocks), slice(side_len, tile_len))
    for load in constants:
        load.wait()

    def sort_slot(slot, carry):
        rows = dot(sort[...], measured[slot]).astype(jnp.bfloat16)
        both = dot(rows, unsort[...]).astype(jnp.bfloat16)
        for b in range(RADIX):
            arranged[slot, b] = both[:, b * part : (b + 1) * part]
        return carry

    lax.fori_loop(0, slots, sort_slot, 0)

    grown[...] = jnp.zeros_like(grown)
    for q in range(RADIX):
        for i in range(2):
            for at in (0, part):
                doubled[q, i, at : at + part, :] = cols_ref[
                    q, i * part : (i + 1) * part, :part
                ].astype(jnp.float32)

    lane = lax.broadcasted_iota(jnp.int32, (1, LANES), 1)
    line = lax.broadcasted_iota(jnp.int32, (part, LANES), 0)
    chunk = 32

    def prepare(slot, carry):
        lift = lax.rem(shift_ref[0, slot], GROUP)
        turn = lax.rem(shift_ref[1, slot], LANES)

        def move_probe(i, carry):
            at = pl.multiple_of(i * chunk, chunk)
            for c in range(2):
                turned = [
                    pltpu.roll(extended[c, b, pl.ds(GROUP - lift + at, chunk), :], turn, 1)
                    for b in range(side_blocks)
                ]
                for b in range(side_blocks):
                    probes[slot, c, b, pl.ds(at, chunk), :] = jnp.where(
                        lane >= turn, turned[b], turned[b - 1]
                    )
            return carry

        lax.fori_loop(0, side_len // chunk, move_probe, 0)
        for k, by in enumerate((lift, turn)):
            for q in range(RADIX):
                cos = pltpu.roll(rows_ref[q, :part, :part].astype(jnp.float32), by, 1)
                sin = pltpu.roll(rows_ref[q, :part, part:].astype(jnp.float32), by, 1)
                cos, sin = in_place(lane >= by, cos, sin, q)
                tables[slot, 0, k, q, 0, :part, :] = cos.astype(jnp.bfloat16)
                tables[slot, 0, k, q, 1, :part, :] = sin.astype(jnp.bfloat16)
                tables[slot, 0, k, q, 0, part:, :] = (-sin).astype(jnp.bfloat16)
                tables[slot, 0, k, q, 1, part:, :] = cos.astype(jnp.bfloat16)
                cos = doubled[q, 0, pl.ds(part - by, part), :]
                sin = doubled[q, 1, pl.ds(part - by, part), :]
                cos, sin = in_place(line >= by, cos, sin, q)
                tables[slot, 1, k, q, 0, :part, :] = cos.astype(jnp.bfloat16)
                tables[slot, 1, k, q, 1, :part, :] = (-sin).astype(jnp.bfloat16)
                tables[slot, 1, k, q, 0, part:, :] = sin.astype(jnp.bfloat16)
                tables[slot, 1, k, q, 1, part:, :] = cos.astype(jnp.bfloat16)
        return carry

    lax.fori_loop(0, slots, prepare, 0)

    for top, across in zip(tops, acrosses):

        @pl.when(has_right)
        def _(top=top):
            top.wait_recv()

        @pl.when(has_up)
        def _(across=across):
            across.start()

    @pl.when(first_turn)
    def _():
        for each in tops + rests:
            each.wait_send()

    @pl.when(jnp.logical_and(first_turn, has_down))
    def _():
        pl.semaphore_signal(
            freed, inc=1, device_id=down, device_id_type=pl.DeviceIdType.MESH
        )

    @pl.when(second_turn)
    def _():
        pl.semaphore_wait(freed, 1)
        for each in rests:
            each.start()


    @pl.when(has_down)
    def _():
        for each in unders:
            each.wait_recv()

    @pl.when(has_right)
    def _():
        for each in rests:
            each.wait_recv()

    @pl.when(has_down)
    def _():
        for each in acrosses:
            each.wait_recv()

    @pl.when(second_turn)
    def _():
        for each in tops + rests:
            each.wait_send()

    @pl.when(has_up)
    def _():
        for each in unders:
            each.wait_send()
        for each in acrosses:
            each.wait_send()


def gather(axes, shifts, own, measured, probe, tables):
    slots, side_len = measured.shape[:2]
    tile_len = own.shape[1]
    span = tile_len + side_len
    part = side_len // RADIX
    side_blocks = side_len // LANES
    hbm = pl.BlockSpec(memory_space=pltpu.HBM)
    vmem = pl.BlockSpec(memory_space=pltpu.VMEM)
    table = (slots, 2, 2, RADIX, 2, 2 * part, part)
    scratch = [
        (own.shape, jnp.float32),
        (measured.shape, jnp.bfloat16),
        ((2, side_blocks, side_len + GROUP, LANES), jnp.float32),
        (tables[0].shape, jnp.bfloat16),
        (tables[1].shape, jnp.bfloat16),
        ((RADIX, 2, 2 * part, part), jnp.float32),
        ((side_len, side_len), jnp.bfloat16),
        ((side_len, side_len), jnp.bfloat16),
    ]
    call = pl.pallas_call(
        functools.partial(gather_kernel, axes),
        out_shape=[
            pltpu.VMEM((2, span // LANES, span, LANES), jnp.bfloat16),
            pltpu.VMEM((slots, 2, side_blocks, side_len, LANES), jnp.float32),
            pltpu.VMEM(table, jnp.bfloat16),
            pltpu.VMEM((slots, RADIX, side_len, part), jnp.bfloat16),
            pltpu.VMEM((2, span // LANES, span, LANES), jnp.float32),
        ],
        in_specs=[pl.BlockSpec(memory_space=pltpu.SMEM)] + [hbm] * 7,
        out_specs=[vmem] * 5,
        scratch_shapes=[pltpu.VMEM(*each) for each in scratch]
        + [
            pltpu.SemaphoreType.DMA((4 + 8,)),
            pltpu.SemaphoreType.DMA((4 + 8,)),
            pltpu.SemaphoreType.DMA((10 + 4 * side_blocks,)),
            pltpu.SemaphoreType.REGULAR,
        ],
        compiler_params=pltpu.CompilerParams(
            collective_id=0, has_side_effects=True, vmem_limit_bytes=room(scratch)
        ),
    )
    prepared = call(shifts, own, measured, probe, *tables, *sorted_by_residue(side_len))
    held = [pltpu.with_memory_space_constraint(each, pltpu.VMEM) for each in prepared]
    return held, room(scratch)


def room(scratch):
    return sum(math.prod(shape) * jnp.dtype(kind).itemsize for shape, kind in scratch) + (1 << 20)


def scatter_kernel(
    axes,
    grown,
    total,
    from_left,
    spill,
    dropped,
    both,
    landed,
    from_up,
    sends,
    receives,
    ready,
):
    side_len = landed.shape[2]
    tile_len = total.shape[1]
    own_blocks = tile_len // LANES
    side_blocks = side_len // LANES
    scan, tile = neighbours(axes)
    has_left, left, has_right, right = scan
    has_up, up, has_down, down = tile
    odd = lax.rem(lax.axis_index(axes[1][0]), 2) == 1
    even = jnp.logical_not(odd)
    barrier = pltpu.get_barrier_semaphore()

    def tell(there, sem, peer):
        @pl.when(there)
        def _():
            pl.semaphore_signal(
                sem, inc=1, device_id=peer, device_id_type=pl.DeviceIdType.MESH
            )

    tell(has_left, barrier, left)
    tell(jnp.logical_and(even, has_up), barrier, up)
    tell(jnp.logical_and(even, has_down), barrier, down)
    corners = [
        remote(both.at[c], landed.at[c], sends, receives, 4 * c, down) for c in range(2)
    ]
    under = remote(dropped, from_up, sends, receives, 1, down)
    rest = remote(
        spill.at[:, :, side_len:, :], from_left.at[:, :, side_len:, :], sends, receives, 2, right
    )
    tops = [
        remote(
            spill.at[c, :, :side_len, :],
            from_left.at[c, :, :side_len, :],
            sends,
            receives,
            3 + 2 * c,
            right,
        )
        for c in range(2)
    ]
    spill[:, :, side_len:, :] = grown[:, own_blocks:, side_len:tile_len, :].astype(jnp.bfloat16)
    from_even = has_up.astype(jnp.int32) + has_down.astype(jnp.int32)
    awaited = has_right.astype(jnp.int32) + jnp.where(odd, from_even, 0)

    @pl.when(awaited > 0)
    def _():
        pl.semaphore_wait(barrier, awaited)

    @pl.when(has_right)
    def _():
        rest.start()

    tell(odd, ready, up)

    both[...] = grown[:, own_blocks:, tile_len:, :].astype(jnp.bfloat16)

    @pl.when(jnp.logical_and(odd, has_down))
    def _():
        for each in corners:
            each.start()

    @pl.when(jnp.logical_not(has_up))
    def _():
        spill[:, :, :side_len, :] = grown[:, own_blocks:, :side_len, :].astype(jnp.bfloat16)

    @pl.when(jnp.logical_and(jnp.logical_not(has_up), has_right))
    def _():
        for each in tops:
            each.start()

    dropped[...] = grown[:, :own_blocks, tile_len:, :].astype(jnp.bfloat16)

    @pl.when(jnp.logical_and(odd, has_down))
    def _():
        under.start()

    for c in range(2):
        for b in range(own_blocks):
            total[c, :, b * LANES : (b + 1) * LANES] = grown[c, b, :tile_len, :]

    @pl.when(jnp.logical_and(even, has_down))
    def _():
        pl.semaphore_wait(ready, 1)
        for each in corners:
            each.start()
        under.start()

    for c in range(2):

        @pl.when(has_up)
        def _(c=c):
            corners[c].wait_recv()
            spill[c, :, :side_len, :] = (
                grown[c, own_blocks:, :side_len, :] + landed[c].astype(jnp.float32)
            ).astype(jnp.bfloat16)

        @pl.when(jnp.logical_and(has_up, has_right))
        def _(c=c):
            tops[c].start()

    def add(blocks, at, source):
        for c in range(2):
            for b in blocks:
                total[c, at, b * LANES : (b + 1) * LANES] += source[c, b, at, :].astype(jnp.float32)

    @pl.when(has_left)
    def _():
        rest.wait_recv()
        add(range(side_blocks), slice(side_len, tile_len), from_left)

    @pl.when(has_up)
    def _():
        under.wait_recv()
        add(range(own_blocks), slice(0, side_len), from_up)

    @pl.when(has_left)
    def _():
        for each in tops:
            each.wait_recv()

    @pl.when(jnp.logical_not(has_left))
    def _():
        from_left[:, :, :side_len, :] = jnp.zeros(
            (2, side_blocks, side_len, LANES), jnp.bfloat16
        )

    @pl.when(has_right)
    def _():
        rest.wait_send()
        for each in tops:
            each.wait_send()

    @pl.when(has_down)
    def _():
        for each in corners:
            each.wait_send()
        under.wait_send()


def scatter(axes, grown, tile_len):
    span = grown.shape[2]
    side_len = span - tile_len
    own_blocks = tile_len // LANES
    side_blocks = side_len // LANES
    vmem = pl.BlockSpec(memory_space=pltpu.VMEM)
    scratch = [
        ((2, side_blocks, tile_len, LANES), jnp.bfloat16),
        ((2, own_blocks, side_len, LANES), jnp.bfloat16),
        ((2, side_blocks, side_len, LANES), jnp.bfloat16),
        ((2, side_blocks, side_len, LANES), jnp.bfloat16),
        ((2, own_blocks, side_len, LANES), jnp.bfloat16),
    ]
    summed = pl.pallas_call(
        functools.partial(scatter_kernel, axes),
        out_shape=[
            pltpu.VMEM((2, tile_len, tile_len), jnp.float32),
            pltpu.VMEM((2, side_blocks, tile_len, LANES), jnp.bfloat16),
        ],
        in_specs=[vmem],
        out_specs=[vmem] * 2,
        scratch_shapes=[pltpu.VMEM(*each) for each in scratch]
        + [
            pltpu.SemaphoreType.DMA((6,)),
            pltpu.SemaphoreType.DMA((6,)),
            pltpu.SemaphoreType.REGULAR,
        ],
        compiler_params=pltpu.CompilerParams(
            collective_id=1, has_side_effects=True, vmem_limit_bytes=room(scratch)
        ),
    )(grown)
    held = [pltpu.with_memory_space_constraint(each, pltpu.VMEM) for each in summed]
    return pl.pallas_call(
        finish_kernel,
        out_shape=jax.ShapeDtypeStruct((2, tile_len, tile_len), jnp.float32),
        in_specs=[vmem] * 2,
        out_specs=pl.BlockSpec(memory_space=pltpu.HBM),
        scratch_shapes=[
            pltpu.VMEM((2, side_len, side_len), jnp.float32),
            pltpu.SemaphoreType.DMA((2, 3)),
        ],
        compiler_params=pltpu.CompilerParams(vmem_limit_bytes=room(scratch)),
    )(*held)


def finish_kernel(total, from_left, out_hbm, head, puts):
    side_len = head.shape[1]
    copies = []
    for c in range(2):
        for i, at in enumerate(
            (
                (c, slice(side_len, None), slice(None)),
                (c, slice(0, side_len), slice(side_len, None)),
            )
        ):
            copies.append(pltpu.make_async_copy(total.at[at], out_hbm.at[at], puts.at[c, i]))
    for copy in copies:
        copy.start()
    for c in range(2):
        for b in range(side_len // LANES):
            cols = slice(b * LANES, (b + 1) * LANES)
            head[c, :, cols] = total[c, :side_len, cols] + from_left[c, b, :side_len, :].astype(
                jnp.float32
            )
        at = (c, slice(0, side_len), slice(0, side_len))
        copies.append(pltpu.make_async_copy(head.at[c], out_hbm.at[at], puts.at[c, 2]))
        copies[-1].start()
    for copy in copies:
        copy.wait()


def side_by_side(*blocks):
    return jnp.concatenate(blocks, axis=1)


def solve_kernel(
    live_ref,
    shift_ref,
    field,
    probes,
    tables,
    measured,
    zeros,
    grown,
    mixed,
    halves,
    misfits,
    spectra,
    backs,
    fence,
):
    side_len = probes.shape[3]
    part = side_len // RADIX
    side_blocks = side_len // LANES
    lane = lax.broadcasted_iota(jnp.int32, (1, LANES), 1)
    line = lax.broadcasted_iota(jnp.int32, (GROUP, LANES), 0)

    def one_slot(slot, carry):
        row = shift_ref[0, slot]
        col = shift_ref[1, slot]
        lift = lax.rem(row, GROUP)
        turn = lax.rem(col, LANES)
        base = pl.multiple_of(row - lift, GROUP)
        block = lax.div(col, LANES)
        stay = lane >= turn
        below = line >= lift

        def table(side, kind, q):
            return side_by_side(tables[slot, side, kind, q, 0], tables[slot, side, kind, q, 1])

        def piece(c, b, at):
            def cut(b):
                start = pl.multiple_of(base + at, GROUP)
                value = field[c, block + b, pl.ds(start, GROUP), :]
                if at == 0:
                    start = pl.multiple_of(base + side_len, GROUP)
                    wrapped = field[c, block + b, pl.ds(start, GROUP), :]
                    value = jnp.where(below, value, wrapped)
                return value

            value = cut(b) if b else jnp.where(stay, cut(0), cut(side_blocks))
            return value.astype(jnp.float32)

        def exit_waves(blocks):
            for at in range(0, part, GROUP):
                for b in blocks:
                    waves = []
                    for p in range(RADIX):
                        here = at + p * part
                        re, im = piece(0, b, here), piece(1, b, here)
                        probe_re = probes[slot, 0, b, here : here + GROUP, :]
                        probe_im = probes[slot, 1, b, here : here + GROUP, :]
                        waves.append((probe_re * re - probe_im * im, probe_re * im + probe_im * re))
                    for q, (re, im) in enumerate(butterfly(waves, -1)):
                        mixed[q, b, at : at + GROUP, :] = re.astype(jnp.bfloat16)
                        mixed[q, b, at + part : at + part + GROUP, :] = im.astype(jnp.bfloat16)

        def split(value):
            return [
                (value[:part, at : at + part], value[part:, at : at + part])
                for at in range(0, value.shape[1], part)
            ]

        def left(q, blocks):
            return split(dot(table(0, 0, q), side_by_side(*(mixed[q, b] for b in blocks))))

        def far_field(other):
            return dot(side_by_side(halves[other, 0], halves[other, 1]), table(1, 1, other))

        def misfit_of(other, far):
            for q in range(RADIX):
                rows = slice(q * part, (q + 1) * part)
                far_re, far_im = far[rows, :part], far[rows, part:]
                seen = measured[slot, other, rows, :].astype(jnp.float32)
                misfit = far_re * far_re + far_im * far_im - seen
                misfits[q, other, :part, :] = (misfit * far_re).astype(jnp.bfloat16)
                misfits[q, other, part:, :] = (misfit * far_im).astype(jnp.bfloat16)

        def left_back(q, pair):
            mixture = dot(table(1, 0, q), side_by_side(*(misfits[q, other] for other in pair)))
            for i, other in enumerate(pair):
                spectra[q, other] = mixture[:, i * part : (i + 1) * part]

        def mix(ats, pair):
            for at in ats:
                for other in pair:
                    parts = [
                        (
                            spectra[q, other, at : at + GROUP, :],
                            spectra[q, other, part + at : part + at + GROUP, :],
                        )
                        for q in range(RADIX)
                    ]
                    for p, (re, im) in enumerate(butterfly(parts, 1)):
                        here = slice(at + p * part, at + p * part + GROUP)
                        backs[other, 0, here, :] = re.astype(jnp.bfloat16)
                        backs[other, 1, here, :] = im.astype(jnp.bfloat16)

        def add(c, b, at, value, mask=None):
            where = pl.ds(pl.multiple_of(base + at, GROUP), value.shape[0])
            if mask is None:
                grown[c, block + b, where, :] += value
            else:
                spot = grown.at[c, block + b, where, :]
                mask = jnp.broadcast_to(mask, value.shape)
                pltpu.store(spot, spot[...] + value, mask=mask)

        def add_wrapped(c, b, at, value, mask=None):
            if at == 0:
                add(c, b, 0, jnp.where(below, value[:GROUP], 0.0), mask)
                add(c, b, side_len, jnp.where(below, 0.0, value[:GROUP]), mask)
                add(c, b, GROUP, value[GROUP:], mask)
            else:
                add(c, b, at, value, mask)

        def right_back(at, tall):
            parts = []
            for other in range(RADIX):
                back = jnp.concatenate(
                    [
                        side_by_side(
                            backs[other, 0, here : here + tall, :],
                            backs[other, 1, here : here + tall, :],
                        )
                        for here in range(at, side_len, part)
                    ],
                    axis=0,
                )
                grad = dot(back, table(0, 1, other))
                parts.append((grad[:, :part], grad[:, part:]))
            return parts

        def accumulate(at, tall, parts):
            for p in range(RADIX):
                here = at + p * part
                rows = slice(p * tall, (p + 1) * tall)
                some = [(re[rows], im[rows]) for re, im in parts]
                for b, (re, im) in enumerate(butterfly(some, 1)):
                    probe_re = probes[slot, 0, b, here : here + tall, :]
                    probe_im = probes[slot, 1, b, here : here + tall, :]
                    values = (probe_re * re + probe_im * im, probe_re * im - probe_im * re)
                    for c, value in enumerate(values):
                        if b == 0:
                            add_wrapped(c, 0, here, value, stay)
                            add_wrapped(c, side_blocks, here, value, jnp.logical_not(stay))
                        else:
                            add_wrapped(c, b, here, value)

        exit_waves((0, 2))
        exit_waves((1, 3))
        pl.semaphore_signal(fence, 1)
        pl.semaphore_wait(fence, 1)
        for q in range(RADIX):
            rows = slice(q * part, (q + 1) * part)
            for other, (re, im) in enumerate(butterfly(left(q, range(RADIX)), -1)):
                halves[other, 0, rows, :] = re.astype(jnp.bfloat16)
                halves[other, 1, rows, :] = im.astype(jnp.bfloat16)
        ahead = far_field(0)
        for other in range(RADIX):
            far = ahead
            if other + 1 < RADIX:
                ahead = far_field(other + 1)
            misfit_of(other, far)
            if other == 2:
                for q in range(RADIX):
                    left_back(q, (0, 1))
        tall = part // 2
        ats = [range(at, at + tall, GROUP) for at in range(0, part, tall)]
        for q in range(RADIX):
            left_back(q, (2, 3))
        mix(ats[0], range(RADIX))
        mix(ats[1], range(RADIX))
        first = right_back(0, tall)
        second = right_back(tall, tall)
        accumulate(0, tall, first)
        accumulate(tall, tall, second)
        return carry

    lax.fori_loop(0, live_ref[0, lax.axis_index("scan")], one_slot, 0)


def solve(live_counts, shifts, prepared, limit):
    grown = prepared[-1]
    side_len = prepared[1].shape[3]
    part = side_len // RADIX
    smem = pl.BlockSpec(memory_space=pltpu.SMEM)
    vmem = pl.BlockSpec(memory_space=pltpu.VMEM)
    wide = (RADIX, RADIX, 2 * part, part)
    tall = (RADIX, 2, side_len, part)
    scratch = [
        (wide, jnp.bfloat16),
        (tall, jnp.bfloat16),
        (wide, jnp.bfloat16),
        (wide, jnp.float32),
        (tall, jnp.bfloat16),
    ]
    return pl.pallas_call(
        solve_kernel,
        out_shape=pltpu.VMEM(grown.shape, grown.dtype),
        in_specs=[smem, smem] + [vmem] * len(prepared),
        out_specs=vmem,
        scratch_shapes=[pltpu.VMEM(*each) for each in scratch] + [pltpu.SemaphoreType.REGULAR],
        input_output_aliases={1 + len(prepared): 0},
        compiler_params=pltpu.CompilerParams(vmem_limit_bytes=limit),
    )(live_counts, shifts, *prepared)


def shards(axes, object_slab, probe_field, intensities, offsets, live_count):
    tables = residue_tables(probe_field.shape[-1])
    shifts = offsets[0, 0].T
    prepared, limit = gather(axes, shifts, object_slab, intensities[0, 0], probe_field, tables)
    grown = solve(live_count.T, shifts, prepared, limit)
    return scatter(axes, grown, object_slab.shape[1])


def solution(mesh):
    placed = (
        P(None, "tile", "scan"),
        P(),
        P("scan", "tile", None, None, None),
        P("scan", "tile", None, None),
        P(None, "tile"),
    )
    axes = tuple((name, mesh.shape[name]) for name in ("scan", "tile"))
    return jax.shard_map(
        functools.partial(shards, axes), mesh=mesh, in_specs=placed, out_specs=P(None, "tile", "scan"), check_vma=False
    )
```
